32 devices in a mesh: row: 4 (over z), col: 2 (over x), pole: 4 (over y, core).
Axes of the slice: x: 2, y: 2, z: 4, core: 2. Of those that a mesh axis runs over, the one named last changes fastest.
Arguments:
- window: bfloat16 [4, 8192, 8192], P('pole', 'col', 'row'), may hold values from -6 to 6
- panels: bfloat16 [4, 2, 8192, 256], P('pole', 'col', 'row'), may hold values from -0.0625 to 0.0625
- row_map: int32 [3, 8192], P(None, 'row'), may hold values from 0 to 8191, as said below
- panel_root: int32 [4, 3], P('pole'), may hold values from 0 to 1
- upper_blocks: bfloat16 [4, 3, 256, 256], P('pole', None, 'row'), may hold values from -0.375 to 0.375
- diag_inverse: float32 [4, 3, 256, 256], P('pole', None, 'row'), may hold values from -6 to 6
- weights: float32 [4], replicated, may hold values from 0.25 to 1
- pole_order: int32 [4], P('pole'), may hold values from 0 to 3, each once
Outputs:
- inv_columns: float32 [3, 2, 4096, 256], P(None, 'col', ('row', 'pole'))
- inv_diag: float32 [3, 256, 256], P(None, ('row', 'pole'))
The draws below stay inside these ranges and needn't reach their ends.
Inputs may be any that keep to these rules, and one draw needn't show every extreme that they name: row_map[k] permutes the positions inside each aligned group of 1024 consecutive positions. `pole_order`: each of the 4 poles appears once.
All inputs are finite; a program needn't handle non-finite values.
Results may differ from the reference program's by a relative error of at most 0.0003.
Values may be sent and summed in bfloat16 or wider, within the bound.
A program may use at most 128 MiB of HBM per device.

```python
import jax
import jax.numpy as jnp
from jax import lax

W = 8192
B = 256
NS = 3
NP = 4
NE = 3
GROUP = 1024
N_ROW = 4
N_COL = 2


def draw_row_map(key, part):
    blocks = NS * (W // GROUP)
    group_keys = jax.random.split(key, blocks)
    shuffled = jax.vmap(lambda one_key: jax.random.permutation(one_key, GROUP))(group_keys)
    offsets = jnp.arange(blocks) % (W // GROUP) * GROUP
    return (shuffled + offsets[:, None]).reshape(NS, W).astype(jnp.int32)


def set_ends(values, own_key, low, high):
    longest = values.shape.index(max(values.shape))
    spots = []
    for shift in (0, 1):
        where = [jax.random.randint(jax.random.fold_in(own_key, axis), (), 0, length) for axis, length in enumerate(values.shape)]
        where[longest] = (where[longest] + shift) % values.shape[longest]
        spots.append(tuple(where))
    return values.at[spots[0]].set(low).at[spots[1]].set(high)


def levels(stream_key, shape, cuts, least, largest):
    def one(axis_at, blocks):
        heights = jax.random.uniform(jax.random.fold_in(jax.random.fold_in(stream_key, 6), axis_at), (blocks,), jnp.float32, least / len(cuts), largest / len(cuts))
        return jnp.repeat(jnp.exp(heights), shape[axis_at] // blocks).reshape((-1,) + (1,) * (len(shape) - axis_at - 1))

    level = one(*cuts[0])
    for cut in cuts[1:]:
        level = level * one(*cut)
    return level


def noise(rng, extent, scale, bound, pieces=(), dtype=jnp.bfloat16):
    result = scale * jax.random.normal(rng, extent, jnp.float32)
    if pieces:
        result = result * levels(rng, extent, pieces, -0.22, 0.18)
    return jnp.clip(result, -bound, bound).astype(dtype)


def setup_inputs(seed: int = 0) -> dict:
    arg_keys = jax.random.split(jax.random.key(seed), 9)
    window = noise(arg_keys[0], (NP, W, W), 1.0, 6.0, ((0, 4), (1, 2), (2, 4)))
    panels = noise(arg_keys[1], (NP, N_COL, W, B), W ** -0.5, 0.0625, ((0, 4), (1, 2), (2, 4)))
    row_map = draw_row_map(jax.random.fold_in(arg_keys[8], 71), 0)
    panel_root = set_ends(jax.random.randint(arg_keys[3], (NP, NS), 0, N_COL), jax.random.fold_in(arg_keys[3], 1), 0, N_COL - 1).astype(jnp.int32)
    upper_blocks = noise(arg_keys[4], (NP, NE, B, B), B ** -0.5, 0.375, ((0, 4), (2, 4)))
    diag_inverse = noise(arg_keys[5], (NP, NS, B, B), 1.0, 6.0, ((0, 4), (2, 4)), jnp.float32)
    weights = jnp.clip(jax.random.uniform(arg_keys[6], (NP,), jnp.float32, 0.25, 1.0), 0.25, 1.0)
    pole_order = jax.random.permutation(arg_keys[7], NP).astype(jnp.int32)
    return {"window": window, "panels": panels, "row_map": row_map, "panel_root": panel_root, "upper_blocks": upper_blocks, "diag_inverse": diag_inverse, "weights": weights, "pole_order": pole_order}


def precise(left, right):
    return jnp.dot(left, right, precision=lax.Precision.HIGHEST, preferred_element_type=jnp.float32)


def pair_index(current, earlier):
    return current * (current - 1) // 2 + earlier


def inverse_block(diagonals, crossed, first, second):
    if first == second:
        return diagonals[first]
    if first < second:
        return crossed[(first, second)]
    return crossed[(second, first)].T


def natural_order(aligned):
    group_rows = W // (N_ROW * N_COL)
    width = aligned.shape[-1]
    return aligned.reshape(N_ROW, N_COL, group_rows, width).transpose(1, 0, 2, 3).reshape(W, width)


def reference(window, panels, row_map, panel_root, upper_blocks, diag_inverse, weights, pole_order):
    def one_pole(pole_index):
        window_block = window[pole_index]
        slot_panels = panels[pole_index]
        factors = upper_blocks[pole_index].astype(jnp.float32)
        inverses = diag_inverse[pole_index]
        pole_roots = lax.dynamic_index_in_dim(panel_root, pole_index, 0, keepdims=False)
        columns = []
        diagonals = []
        crossed = {}
        for current in range(NS):
            panel_slab = lax.dynamic_index_in_dim(slot_panels, pole_roots[current], 0, keepdims=False)
            aligned = jnp.take(panel_slab, row_map[current], axis=0)
            own_rows = natural_order(aligned).astype(jnp.float32)
            y_window = jnp.dot(window_block, aligned, preferred_element_type=jnp.float32)
            for earlier in range(current):
                y_window = y_window + precise(columns[earlier], factors[pair_index(current, earlier)])
            y_blocks = []
            for earlier in range(current):
                block_sum = precise(columns[earlier].T, own_rows)
                for other_node in range(current):
                    block_sum = block_sum + precise(inverse_block(diagonals, crossed, earlier, other_node), factors[pair_index(current, other_node)])
                y_blocks.append(block_sum)
            diagonal = inverses[current] + precise(own_rows.T, y_window)
            for earlier in range(current):
                diagonal = diagonal + precise(factors[pair_index(current, earlier)].T, y_blocks[earlier])
                crossed[(earlier, current)] = -y_blocks[earlier]
            columns.append(-y_window)
            diagonals.append(diagonal)
        return jnp.stack(columns), jnp.stack(diagonals)

    all_columns, all_diagonals = lax.map(one_pole, jnp.arange(NP))
    pole_weights = jnp.take(weights, pole_order)
    inv_columns = jnp.einsum("p,pkwb->kwb", pole_weights, all_columns).reshape(NS, N_COL, W // N_COL, B)
    inv_diag = jnp.einsum("p,pkab->kab", pole_weights, all_diagonals)
    return inv_columns, inv_diag
```

```python
import jax
import jax.numpy as jnp
from jax import lax
from jax.experimental import pallas as pl
from jax.experimental.pallas import tpu as pltpu
from jax.sharding import PartitionSpec as P


NS = 3
CHUNKS = 2


def precise(left, right):
    return jnp.dot(left, right, precision=lax.Precision.HIGHEST, preferred_element_type=jnp.float32)


def pair_index(current, earlier):
    return current * (current - 1) // 2 + earlier


def split(value):
    high = value.astype(jnp.bfloat16)
    return high, (value - high.astype(jnp.float32)).astype(jnp.bfloat16)


def pick(stacked, index, axis=0):
    return lax.dynamic_index_in_dim(stacked, index, axis, keepdims=False)


def swap(block, axis_name, bit):
    size = lax.axis_size(axis_name)
    return lax.ppermute(block, axis_name, [(i, i ^ bit) for i in range(size)])


def shift(block, axis_name, distance):
    size = lax.axis_size(axis_name)
    return lax.ppermute(block, axis_name, [(i, (i + distance) % size) for i in range(size)])


def encode(value):
    top = jnp.maximum(jnp.max(jnp.abs(value), axis=-1), 1e-30)
    return jnp.round(value * (32000.0 / top)[..., None]).astype(jnp.int16), top


def decode(code, top):
    return code.astype(jnp.float32) * (top * (1.0 / 32000.0))[..., None]


def halving_sum(blocks, axis_name, bit):
    size = lax.axis_size(axis_name)
    index = lax.axis_index(axis_name)
    while bit < size:
        side = (index // bit) % 2
        paired = blocks.reshape((blocks.shape[0], blocks.shape[1] // 2, 2) + blocks.shape[2:])
        blocks = pick(paired, side, 2) + swap(pick(paired, 1 - side, 2), axis_name, bit)
        bit *= 2
    return blocks[:, 0]


def shift_sum(blocks, axis_name):
    size = lax.axis_size(axis_name)
    index = lax.axis_index(axis_name)
    total = pick(blocks, index)
    arrived = []
    for distance in range(1, size):
        arrived.append(shift(pick(blocks, (index + distance) % size), axis_name, distance))
    return sum(arrived, total)


def coded_sum(blocks, axis_name):
    size = lax.axis_size(axis_name)
    index = lax.axis_index(axis_name)
    total = pick(blocks, index)
    code, top = encode(blocks)
    arrived = []
    for distance in range(1, size):
        at = (index + distance) % size
        sent = shift(pick(code, at), axis_name, distance)
        arrived.append(decode(sent, shift(pick(top, at), axis_name, distance)))
    return sum(arrived, total)


def shift_gather(block, axis_name):
    size = lax.axis_size(axis_name)
    blocks = [block]
    for distance in range(1, size):
        blocks.append(shift(block, axis_name, distance))
    return blocks


def reorder_kernel(slab_ref, map_ref, rows_ref, out_ref):
    size = rows_ref.shape[2]
    chosen = lax.broadcasted_iota(jnp.int32, (size, size), 0) == map_ref[0, 0]
    out_ref[...] = lax.dot_general(
        jnp.where(chosen, 1.0, 0.0).astype(rows_ref.dtype),
        rows_ref[0, 0],
        (((0,), (0,)), ((), ())),
        preferred_element_type=jnp.float32,
    ).astype(out_ref.dtype)


def reorder(slab_index, maps, sources):
    _, groups, group, width = sources.shape
    return pl.pallas_call(
        reorder_kernel,
        out_shape=jax.ShapeDtypeStruct((groups * group, NS * width), sources.dtype),
        grid_spec=pltpu.PrefetchScalarGridSpec(
            num_scalar_prefetch=1,
            grid=(groups, NS),
            in_specs=[
                pl.BlockSpec((1, 1, 1, group), lambda a, k, slabs: (a, k, 0, 0)),
                pl.BlockSpec((1, 1, group, width), lambda a, k, slabs: (slabs[k], a, 0, 0)),
            ],
            out_specs=pl.BlockSpec((group, width), lambda a, k, slabs: (a, k)),
        ),
        cost_estimate=pl.CostEstimate(
            flops=2 * groups * NS * group * group * width,
            bytes_accessed=4 * groups * NS * group * width,
            transcendentals=0,
        ),
    )(slab_index, maps[:, :, None], sources)


def window_kernel(core_ref, weight_ref, window_ref, aligned_ref, factor_ref, away_ref, keep_ref):
    width = factor_ref.shape[2]
    half = pl.num_programs(0) // 2
    y_window = jnp.dot(window_ref[0], aligned_ref[...], preferred_element_type=jnp.float32)
    y_window = y_window * weight_ref[0]
    columns, parts = [], []
    for k in range(NS):
        column = y_window[:, k * width : (k + 1) * width]
        for m in range(k):
            for part in parts[m]:
                column = column - jnp.dot(
                    part, factor_ref[pair_index(k, m)], preferred_element_type=jnp.float32
                )
        columns.append(column)
        parts.append(split(column))

    @pl.when(pl.program_id(0) < half)
    def _():
        for k in range(NS):
            away_ref[0, 0, :, k * width : (k + 1) * width] = columns[k]

    @pl.when(pl.program_id(0) >= half)
    def _():
        for k in range(NS):
            keep_ref[0, 0, :, k * width : (k + 1) * width] = columns[k]


def window_columns(place, scale, window_rows, aligned, factors, other, n_row, n_pole):
    share = window_rows.shape[1]
    side = n_pole // 4
    half = n_row * side
    depth, total = aligned.shape

    def window_at(i, place_ref):
        j = i % half
        core = jnp.where(i < half, 1 - place_ref[1], place_ref[1])
        second = 1 - place_ref[2] if other else place_ref[2]
        return (j // side) * n_pole + (j % side) * 4 + second * 2 + core, 0, 0

    def away_at(i, place_ref):
        j = jnp.minimum(i, half - 1)
        return j // side, j % side, 0, 0

    def keep_at(i, place_ref):
        j = jnp.maximum(i - half, 0)
        return j // side, j % side, 0, 0

    shape = jax.ShapeDtypeStruct((n_row, side, share, total), jnp.float32)
    return pl.pallas_call(
        window_kernel,
        out_shape=(shape, shape),
        grid_spec=pltpu.PrefetchScalarGridSpec(
            num_scalar_prefetch=1,
            grid=(2 * half,),
            in_specs=[
                pl.BlockSpec(memory_space=pltpu.SMEM),
                pl.BlockSpec((1, share, depth), window_at),
                pl.BlockSpec((depth, total), lambda i, c: (0, 0)),
                pl.BlockSpec(factors.shape, lambda i, c: (0, 0, 0)),
            ],
            out_specs=(
                pl.BlockSpec((1, 1, share, total), away_at),
                pl.BlockSpec((1, 1, share, total), keep_at),
            ),
        ),
        cost_estimate=pl.CostEstimate(
            flops=4 * half * share * depth * total,
            bytes_accessed=4 * half * share * (depth + 2 * total),
            transcendentals=0,
        ),
    )(place, scale, window_rows, aligned, factors)


def inner_kernel(place_ref, own_away_ref, own_keep_ref, away_ref, keep_ref, sum_ref):
    width = sum_ref.shape[1]

    @pl.when((pl.program_id(0) == 0) & (pl.program_id(1) == 0))
    def _():
        sum_ref[...] = jnp.zeros_like(sum_ref)

    for own_ref, term_ref in ((own_away_ref, away_ref), (own_keep_ref, keep_ref)):
        for m in range(NS):
            for part in split(term_ref[0, 0, :, m * width : (m + 1) * width]):
                for k in range(m, NS):
                    sum_ref[k * (k + 1) // 2 + m] += lax.dot_general(
                        own_ref[0, 0, :, k * width : (k + 1) * width],
                        part,
                        (((0,), (0,)), ((), ())),
                        preferred_element_type=jnp.float32,
                    )


def inner_products(place, own, away, keep, other, width):
    n_row, side, share, total = away.shape
    n_pole = 4 * side

    def own_at(flip):
        def at(d, j, place_ref):
            core = 1 - place_ref[1] if flip else place_ref[1]
            second = 1 - place_ref[2] if other else place_ref[2]
            return d, j * 4 + second * 2 + core, 0, 0

        return at

    def term_at(d, j, place_ref):
        return (place_ref[0] - d + n_row) % n_row, j, 0, 0

    pairs = NS * (NS + 1) // 2
    return pl.pallas_call(
        inner_kernel,
        out_shape=jax.ShapeDtypeStruct((pairs, width, width), jnp.float32),
        grid_spec=pltpu.PrefetchScalarGridSpec(
            num_scalar_prefetch=1,
            grid=(n_row, side),
            in_specs=[
                pl.BlockSpec((1, 1, share, total), own_at(True)),
                pl.BlockSpec((1, 1, share, total), own_at(False)),
                pl.BlockSpec((1, 1, share, total), term_at),
                pl.BlockSpec((1, 1, share, total), term_at),
            ],
            out_specs=pl.BlockSpec((pairs, width, width), lambda d, j, p: (0, 0, 0)),
        ),
        cost_estimate=pl.CostEstimate(
            flops=2 * n_row * n_pole * share * pairs * width * width,
            bytes_accessed=3 * n_row * n_pole * share * total,
            transcendentals=0,
        ),
    )(place, own, own, away, keep)


def staged(window, panels, row_map, panel_root, upper_blocks, diag_inverse, weights, pole_order):
    n_row, n_col, n_pole = (lax.axis_size(name) for name in ("row", "col", "pole"))
    row_index, col_index = lax.axis_index("row"), lax.axis_index("col")
    window_block = window[0]
    slab = panels[0, 0]
    width = slab.shape[1]
    group = window_block.shape[0] // n_row
    share = group // n_pole
    pole_weight = jnp.sum(jnp.where(jnp.arange(weights.shape[0]) == pole_order[0], weights, 0.0))
    pole_index = lax.axis_index("pole")
    core, second = pole_index % 2, (pole_index // 2) % 2
    place = jnp.stack([row_index, core, second]).astype(jnp.int32)
    slab_index = (col_index - panel_root[0] + n_col) % n_col
    local_map = row_map % group
    own_start = col_index * group

    slabs = [slab]
    for distance in range(1, n_col):
        slabs.append(shift(slab, "col", distance))
    own_map = lax.dynamic_slice_in_dim(local_map, own_start, group, 1)
    packed_map = jnp.concatenate([own_map // 32, own_map % 32]).astype(jnp.bfloat16).reshape(-1)
    packed_map = jnp.pad(packed_map, (0, -packed_map.shape[0] % width)).reshape(-1, width)
    part_rows = upper_blocks.shape[2]
    pairs = upper_blocks.shape[1]
    gathered = shift_gather(
        jnp.concatenate([upper_blocks[0].reshape(-1, width), packed_map]), "row"
    )
    own_slab = [shift_gather(lax.dynamic_slice_in_dim(slab, own_start, group, 0), "row")]
    factors = jnp.zeros((pairs, part_rows * n_row, width), upper_blocks.dtype)
    maps = []
    for back, g in enumerate(gathered):
        at = (row_index - back + n_row) % n_row
        factors = lax.dynamic_update_slice_in_dim(
            factors, g[: pairs * part_rows].reshape(pairs, part_rows, width), at * part_rows, 1
        )
        flat = g[pairs * part_rows :].reshape(-1)[: 2 * NS * group].astype(jnp.int32)
        maps.append((flat[: NS * group] * 32 + flat[NS * group :]).reshape(NS, group))

    stacked_slabs = jnp.stack(slabs).reshape(n_col, n_col, group, width)
    stacked_map = jnp.stack([local_map[:, c * group : (c + 1) * group] for c in range(n_col)])
    aligned = reorder(slab_index, stacked_map, stacked_slabs)
    own_slab += [
        shift_gather(lax.dynamic_slice_in_dim(other, own_start, group, 0), "row")
        for other in slabs[1:]
    ]

    window_rows = window_block.reshape(n_row * n_pole, share, window_block.shape[1])
    scale = (-pole_weight).reshape(1)
    first_away, first_keep = window_columns(
        place, scale, window_rows, aligned, factors, True, n_row, n_pole
    )
    last_away, last_keep = window_columns(
        place, scale, window_rows, aligned, factors, False, n_row, n_pole
    )
    first_come = swap(first_away, "pole", 1)
    last_come = swap(last_away, "pole", 1)
    step = share // CHUNKS if share % (8 * CHUNKS) == 0 else share
    pieces = [slice(at, at + step) for at in range(0, share, step)]
    sent = [first_keep[:, :, piece] + first_come[:, :, piece] for piece in pieces]
    kept = [last_keep[:, :, piece] + last_come[:, :, piece] for piece in pieces]
    _, own_slab = lax.optimization_barrier((sent, own_slab))
    column_parts = []
    for away, keep in zip(sent, kept):
        code, top = encode(away)
        code = swap(code, "pole", 2)
        top = swap(top, "pole", 2)
        total = keep + decode(code, top)
        column_parts.append(coded_sum(halving_sum(total, "pole", 4), "row"))
    summed_columns = jnp.stack(
        [
            jnp.concatenate([part[:, k * width : (k + 1) * width] for part in column_parts])
            for k in range(NS)
        ]
    )

    stacked_own = jnp.stack([jnp.stack(blocks) for blocks in own_slab])
    own = reorder(slab_index, jnp.stack(maps), stacked_own)
    own = own.reshape(n_row, n_pole, share, NS * width)
    products = inner_products(place, own, first_away, first_keep, True, width)
    products += inner_products(place, own, last_away, last_keep, False, width)
    inner = {(k, m): products[k * (k + 1) // 2 + m] for k in range(NS) for m in range(k + 1)}

    wide = [factors[e].astype(jnp.float32) for e in range(pairs)]
    spread = jnp.zeros((NS, diag_inverse.shape[2] * n_row, width), jnp.float32)
    spread = lax.dynamic_update_slice_in_dim(
        spread, diag_inverse[0] * (pole_weight / n_col), row_index * diag_inverse.shape[2], 1
    )
    diagonals, crossed = [], {}

    def inverse_block(m, n):
        if m == n:
            return diagonals[m]
        return crossed[m, n] if m < n else crossed[n, m].T

    for k in range(NS):
        diagonal = spread[k] - inner[k, k]
        for m in range(k):
            y_block = inner[k, m].T
            for n in range(k):
                y_block = y_block + precise(inverse_block(m, n), wide[pair_index(k, n)])
            crossed[m, k] = -y_block
            diagonal = diagonal + precise(wide[pair_index(k, m)].T, y_block)
        diagonals.append(diagonal)
    blocks = jnp.concatenate(diagonals, axis=1).reshape(n_row, n_pole, -1, NS * width)
    summed_diagonals = shift_sum(halving_sum(blocks, "pole", 1), "row")
    bit = 1
    while bit < n_col:
        summed_diagonals = summed_diagonals + lax.ppermute(
            summed_diagonals, "col", [(i, i ^ bit) for i in range(n_col)]
        )
        bit *= 2
    summed_diagonals = summed_diagonals.reshape(-1, NS, width).transpose(1, 0, 2)
    return (summed_columns[:, None], summed_diagonals)


def solution(mesh):
    return jax.shard_map(
        staged,
        mesh=mesh,
        in_specs=(
            P("pole", "col", "row"),
            P("pole", "col", "row", None),
            P(None, "row"),
            P("pole", None),
            P("pole", None, "row", None),
            P("pole", None, "row", None),
            P(),
            P("pole"),
        ),
        out_specs=(P(None, "col", ("row", "pole"), None), P(None, ("row", "pole"), None)),
        check_vma=False,
    )
```

```python
import jax
import jax.numpy as jnp
from jax import lax
from jax.experimental import pallas as pl
from jax.experimental.pallas import tpu as pltpu
from jax.sharding import PartitionSpec as P


NS = 3
CHUNKS = 2


def precise(left, right):
    return jnp.dot(left, right, precision=lax.Precision.HIGHEST, preferred_element_type=jnp.float32)


def pair_index(current, earlier):
    return current * (current - 1) // 2 + earlier


def split(value):
    high = value.astype(jnp.bfloat16)
    return high, (value - high.astype(jnp.float32)).astype(jnp.bfloat16)


def pick(stacked, index, axis=0):
    return lax.dynamic_index_in_dim(stacked, index, axis, keepdims=False)


def swap(block, axis_name, bit):
    size = lax.axis_size(axis_name)
    return lax.ppermute(block, axis_name, [(i, i ^ bit) for i in range(size)])


def shift(block, axis_name, distance):
    size = lax.axis_size(axis_name)
    return lax.ppermute(block, axis_name, [(i, (i + distance) % size) for i in range(size)])


def encode(value):
    top = jnp.maximum(jnp.max(jnp.abs(value), axis=-1), 1e-30)
    return jnp.round(value * (32000.0 / top)[..., None]).astype(jnp.int16), top


def decode(code, top):
    return code.astype(jnp.float32) * (top * (1.0 / 32000.0))[..., None]


def halving_sum(blocks, axis_name, bit):
    size = lax.axis_size(axis_name)
    index = lax.axis_index(axis_name)
    while bit < size:
        side = (index // bit) % 2
        paired = blocks.reshape((blocks.shape[0], blocks.shape[1] // 2, 2) + blocks.shape[2:])
        blocks = pick(paired, side, 2) + swap(pick(paired, 1 - side, 2), axis_name, bit)
        bit *= 2
    return blocks[:, 0]


def shift_sum(blocks, axis_name):
    size = lax.axis_size(axis_name)
    index = lax.axis_index(axis_name)
    total = pick(blocks, index)
    arrived = []
    for distance in range(1, size):
        arrived.append(shift(pick(blocks, (index + distance) % size), axis_name, distance))
    return sum(arrived, total)


def coded_sum(blocks, axis_name):
    size = lax.axis_size(axis_name)
    index = lax.axis_index(axis_name)
    total = pick(blocks, index)
    code, top = encode(blocks)
    arrived = []
    for distance in range(1, size):
        at = (index + distance) % size
        sent = shift(pick(code, at), axis_name, distance)
        arrived.append(decode(sent, shift(pick(top, at), axis_name, distance)))
    return sum(arrived, total)


def shift_gather(block, axis_name):
    size = lax.axis_size(axis_name)
    blocks = [block]
    for distance in range(1, size):
        blocks.append(shift(block, axis_name, distance))
    return blocks


def reorder_kernel(slab_ref, map_ref, rows_ref, out_ref):
    size = rows_ref.shape[2]
    chosen = lax.broadcasted_iota(jnp.int32, (size, size), 0) == map_ref[0, 0]
    out_ref[...] = lax.dot_general(
        jnp.where(chosen, 1.0, 0.0).astype(rows_ref.dtype),
        rows_ref[0, 0],
        (((0,), (0,)), ((), ())),
        preferred_element_type=jnp.float32,
    ).astype(out_ref.dtype)


def reorder(slab_index, maps, sources):
    _, groups, group, width = sources.shape
    return pl.pallas_call(
        reorder_kernel,
        out_shape=jax.ShapeDtypeStruct((groups * group, NS * width), sources.dtype),
        grid_spec=pltpu.PrefetchScalarGridSpec(
            num_scalar_prefetch=1,
            grid=(groups, NS),
            in_specs=[
                pl.BlockSpec((1, 1, 1, group), lambda a, k, slabs: (a, k, 0, 0)),
                pl.BlockSpec((1, 1, group, width), lambda a, k, slabs: (slabs[k], a, 0, 0)),
            ],
            out_specs=pl.BlockSpec((group, width), lambda a, k, slabs: (a, k)),
        ),
        cost_estimate=pl.CostEstimate(
            flops=2 * groups * NS * group * group * width,
            bytes_accessed=4 * groups * NS * group * width,
            transcendentals=0,
        ),
    )(slab_index, maps[:, :, None], sources)


def window_kernel(core_ref, weight_ref, window_ref, aligned_ref, factor_ref, away_ref, keep_ref):
    width = factor_ref.shape[2]
    half = pl.num_programs(0) // 2
    y_window = jnp.dot(window_ref[0], aligned_ref[...], preferred_element_type=jnp.float32)
    y_window = y_window * weight_ref[0]
    columns, parts = [], []
    for k in range(NS):
        column = y_window[:, k * width : (k + 1) * width]
        for m in range(k):
            for part in parts[m]:
                column = column - jnp.dot(
                    part, factor_ref[pair_index(k, m)], preferred_element_type=jnp.float32
                )
        columns.append(column)
        parts.append(split(column))

    @pl.when(pl.program_id(0) < half)
    def _():
        for k in range(NS):
            away_ref[0, 0, :, k * width : (k + 1) * width] = columns[k]

    @pl.when(pl.program_id(0) >= half)
    def _():
        for k in range(NS):
            keep_ref[0, 0, :, k * width : (k + 1) * width] = columns[k]


def window_columns(place, scale, window_rows, aligned, factors, other, n_row, n_pole):
    share = window_rows.shape[1]
    side = n_pole // 4
    half = n_row * side
    depth, total = aligned.shape

    def window_at(i, place_ref):
        j = i % half
        core = jnp.where(i < half, 1 - place_ref[1], place_ref[1])
        second = 1 - place_ref[2] if other else place_ref[2]
        return (j // side) * n_pole + (j % side) * 4 + second * 2 + core, 0, 0

    def away_at(i, place_ref):
        j = jnp.minimum(i, half - 1)
        return j // side, j % side, 0, 0

    def keep_at(i, place_ref):
        j = jnp.maximum(i - half, 0)
        return j // side, j % side, 0, 0

    shape = jax.ShapeDtypeStruct((n_row, side, share, total), jnp.float32)
    return pl.pallas_call(
        window_kernel,
        out_shape=(shape, shape),
        grid_spec=pltpu.PrefetchScalarGridSpec(
            num_scalar_prefetch=1,
            grid=(2 * half,),
            in_specs=[
                pl.BlockSpec(memory_space=pltpu.SMEM),
                pl.BlockSpec((1, share, depth), window_at),
                pl.BlockSpec((depth, total), lambda i, c: (0, 0)),
                pl.BlockSpec(factors.shape, lambda i, c: (0, 0, 0)),
            ],
            out_specs=(
                pl.BlockSpec((1, 1, share, total), away_at),
                pl.BlockSpec((1, 1, share, total), keep_at),
            ),
        ),
        cost_estimate=pl.CostEstimate(
            flops=4 * half * share * depth * total,
            bytes_accessed=4 * half * share * (depth + 2 * total),
            transcendentals=0,
        ),
    )(place, scale, window_rows, aligned, factors)


def inner_kernel(place_ref, own_away_ref, own_keep_ref, away_ref, keep_ref, sum_ref):
    width = sum_ref.shape[1]

    @pl.when((pl.program_id(0) == 0) & (pl.program_id(1) == 0))
    def _():
        sum_ref[...] = jnp.zeros_like(sum_ref)

    for own_ref, term_ref in ((own_away_ref, away_ref), (own_keep_ref, keep_ref)):
        for m in range(NS):
            for part in split(term_ref[0, 0, :, m * width : (m + 1) * width]):
                for k in range(m, NS):
                    sum_ref[k * (k + 1) // 2 + m] += lax.dot_general(
                        own_ref[0, 0, :, k * width : (k + 1) * width],
                        part,
                        (((0,), (0,)), ((), ())),
                        preferred_element_type=jnp.float32,
                    )


def inner_products(place, own, away, keep, other, width):
    n_row, side, share, total = away.shape
    n_pole = 4 * side

    def own_at(flip):
        def at(d, j, place_ref):
            core = 1 - place_ref[1] if flip else place_ref[1]
            second = 1 - place_ref[2] if other else place_ref[2]
            return d, j * 4 + second * 2 + core, 0, 0

        return at

    def term_at(d, j, place_ref):
        return (place_ref[0] - d + n_row) % n_row, j, 0, 0

    pairs = NS * (NS + 1) // 2
    return pl.pallas_call(
        inner_kernel,
        out_shape=jax.ShapeDtypeStruct((pairs, width, width), jnp.float32),
        grid_spec=pltpu.PrefetchScalarGridSpec(
            num_scalar_prefetch=1,
            grid=(n_row, side),
            in_specs=[
                pl.BlockSpec((1, 1, share, total), own_at(True)),
                pl.BlockSpec((1, 1, share, total), own_at(False)),
                pl.BlockSpec((1, 1, share, total), term_at),
                pl.BlockSpec((1, 1, share, total), term_at),
            ],
            out_specs=pl.BlockSpec((pairs, width, width), lambda d, j, p: (0, 0, 0)),
        ),
        cost_estimate=pl.CostEstimate(
            flops=2 * n_row * n_pole * share * pairs * width * width,
            bytes_accessed=3 * n_row * n_pole * share * total,
            transcendentals=0,
        ),
    )(place, own, own, away, keep)


def staged(window, panels, row_map, panel_root, upper_blocks, diag_inverse, weights, pole_order):
    n_row, n_col, n_pole = (lax.axis_size(name) for name in ("row", "col", "pole"))
    row_index, col_index = lax.axis_index("row"), lax.axis_index("col")
    window_block = window[0]
    slab = panels[0, 0]
    width = slab.shape[1]
    group = window_block.shape[0] // n_row
    share = group // n_pole
    pole_weight = jnp.sum(jnp.where(jnp.arange(weights.shape[0]) == pole_order[0], weights, 0.0))
    pole_index = lax.axis_index("pole")
    core, second = pole_index % 2, (pole_index // 2) % 2
    place = jnp.stack([row_index, core, second]).astype(jnp.int32)
    slab_index = (col_index - panel_root[0] + n_col) % n_col
    local_map = row_map % group
    own_start = col_index * group

    slabs = [slab]
    for distance in range(1, n_col):
        slabs.append(shift(slab, "col", distance))
    own_map = lax.dynamic_slice_in_dim(local_map, own_start, group, 1)
    packed_map = jnp.concatenate([own_map // 32, own_map % 32]).astype(jnp.bfloat16).reshape(-1)
    packed_map = jnp.pad(packed_map, (0, -packed_map.shape[0] % width)).reshape(-1, width)
    part_rows = upper_blocks.shape[2]
    pairs = upper_blocks.shape[1]
    gathered = shift_gather(
        jnp.concatenate([upper_blocks[0].reshape(-1, width), packed_map]), "row"
    )
    own_slab = [shift_gather(lax.dynamic_slice_in_dim(slab, own_start, group, 0), "row")]
    factors = jnp.zeros((pairs, part_rows * n_row, width), upper_blocks.dtype)
    maps = []
    for back, g in enumerate(gathered):
        at = (row_index - back + n_row) % n_row
        factors = lax.dynamic_update_slice_in_dim(
            factors, g[: pairs * part_rows].reshape(pairs, part_rows, width), at * part_rows, 1
        )
        flat = g[pairs * part_rows :].reshape(-1)[: 2 * NS * group].astype(jnp.int32)
        maps.append((flat[: NS * group] * 32 + flat[NS * group :]).reshape(NS, group))

    stacked_slabs = jnp.stack(slabs).reshape(n_col, n_col, group, width)
    stacked_map = jnp.stack([local_map[:, c * group : (c + 1) * group] for c in range(n_col)])
    aligned = reorder(slab_index, stacked_map, stacked_slabs)
    own_slab += [
        shift_gather(lax.dynamic_slice_in_dim(other, own_start, group, 0), "row")
        for other in slabs[1:]
    ]

    window_rows = window_block.reshape(n_row * n_pole, share, window_block.shape[1])
    scale = (-pole_weight).reshape(1)
    first_away, first_keep = window_columns(
        place, scale, window_rows, aligned, factors, True, n_row, n_pole
    )
    last_away, last_keep = window_columns(
        place, scale, window_rows, aligned, factors, False, n_row, n_pole
    )
    first_come = swap(first_away, "pole", 1)
    last_come = swap(last_away, "pole", 1)
    step = share // CHUNKS if share % (8 * CHUNKS) == 0 else share
    pieces = [slice(at, at + step) for at in range(0, share, step)]
    sent = [first_keep[:, :, piece] + first_come[:, :, piece] for piece in pieces]
    kept = [last_keep[:, :, piece] + last_come[:, :, piece] for piece in pieces]
    _, own_slab = lax.optimization_barrier((sent, own_slab))
    column_parts = []
    for away, keep in zip(sent, kept):
        code, top = encode(away)
        code = swap(code, "pole", 2)
        top = swap(top, "pole", 2)
        total = keep + decode(code, top)
        column_parts.append(coded_sum(halving_sum(total, "pole", 4), "row"))
    summed_columns = jnp.stack(
        [
            jnp.concatenate([part[:, k * width : (k + 1) * width] for part in column_parts])
            for k in range(NS)
        ]
    )

    stacked_own = jnp.stack([jnp.stack(blocks) for blocks in own_slab])
    own = reorder(slab_index, jnp.stack(maps), stacked_own)
    own = own.reshape(n_row, n_pole, share, NS * width)
    products = inner_products(place, own, first_away, first_keep, True, width)
    products += inner_products(place, own, last_away, last_keep, False, width)
    inner = {(k, m): products[k * (k + 1) // 2 + m] for k in range(NS) for m in range(k + 1)}

    wide = [factors[e].astype(jnp.float32) for e in range(pairs)]
    spread = jnp.zeros((NS, diag_inverse.shape[2] * n_row, width), jnp.float32)
    spread = lax.dynamic_update_slice_in_dim(
        spread, diag_inverse[0] * (pole_weight / n_col), row_index * diag_inverse.shape[2], 1
    )
    diagonals, crossed = [], {}

    def inverse_block(m, n):
        if m == n:
            return diagonals[m]
        return crossed[m, n] if m < n else crossed[n, m].T

    for k in range(NS):
        diagonal = spread[k] - inner[k, k]
        for m in range(k):
            y_block = inner[k, m].T
            for n in range(k):
                y_block = y_block + precise(inverse_block(m, n), wide[pair_index(k, n)])
            crossed[m, k] = -y_block
            diagonal = diagonal + precise(wide[pair_index(k, m)].T, y_block)
        diagonals.append(diagonal)
    blocks = jnp.concatenate(diagonals, axis=1).reshape(n_row, n_pole, -1, NS * width)
    summed_diagonals = shift_sum(halving_sum(blocks, "pole", 1), "row")
    bit = 1
    while bit < n_col:
        summed_diagonals = summed_diagonals + lax.ppermute(
            summed_diagonals, "col", [(i, i ^ bit) for i in range(n_col)]
        )
        bit *= 2
    summed_diagonals = summed_diagonals.reshape(-1, NS, width).transpose(1, 0, 2)
    return (summed_columns[:, None], summed_diagonals)


MESH = pl.DeviceIdType.MESH
LEVELS = 32000.0


def code_of(value):
    top = jnp.maximum(jnp.max(jnp.abs(value), axis=0, keepdims=True), 1e-30)
    return jnp.round(value * (LEVELS / top)).astype(jnp.int32).astype(jnp.int16), top


def value_of(code, top):
    return code.astype(jnp.int32).astype(jnp.float32) * (top * (1.0 / LEVELS))


def fused_kernel(
    weights_ref, order_ref, root_ref, window_ref, slab_ref, map_ref, upper_ref, diag_ref,
    columns_ref, diagonal_ref,
    win, own_slab, far_slab, maps, fac, al, y, core_in, y_out, y_out_top, y_in, y_in_top,
    z_out, z_out_top, z_in, z_in_top, inner, spread, g_all, g_core, g_half, g_y, g_sum, g_z, g_x, g_last,
    x_send, x_recv, here, win_sem, own_send, own_recv, small_send, small_recv,
    core_send, core_recv, y_send, y_recv, z_send, z_recv,
    gc_send, gc_recv, gy_send, gy_recv, gz_send, gz_recv, gx_send, gx_recv,
):
    n_row, n_col, n_pole = (lax.axis_size(name) for name in ("row", "col", "pole"))
    r, c, p = (lax.axis_index(name) for name in ("row", "col", "pole"))
    side, core = p // 2, p % 2
    share, width = columns_ref.shape[1:]
    group = share * n_pole
    depth = diagonal_ref.shape[1]
    part = upper_ref.shape[1]
    to_col, to_core, to_side = {"col": 1 - c}, {"pole": side * 2 + 1 - core}, {"pole": (1 - side) * 2 + core}

    def remote(src, dst, send, recv, device):
        return pltpu.make_async_remote_copy(
            src_ref=src, dst_ref=dst, send_sem=send, recv_sem=recv, device_id=device, device_id_type=MESH
        )

    def half(at):
        return pl.ds(pl.multiple_of(at * group, group), group)

    def others():
        return [lax.rem(r + distance, n_row) for distance in range(1, n_row)]

    barrier = pltpu.get_barrier_semaphore()
    for device in [to_col, to_core, to_side] + [{"row": at} for at in others()]:
        pl.semaphore_signal(barrier, inc=1, device_id=device, device_id_type=MESH)
    pl.semaphore_wait(barrier, 2 + n_row)

    def x_copy(at):
        src, dst = ((half(1 - c), own_slab.at[r, 1]), (half(c), far_slab.at[1]))[at]
        return remote(slab_ref.at[src], dst, x_send.at[at], x_recv.at[at], to_col)

    def own_copy(block, j, right, first=False):
        src = slab_ref.at[half(c)] if first else own_slab.at[block, j]
        return remote(
            src, own_slab.at[block, j], own_send.at[block, j, 1 - right], own_recv.at[block, j],
            {"row": r + 1 if right else r - 1},
        )

    def small_copy(at):
        rows = pl.ds(pl.multiple_of(r * part, part), part)
        return (
            remote(upper_ref, fac.at[:, rows], small_send.at[at, 0], small_recv.at[r, 0], {"row": at}),
            remote(map_ref, maps.at[r], small_send.at[at, 1], small_recv.at[r, 1], {"row": at}),
        )

    def small_arrival(at):
        rows = pl.ds(pl.multiple_of(at * part, part), part)
        return (
            remote(upper_ref, fac.at[:, rows], small_send.at[at, 0], small_recv.at[at, 0], {"row": at}),
            remote(map_ref, maps.at[at], small_send.at[at, 1], small_recv.at[at, 1], {"row": at}),
        )

    def both_ways(j, first):
        for right in (1, 0):
            @pl.when(r < n_row - 1 if right else r > 0)
            def _(right=right):
                own_copy(r, j, right, first).start()

    x_copy(0).start()
    for at in others():
        for copy in small_copy(at):
            copy.start()
    both_ways(0, True)
    x_copy(1).start()
    locals_ = [
        pltpu.make_async_copy(slab_ref.at[half(c)], own_slab.at[r, 0], here.at[0]),
        pltpu.make_async_copy(slab_ref.at[half(1 - c)], far_slab.at[0], here.at[1]),
    ]
    loads = []
    for slot, at in ((0, c), (1, 1 - c)):
        for pole in range(n_pole):
            loads.append(
                pltpu.make_async_copy(
                    window_ref.at[:, pole, :, half(at)], win.at[slot, pole], win_sem.at[slot, pole]
                )
            )
    for copy in locals_ + loads:
        copy.start()

    maps[r] = map_ref[...]
    fac[:, pl.ds(pl.multiple_of(r * part, part), part)] = upper_ref[...]
    weight = jnp.float32(0.0)
    for at in range(weights_ref.shape[0]):
        weight += jnp.where(order_ref[0] == at, weights_ref[at], 0.0)
    inner[...] = jnp.zeros_like(inner)

    def reorder(slot, source, block, at):
        def one(k, carry):
            row = maps[block, pl.ds(k, 1), half(at)] - (block * n_col + at) * group
            chosen = lax.broadcasted_iota(jnp.int32, (group, group), 0) == row
            column = lax.rem(root_ref[0, k] + n_col - c, n_col)
            rows = source[0]
            for j in range(1, n_col):
                rows = jnp.where(column == j, source[j], rows)
            placed = lax.dot_general(
                jnp.where(chosen, 1.0, 0.0).astype(rows.dtype), rows, (((0,), (0,)), ((), ())),
                preferred_element_type=jnp.float32,
            )
            al[slot, :, pl.ds(pl.multiple_of(k * width, width), width)] = placed.astype(al.dtype)
            return carry

        lax.fori_loop(0, NS, one, 0)

    near = jnp.minimum(r, n_row - 1 - r)
    toward = jnp.where(r < n_row - 1 - r, 1, -1)

    def block_at(step):
        odd = lax.rem(step, 2)
        zigzag = r + (2 * odd - 1) * ((step + 1) // 2)
        return jnp.where(step <= 2 * near, zigzag, r + toward * (step - near))

    def passes_on():
        return (r > 0) & (r < n_row - 1)

    def pass_on(step, j):
        @pl.when(passes_on())
        def _():
            block = block_at(step)
            own_copy(block, j, 1).wait_recv()

            @pl.when(block < r)
            def _():
                own_copy(block, j, 1).start()

            @pl.when(block > r)
            def _():
                own_copy(block, j, 0).start()

    x_copy(0).wait_recv()
    both_ways(1, False)
    for copy in locals_:
        copy.wait()
    early = range(1, min(3, n_row))
    for step in early:
        pass_on(step, 0)
    reorder(0, own_slab.at[r], r, c)
    for copy in loads[:n_pole]:
        copy.wait()

    def first_pass(pole, carry):
        left = win[0, pole].reshape(n_row * share, group)
        y[pole] = jnp.dot(left, al[0], preferred_element_type=jnp.float32).reshape(n_row, share, NS * width)
        return carry

    lax.fori_loop(0, n_pole, first_pass, 0)
    x_copy(1).wait_recv()
    reorder(1, far_slab, r, 1 - c)
    for copy in loads[n_pole:]:
        copy.wait()
    for at in others():
        for copy in small_arrival(at):
            copy.wait_recv()

    n_half = n_row // 2

    def core_copy(place, h):
        pole = jnp.where(place == 0, 1 - side, side) * 2 + 1 - core
        rows = pl.ds(h * n_half, n_half)
        return remote(
            y.at[pole, rows], core_in.at[place, rows], core_send.at[place, h], core_recv.at[place, h], to_core
        )

    def y_copy(h):
        return (
            remote(y_out.at[h], y_in.at[h], y_send.at[h, 0], y_recv.at[h, 0], to_side),
            remote(y_out_top.at[h], y_in_top.at[h], y_send.at[h, 1], y_recv.at[h, 1], to_side),
        )

    def last_pass(i, carry):
        kind, h = i // 2, lax.rem(i, 2)
        place = kind // 2
        pole = jnp.where(place == 0, 1 - side, side) * 2 + jnp.where(lax.rem(kind, 2) == 0, 1 - core, core)
        rows = pl.ds(h * n_half, n_half)
        left = win[1, pole, rows].reshape(n_half * share, group)
        total = y[pole, rows].reshape(n_half * share, NS * width)
        total = (total + jnp.dot(left, al[1], preferred_element_type=jnp.float32)) * -weight
        columns, parts = [], []
        for k in range(NS):
            column = total[:, k * width : (k + 1) * width]
            for m in range(k):
                for piece in parts[m]:
                    column = column - jnp.dot(piece, fac[pair_index(k, m)], preferred_element_type=jnp.float32)
            columns.append(column)
            parts.append(split(column))
            y[pole, rows, :, k * width : (k + 1) * width] = column.reshape(n_half, share, width)

        @pl.when(lax.rem(kind, 2) == 0)
        def _():
            core_copy(place, h).start()

        @pl.when(kind == 1)
        def _():
            core_copy(0, h).wait_recv()
            for at in range(n_half):
                code, top = code_of(y[pole, h * n_half + at] + core_in[0, h * n_half + at])
                y_out[h, at] = code
                y_out_top[h, at] = top
            for copy in y_copy(h):
                copy.start()

        @pl.when(i == 3)
        def _():
            for step in early:
                pass_on(step, 1)

        return carry

    lax.fori_loop(0, 8, last_pass, 0)
    for step in range(3, n_row):
        for j in range(2):
            pass_on(step, j)

    mine = side * 2 + core

    def z_copy(at, slot):
        return (
            remote(z_out.at[at], z_in.at[slot], z_send.at[at, 0], z_recv.at[slot, 0], {"row": at}),
            remote(z_out_top.at[at], z_in_top.at[slot], z_send.at[at, 1], z_recv.at[slot, 1], {"row": at}),
        )

    def finish(h):
        core_copy(1, h).wait_recv()
        for copy in y_copy(h):
            copy.wait_recv()
        for at in range(n_half):
            row = h * n_half + at
            total = y[mine, row] + core_in[1, row] + value_of(y_in[h, at], y_in_top[h, at])
            core_in[1, row] = total
            code, top = code_of(total)
            z_out[row] = code
            z_out_top[row] = top

            @pl.when(r != row)
            def _(row=row):
                for copy in z_copy(row, r):
                    copy.start()

    def gather_inner(step, carry):
        block = block_at(step)

        @pl.when(step > 0)
        def _():
            @pl.when((r == 0) | (r == n_row - 1))
            def _():
                for j in range(2):
                    own_copy(block, j, 1).wait_recv()

            reorder(1, own_slab.at[block], block, c)

        slot = jnp.minimum(step, 1)
        for m in range(NS):
            column = jnp.concatenate(
                [y[pole, block, :, m * width : (m + 1) * width] for pole in range(n_pole)]
            )
            pieces = split(column)
            for k in range(m, NS):
                rows = al[slot, :, k * width : (k + 1) * width]
                for piece in pieces:
                    inner[k * (k + 1) // 2 + m] += lax.dot_general(
                        rows, piece, (((0,), (0,)), ((), ())), preferred_element_type=jnp.float32
                    )

        @pl.when(step == n_row - 2)
        def _():
            finish(0)
            finish(1)

        return carry

    lax.fori_loop(0, n_row, gather_inner, 0)

    spread[...] = jnp.zeros_like(spread)
    spread[:, pl.ds(pl.multiple_of(r * part, part), part)] = diag_ref[...] * (weight * (1.0 / n_col))
    wide = [fac[e].astype(jnp.float32) for e in range(fac.shape[0])]
    diagonals, crossed = [], {}

    def inverse_block(m, n):
        if m == n:
            return diagonals[m]
        return crossed[m, n] if m < n else crossed[n, m].T

    for k in range(NS):
        diagonal = spread[k] - inner[k * (k + 1) // 2 + k]
        for m in range(k):
            y_block = inner[k * (k + 1) // 2 + m].T
            for n in range(k):
                y_block = y_block + precise(inverse_block(m, n), wide[pair_index(k, n)])
            crossed[m, k] = -y_block
            diagonal = diagonal + precise(wide[pair_index(k, m)].T, y_block)
        diagonals.append(diagonal)
        blocks = diagonal.reshape(n_row, n_pole, depth, width)
        for pole in range(n_pole):
            g_all[pole, :, :, k * width : (k + 1) * width] = blocks[:, pole]

    def gc_copy(at):
        return remote(g_all.at[at * 2 + 1 - core], g_core.at[at], gc_send.at[at], gc_recv.at[at], to_core)

    for at in range(2):
        gc_copy(at).start()
    gc_copy(1 - side).wait_recv()
    g_half[...] = g_all[(1 - side) * 2 + core] + g_core[1 - side]
    gy_copy = remote(g_half, g_y, gy_send, gy_recv, to_side)
    gy_copy.start()
    gc_copy(side).wait_recv()
    gy_copy.wait_recv()
    g_sum[...] = g_all[mine] + g_core[side] + g_y[...]

    def gz_copy(at, slot):
        return remote(g_sum.at[at], g_z.at[slot], gz_send.at[at], gz_recv.at[slot], {"row": at})

    for at in others():
        gz_copy(at, r).start()

    total = core_in[1, r]
    for at in others():
        for copy in z_copy(at, at):
            copy.wait_recv()
        total = total + value_of(z_in[at], z_in_top[at])
    for k in range(NS):
        columns_ref[k] = total[:, k * width : (k + 1) * width]

    total = g_sum[r]
    for at in others():
        gz_copy(at, at).wait_recv()
        total = total + g_z[at]
    g_last[...] = total
    gx_copy = remote(g_last, g_x, gx_send, gx_recv, to_col)
    gx_copy.start()
    gx_copy.wait_recv()
    total = total + g_x[...]
    for k in range(NS):
        diagonal_ref[k] = total[:, k * width : (k + 1) * width]

    for at in range(2):
        x_copy(at).wait_send()
        gc_copy(at).wait_send()
        for h in range(2):
            core_copy(at, h).wait_send()
        for copy in y_copy(at):
            copy.wait_send()
    gy_copy.wait_send()
    gx_copy.wait_send()
    for at in others():
        for copy in small_copy(at) + z_copy(at, r):
            copy.wait_send()
        gz_copy(at, r).wait_send()
    for j in range(2):
        for right in (1, 0):
            @pl.when(r < n_row - 1 if right else r > 0)
            def _(right=right, j=j):
                own_copy(r, j, right, j == 0).wait_send()

        for step in range(1, n_row):
            @pl.when(passes_on())
            def _(step=step, j=j):
                block = block_at(step)

                @pl.when(block < r)
                def _():
                    own_copy(block, j, 1).wait_send()

                @pl.when(block > r)
                def _():
                    own_copy(block, j, 0).wait_send()


def fused(window, panels, row_map, panel_root, upper_blocks, diag_inverse, weights, pole_order):
    n_row, n_col, n_pole = (lax.axis_size(name) for name in ("row", "col", "pole"))
    slab = panels[0, 0]
    width = slab.shape[1]
    group = window.shape[1] // n_row
    share = group // n_pole
    depth = width // (n_row * n_pole)
    pairs = upper_blocks.shape[1]
    total = NS * width
    rows = window[0].reshape(n_row, n_pole, share, n_col * group)
    smem, vmem, hbm = (pl.BlockSpec(memory_space=m) for m in (pltpu.SMEM, pltpu.VMEM, pl.ANY))
    bf16, f32, i16, i32 = jnp.bfloat16, jnp.float32, jnp.int16, jnp.int32
    dma = pltpu.SemaphoreType.DMA
    columns, diagonal = pl.pallas_call(
        fused_kernel,
        out_shape=(
            jax.ShapeDtypeStruct((NS, share, width), f32),
            jax.ShapeDtypeStruct((NS, depth, width), f32),
        ),
        in_specs=[smem, smem, smem, hbm, hbm, vmem, vmem, vmem],
        out_specs=(vmem, vmem),
        scratch_shapes=[
            pltpu.VMEM((n_col, n_pole, n_row, share, group), bf16),
            pltpu.VMEM((n_row, n_col, group, width), bf16),
            pltpu.VMEM((n_col, group, width), bf16),
            pltpu.VMEM((n_row, NS, n_col * group), i32),
            pltpu.VMEM((pairs, width, width), bf16),
            pltpu.VMEM((2, group, total), bf16),
            pltpu.VMEM((n_pole, n_row, share, total), f32),
            pltpu.VMEM((2, n_row, share, total), f32),
            pltpu.VMEM((2, n_row // 2, share, total), i16),
            pltpu.VMEM((2, n_row // 2, 1, total), f32),
            pltpu.VMEM((2, n_row // 2, share, total), i16),
            pltpu.VMEM((2, n_row // 2, 1, total), f32),
            pltpu.VMEM((n_row, share, total), i16),
            pltpu.VMEM((n_row, 1, total), f32),
            pltpu.VMEM((n_row, share, total), i16),
            pltpu.VMEM((n_row, 1, total), f32),
            pltpu.VMEM((NS * (NS + 1) // 2, width, width), f32),
            pltpu.VMEM((NS, width, width), f32),
            pltpu.VMEM((n_pole, n_row, depth, total), f32),
            pltpu.VMEM((2, n_row, depth, total), f32),
            pltpu.VMEM((n_row, depth, total), f32),
            pltpu.VMEM((n_row, depth, total), f32),
            pltpu.VMEM((n_row, depth, total), f32),
            pltpu.VMEM((n_row, depth, total), f32),
            pltpu.VMEM((depth, total), f32),
            pltpu.VMEM((depth, total), f32),
            dma((2,)), dma((2,)), dma((2,)), dma((n_col, n_pole)),
            dma((n_row, 2, 2)), dma((n_row, 2)), dma((n_row, 2)), dma((n_row, 2)),
            dma((2, 2)), dma((2, 2)), dma((2, 2)), dma((2, 2)), dma((n_row, 2)), dma((n_row, 2)),
            dma((2,)), dma((2,)), dma, dma, dma((n_row,)), dma((n_row,)), dma, dma,
        ],
        compiler_params=pltpu.CompilerParams(
            collective_id=0, has_side_effects=True, vmem_limit_bytes=67043328
        ),
        name="fused",
    )(weights, pole_order, panel_root, rows, slab, row_map, upper_blocks[0], diag_inverse[0])
    return columns[:, None], diagonal


def fits(mesh, window, upper_blocks):
    n_row, n_col, n_pole = (mesh.shape[name] for name in ("row", "col", "pole"))
    share = window.shape[1] // (n_row * n_col * n_pole)
    depth = upper_blocks.shape[3] // (n_row * n_pole)
    return n_col == 2 and n_pole == 4 and n_row % 2 == 0 and share % 128 == 0 and depth % 8 == 0


def solution(mesh):
    step = jax.shard_map(
        staged,
        mesh=mesh,
        in_specs=(
            P("pole", "col", "row"),
            P("pole", "col", "row", None),
            P(None, "row"),
            P("pole", None),
            P("pole", None, "row", None),
            P("pole", None, "row", None),
            P(),
            P("pole"),
        ),
        out_specs=(P(None, "col", ("row", "pole"), None), P(None, ("row", "pole"), None)),
        check_vma=False,
    )
    staged_step = step
    fused_step = jax.shard_map(
        fused,
        mesh=mesh,
        in_specs=(
            P("pole", "col", "row"),
            P("pole", "col", "row", None),
            P(None, "row"),
            P("pole", None),
            P("pole", None, "row", None),
            P("pole", None, "row", None),
            P(),
            P("pole"),
        ),
        out_specs=(P(None, "col", ("row", "pole"), None), P(None, ("row", "pole"), None)),
        check_vma=False,
    )

    def chosen(window, panels, row_map, panel_root, upper_blocks, *rest):
        one = fused_step if fits(mesh, window, upper_blocks) else staged_step
        return one(window, panels, row_map, panel_root, upper_blocks, *rest)

    return chosen
```

```python
import jax
import jax.numpy as jnp
from jax import lax
from jax.experimental import pallas as pl
from jax.experimental.pallas import tpu as pltpu
from jax.sharding import PartitionSpec as P


NS = 3
CHUNKS = 2


def precise(left, right):
    return jnp.dot(left, right, precision=lax.Precision.HIGHEST, preferred_element_type=jnp.float32)


def pair_index(current, earlier):
    return current * (current - 1) // 2 + earlier


def split(value):
    high = value.astype(jnp.bfloat16)
    return high, (value - high.astype(jnp.float32)).astype(jnp.bfloat16)


def pick(stacked, index, axis=0):
    return lax.dynamic_index_in_dim(stacked, index, axis, keepdims=False)


def swap(block, axis_name, bit):
    size = lax.axis_size(axis_name)
    return lax.ppermute(block, axis_name, [(i, i ^ bit) for i in range(size)])


def shift(block, axis_name, distance):
    size = lax.axis_size(axis_name)
    return lax.ppermute(block, axis_name, [(i, (i + distance) % size) for i in range(size)])


def encode(value):
    top = jnp.maximum(jnp.max(jnp.abs(value), axis=-1), 1e-30)
    return jnp.round(value * (32000.0 / top)[..., None]).astype(jnp.int16), top


def decode(code, top):
    return code.astype(jnp.float32) * (top * (1.0 / 32000.0))[..., None]


def halving_sum(blocks, axis_name, bit):
    size = lax.axis_size(axis_name)
    index = lax.axis_index(axis_name)
    while bit < size:
        side = (index // bit) % 2
        paired = blocks.reshape((blocks.shape[0], blocks.shape[1] // 2, 2) + blocks.shape[2:])
        blocks = pick(paired, side, 2) + swap(pick(paired, 1 - side, 2), axis_name, bit)
        bit *= 2
    return blocks[:, 0]


def shift_sum(blocks, axis_name):
    size = lax.axis_size(axis_name)
    index = lax.axis_index(axis_name)
    total = pick(blocks, index)
    arrived = []
    for distance in range(1, size):
        arrived.append(shift(pick(blocks, (index + distance) % size), axis_name, distance))
    return sum(arrived, total)


def coded_sum(blocks, axis_name):
    size = lax.axis_size(axis_name)
    index = lax.axis_index(axis_name)
    total = pick(blocks, index)
    code, top = encode(blocks)
    arrived = []
    for distance in range(1, size):
        at = (index + distance) % size
        sent = shift(pick(code, at), axis_name, distance)
        arrived.append(decode(sent, shift(pick(top, at), axis_name, distance)))
    return sum(arrived, total)


def shift_gather(block, axis_name):
    size = lax.axis_size(axis_name)
    blocks = [block]
    for distance in range(1, size):
        blocks.append(shift(block, axis_name, distance))
    return blocks


def reorder_kernel(slab_ref, map_ref, rows_ref, out_ref):
    size = rows_ref.shape[2]
    chosen = lax.broadcasted_iota(jnp.int32, (size, size), 0) == map_ref[0, 0]
    out_ref[...] = lax.dot_general(
        jnp.where(chosen, 1.0, 0.0).astype(rows_ref.dtype),
        rows_ref[0, 0],
        (((0,), (0,)), ((), ())),
        preferred_element_type=jnp.float32,
    ).astype(out_ref.dtype)


def reorder(slab_index, maps, sources):
    _, groups, group, width = sources.shape
    return pl.pallas_call(
        reorder_kernel,
        out_shape=jax.ShapeDtypeStruct((groups * group, NS * width), sources.dtype),
        grid_spec=pltpu.PrefetchScalarGridSpec(
            num_scalar_prefetch=1,
            grid=(groups, NS),
            in_specs=[
                pl.BlockSpec((1, 1, 1, group), lambda a, k, slabs: (a, k, 0, 0)),
                pl.BlockSpec((1, 1, group, width), lambda a, k, slabs: (slabs[k], a, 0, 0)),
            ],
            out_specs=pl.BlockSpec((group, width), lambda a, k, slabs: (a, k)),
        ),
        cost_estimate=pl.CostEstimate(
            flops=2 * groups * NS * group * group * width,
            bytes_accessed=4 * groups * NS * group * width,
            transcendentals=0,
        ),
    )(slab_index, maps[:, :, None], sources)


def window_kernel(core_ref, weight_ref, window_ref, aligned_ref, factor_ref, away_ref, keep_ref):
    width = factor_ref.shape[2]
    half = pl.num_programs(0) // 2
    y_window = jnp.dot(window_ref[0], aligned_ref[...], preferred_element_type=jnp.float32)
    y_window = y_window * weight_ref[0]
    columns, parts = [], []
    for k in range(NS):
        column = y_window[:, k * width : (k + 1) * width]
        for m in range(k):
            for part in parts[m]:
                column = column - jnp.dot(
                    part, factor_ref[pair_index(k, m)], preferred_element_type=jnp.float32
                )
        columns.append(column)
        parts.append(split(column))

    @pl.when(pl.program_id(0) < half)
    def _():
        for k in range(NS):
            away_ref[0, 0, :, k * width : (k + 1) * width] = columns[k]

    @pl.when(pl.program_id(0) >= half)
    def _():
        for k in range(NS):
            keep_ref[0, 0, :, k * width : (k + 1) * width] = columns[k]


def window_columns(place, scale, window_rows, aligned, factors, other, n_row, n_pole):
    share = window_rows.shape[1]
    side = n_pole // 4
    half = n_row * side
    depth, total = aligned.shape

    def window_at(i, place_ref):
        j = i % half
        core = jnp.where(i < half, 1 - place_ref[1], place_ref[1])
        second = 1 - place_ref[2] if other else place_ref[2]
        return (j // side) * n_pole + (j % side) * 4 + second * 2 + core, 0, 0

    def away_at(i, place_ref):
        j = jnp.minimum(i, half - 1)
        return j // side, j % side, 0, 0

    def keep_at(i, place_ref):
        j = jnp.maximum(i - half, 0)
        return j // side, j % side, 0, 0

    shape = jax.ShapeDtypeStruct((n_row, side, share, total), jnp.float32)
    return pl.pallas_call(
        window_kernel,
        out_shape=(shape, shape),
        grid_spec=pltpu.PrefetchScalarGridSpec(
            num_scalar_prefetch=1,
            grid=(2 * half,),
            in_specs=[
                pl.BlockSpec(memory_space=pltpu.SMEM),
                pl.BlockSpec((1, share, depth), window_at),
                pl.BlockSpec((depth, total), lambda i, c: (0, 0)),
                pl.BlockSpec(factors.shape, lambda i, c: (0, 0, 0)),
            ],
            out_specs=(
                pl.BlockSpec((1, 1, share, total), away_at),
                pl.BlockSpec((1, 1, share, total), keep_at),
            ),
        ),
        cost_estimate=pl.CostEstimate(
            flops=4 * half * share * depth * total,
            bytes_accessed=4 * half * share * (depth + 2 * total),
            transcendentals=0,
        ),
    )(place, scale, window_rows, aligned, factors)


def inner_kernel(place_ref, own_away_ref, own_keep_ref, away_ref, keep_ref, sum_ref):
    width = sum_ref.shape[1]

    @pl.when((pl.program_id(0) == 0) & (pl.program_id(1) == 0))
    def _():
        sum_ref[...] = jnp.zeros_like(sum_ref)

    for own_ref, term_ref in ((own_away_ref, away_ref), (own_keep_ref, keep_ref)):
        for m in range(NS):
            for part in split(term_ref[0, 0, :, m * width : (m + 1) * width]):
                for k in range(m, NS):
                    sum_ref[k * (k + 1) // 2 + m] += lax.dot_general(
                        own_ref[0, 0, :, k * width : (k + 1) * width],
                        part,
                        (((0,), (0,)), ((), ())),
                        preferred_element_type=jnp.float32,
                    )


def inner_products(place, own, away, keep, other, width):
    n_row, side, share, total = away.shape
    n_pole = 4 * side

    def own_at(flip):
        def at(d, j, place_ref):
            core = 1 - place_ref[1] if flip else place_ref[1]
            second = 1 - place_ref[2] if other else place_ref[2]
            return d, j * 4 + second * 2 + core, 0, 0

        return at

    def term_at(d, j, place_ref):
        return (place_ref[0] - d + n_row) % n_row, j, 0, 0

    pairs = NS * (NS + 1) // 2
    return pl.pallas_call(
        inner_kernel,
        out_shape=jax.ShapeDtypeStruct((pairs, width, width), jnp.float32),
        grid_spec=pltpu.PrefetchScalarGridSpec(
            num_scalar_prefetch=1,
            grid=(n_row, side),
            in_specs=[
                pl.BlockSpec((1, 1, share, total), own_at(True)),
                pl.BlockSpec((1, 1, share, total), own_at(False)),
                pl.BlockSpec((1, 1, share, total), term_at),
                pl.BlockSpec((1, 1, share, total), term_at),
            ],
            out_specs=pl.BlockSpec((pairs, width, width), lambda d, j, p: (0, 0, 0)),
        ),
        cost_estimate=pl.CostEstimate(
            flops=2 * n_row * n_pole * share * pairs * width * width,
            bytes_accessed=3 * n_row * n_pole * share * total,
            transcendentals=0,
        ),
    )(place, own, own, away, keep)


def staged(window, panels, row_map, panel_root, upper_blocks, diag_inverse, weights, pole_order):
    n_row, n_col, n_pole = (lax.axis_size(name) for name in ("row", "col", "pole"))
    row_index, col_index = lax.axis_index("row"), lax.axis_index("col")
    window_block = window[0]
    slab = panels[0, 0]
    width = slab.shape[1]
    group = window_block.shape[0] // n_row
    share = group // n_pole
    pole_weight = jnp.sum(jnp.where(jnp.arange(weights.shape[0]) == pole_order[0], weights, 0.0))
    pole_index = lax.axis_index("pole")
    core, second = pole_index % 2, (pole_index // 2) % 2
    place = jnp.stack([row_index, core, second]).astype(jnp.int32)
    slab_index = (col_index - panel_root[0] + n_col) % n_col
    local_map = row_map % group
    own_start = col_index * group

    slabs = [slab]
    for distance in range(1, n_col):
        slabs.append(shift(slab, "col", distance))
    own_map = lax.dynamic_slice_in_dim(local_map, own_start, group, 1)
    packed_map = jnp.concatenate([own_map // 32, own_map % 32]).astype(jnp.bfloat16).reshape(-1)
    packed_map = jnp.pad(packed_map, (0, -packed_map.shape[0] % width)).reshape(-1, width)
    part_rows = upper_blocks.shape[2]
    pairs = upper_blocks.shape[1]
    gathered = shift_gather(
        jnp.concatenate([upper_blocks[0].reshape(-1, width), packed_map]), "row"
    )
    own_slab = [shift_gather(lax.dynamic_slice_in_dim(slab, own_start, group, 0), "row")]
    factors = jnp.zeros((pairs, part_rows * n_row, width), upper_blocks.dtype)
    maps = []
    for back, g in enumerate(gathered):
        at = (row_index - back + n_row) % n_row
        factors = lax.dynamic_update_slice_in_dim(
            factors, g[: pairs * part_rows].reshape(pairs, part_rows, width), at * part_rows, 1
        )
        flat = g[pairs * part_rows :].reshape(-1)[: 2 * NS * group].astype(jnp.int32)
        maps.append((flat[: NS * group] * 32 + flat[NS * group :]).reshape(NS, group))

    stacked_slabs = jnp.stack(slabs).reshape(n_col, n_col, group, width)
    stacked_map = jnp.stack([local_map[:, c * group : (c + 1) * group] for c in range(n_col)])
    aligned = reorder(slab_index, stacked_map, stacked_slabs)
    own_slab += [
        shift_gather(lax.dynamic_slice_in_dim(other, own_start, group, 0), "row")
        for other in slabs[1:]
    ]

    window_rows = window_block.reshape(n_row * n_pole, share, window_block.shape[1])
    scale = (-pole_weight).reshape(1)
    first_away, first_keep = window_columns(
        place, scale, window_rows, aligned, factors, True, n_row, n_pole
    )
    last_away, last_keep = window_columns(
        place, scale, window_rows, aligned, factors, False, n_row, n_pole
    )
    first_come = swap(first_away, "pole", 1)
    last_come = swap(last_away, "pole", 1)
    step = share // CHUNKS if share % (8 * CHUNKS) == 0 else share
    pieces = [slice(at, at + step) for at in range(0, share, step)]
    sent = [first_keep[:, :, piece] + first_come[:, :, piece] for piece in pieces]
    kept = [last_keep[:, :, piece] + last_come[:, :, piece] for piece in pieces]
    _, own_slab = lax.optimization_barrier((sent, own_slab))
    column_parts = []
    for away, keep in zip(sent, kept):
        code, top = encode(away)
        code = swap(code, "pole", 2)
        top = swap(top, "pole", 2)
        total = keep + decode(code, top)
        column_parts.append(coded_sum(halving_sum(total, "pole", 4), "row"))
    summed_columns = jnp.stack(
        [
            jnp.concatenate([part[:, k * width : (k + 1) * width] for part in column_parts])
            for k in range(NS)
        ]
    )

    stacked_own = jnp.stack([jnp.stack(blocks) for blocks in own_slab])
    own = reorder(slab_index, jnp.stack(maps), stacked_own)
    own = own.reshape(n_row, n_pole, share, NS * width)
    products = inner_products(place, own, first_away, first_keep, True, width)
    products += inner_products(place, own, last_away, last_keep, False, width)
    inner = {(k, m): products[k * (k + 1) // 2 + m] for k in range(NS) for m in range(k + 1)}

    wide = [factors[e].astype(jnp.float32) for e in range(pairs)]
    spread = jnp.zeros((NS, diag_inverse.shape[2] * n_row, width), jnp.float32)
    spread = lax.dynamic_update_slice_in_dim(
        spread, diag_inverse[0] * (pole_weight / n_col), row_index * diag_inverse.shape[2], 1
    )
    diagonals, crossed = [], {}

    def inverse_block(m, n):
        if m == n:
            return diagonals[m]
        return crossed[m, n] if m < n else crossed[n, m].T

    for k in range(NS):
        diagonal = spread[k] - inner[k, k]
        for m in range(k):
            y_block = inner[k, m].T
            for n in range(k):
                y_block = y_block + precise(inverse_block(m, n), wide[pair_index(k, n)])
            crossed[m, k] = -y_block
            diagonal = diagonal + precise(wide[pair_index(k, m)].T, y_block)
        diagonals.append(diagonal)
    blocks = jnp.concatenate(diagonals, axis=1).reshape(n_row, n_pole, -1, NS * width)
    summed_diagonals = shift_sum(halving_sum(blocks, "pole", 1), "row")
    bit = 1
    while bit < n_col:
        summed_diagonals = summed_diagonals + lax.ppermute(
            summed_diagonals, "col", [(i, i ^ bit) for i in range(n_col)]
        )
        bit *= 2
    summed_diagonals = summed_diagonals.reshape(-1, NS, width).transpose(1, 0, 2)
    return (summed_columns[:, None], summed_diagonals)


MESH = pl.DeviceIdType.MESH
LEVELS = 32000.0
NEAREST = 12582912.0


def code_of(value):
    top = jnp.maximum(jnp.max(jnp.abs(value), axis=0, keepdims=True), 1e-30)
    nearest = (value * (LEVELS / top) + NEAREST) - NEAREST
    return nearest.astype(jnp.int32).astype(jnp.int16), top


def value_of(code, top):
    return code.astype(jnp.int32).astype(jnp.float32) * (top * (1.0 / LEVELS))


def fused_kernel(
    weights_ref, order_ref, root_ref, window_ref, slab_ref, map_ref, upper_ref, diag_ref,
    columns_ref, diagonal_ref,
    win, own_slab, far_slab, maps, fac, al, y, core_in, y_out, y_out_top, y_in, y_in_top,
    z_out, z_out_top, z_in, z_in_top, inner, spread, g_all, g_core, g_out, g_out_top, g_in, g_in_top,
    g_sum, gz_out, gz_out_top, gz_in, gz_in_top, g_x, g_last,
    x_send, x_recv, here, win_sem, own_send, own_recv, small_send, small_recv,
    core_send, core_recv, y_send, y_recv, z_send, z_recv,
    gc_send, gc_recv, gy_send, gy_recv, gz_send, gz_recv, gx_send, gx_recv,
):
    n_row, n_col, n_pole = (lax.axis_size(name) for name in ("row", "col", "pole"))
    r, c, p = (lax.axis_index(name) for name in ("row", "col", "pole"))
    side, core = p // 2, p % 2
    share, width = columns_ref.shape[1:]
    group = share * n_pole
    depth = diagonal_ref.shape[1]
    part = upper_ref.shape[1]
    to_col, to_core, to_side = {"col": 1 - c}, {"pole": side * 2 + 1 - core}, {"pole": (1 - side) * 2 + core}

    def remote(src, dst, send, recv, device):
        return pltpu.make_async_remote_copy(
            src_ref=src, dst_ref=dst, send_sem=send, recv_sem=recv, device_id=device, device_id_type=MESH
        )

    def half(at):
        return pl.ds(pl.multiple_of(at * group, group), group)

    def others():
        return [lax.rem(r + distance, n_row) for distance in range(1, n_row)]

    barrier = pltpu.get_barrier_semaphore()
    for device in [to_col, to_core, to_side] + [{"row": at} for at in others()]:
        pl.semaphore_signal(barrier, inc=1, device_id=device, device_id_type=MESH)
    pl.semaphore_wait(barrier, 2 + n_row)

    def x_copy(at):
        src, dst = ((half(1 - c), own_slab.at[r, 1]), (half(c), far_slab.at[1]))[at]
        return remote(slab_ref.at[src], dst, x_send.at[at], x_recv.at[at], to_col)

    def own_copy(block, j, right, first=False):
        src = slab_ref.at[half(c)] if first else own_slab.at[block, j]
        return remote(
            src, own_slab.at[block, j], own_send.at[block, j, 1 - right], own_recv.at[block, j],
            {"row": r + 1 if right else r - 1},
        )

    def small_copy(at):
        rows = pl.ds(pl.multiple_of(r * part, part), part)
        return (
            remote(upper_ref, fac.at[:, rows], small_send.at[at, 0], small_recv.at[r, 0], {"row": at}),
            remote(
                map_ref.at[:, half(c)], maps.at[r, :, half(c)], small_send.at[at, 1], small_recv.at[r, 1],
                {"row": at},
            ),
        )

    def small_arrival(at):
        rows = pl.ds(pl.multiple_of(at * part, part), part)
        return (
            remote(upper_ref, fac.at[:, rows], small_send.at[at, 0], small_recv.at[at, 0], {"row": at}),
            remote(
                map_ref.at[:, half(c)], maps.at[at, :, half(c)], small_send.at[at, 1], small_recv.at[at, 1],
                {"row": at},
            ),
        )

    def both_ways(j, first):
        for right in (1, 0):
            @pl.when(r < n_row - 1 if right else r > 0)
            def _(right=right):
                own_copy(r, j, right, first).start()

    x_copy(0).start()
    both_ways(0, True)
    x_copy(1).start()
    for at in others():
        for copy in small_copy(at):
            copy.start()
    locals_ = [
        pltpu.make_async_copy(slab_ref.at[half(c)], own_slab.at[r, 0], here.at[0]),
        pltpu.make_async_copy(slab_ref.at[half(1 - c)], far_slab.at[0], here.at[1]),
    ]
    loads = []
    for slot, at in ((0, c), (1, 1 - c)):
        for pole in range(n_pole):
            loads.append(
                pltpu.make_async_copy(
                    window_ref.at[:, pole, :, half(at)], win.at[slot, pole], win_sem.at[slot, pole]
                )
            )
    for copy in locals_ + loads:
        copy.start()

    maps[r] = map_ref[...]
    fac[:, pl.ds(pl.multiple_of(r * part, part), part)] = upper_ref[...]
    weight = jnp.float32(0.0)
    for at in range(weights_ref.shape[0]):
        weight += jnp.where(order_ref[0] == at, weights_ref[at], 0.0)
    inner[...] = jnp.zeros_like(inner)

    def reorder(slot, source, block, at):
        def one(k, carry):
            row = maps[block, pl.ds(k, 1), half(at)] - (block * n_col + at) * group
            chosen = lax.broadcasted_iota(jnp.int32, (group, group), 0) == row
            column = lax.rem(root_ref[0, k] + n_col - c, n_col)
            rows = source[0]
            for j in range(1, n_col):
                rows = jnp.where(column == j, source[j], rows)
            placed = lax.dot_general(
                jnp.where(chosen, 1.0, 0.0).astype(rows.dtype), rows, (((0,), (0,)), ((), ())),
                preferred_element_type=jnp.float32,
            )
            al[slot, :, pl.ds(pl.multiple_of(k * width, width), width)] = placed.astype(al.dtype)
            return carry

        lax.fori_loop(0, NS, one, 0)

    near = jnp.minimum(r, n_row - 1 - r)
    toward = jnp.where(r < n_row - 1 - r, 1, -1)

    def block_at(step):
        odd = lax.rem(step, 2)
        zigzag = r + (2 * odd - 1) * ((step + 1) // 2)
        return jnp.where(step <= 2 * near, zigzag, r + toward * (step - near))

    def passes_on():
        return (r > 0) & (r < n_row - 1)

    def pass_on(step, j):
        @pl.when(passes_on())
        def _():
            block = block_at(step)
            own_copy(block, j, 1).wait_recv()

            @pl.when(block < r)
            def _():
                own_copy(block, j, 1).start()

            @pl.when(block > r)
            def _():
                own_copy(block, j, 0).start()

    x_copy(0).wait_recv()
    both_ways(1, False)
    for copy in locals_:
        copy.wait()
    early = range(1, min(3, n_row))
    reorder(0, own_slab.at[r], r, c)
    for step in early:
        pass_on(step, 0)
    for copy in loads[:n_pole]:
        copy.wait()

    def first_pass(pole, carry):
        left = win[0, pole].reshape(n_row * share, group)
        y[pole] = jnp.dot(left, al[0], preferred_element_type=jnp.float32).reshape(n_row, share, NS * width)
        return carry

    lax.fori_loop(0, n_pole, first_pass, 0)
    x_copy(1).wait_recv()
    reorder(1, far_slab, r, 1 - c)
    for copy in loads[n_pole:]:
        copy.wait()
    for at in others():
        for copy in small_arrival(at):
            copy.wait_recv()

    n_half = n_row // 2

    def core_copy(place, h):
        pole = jnp.where(place == 0, 1 - side, side) * 2 + 1 - core
        rows = pl.ds(h * n_half, n_half)
        return remote(
            y.at[pole, rows], core_in.at[place, rows], core_send.at[place, h], core_recv.at[place, h], to_core
        )

    def y_copy(h):
        return (
            remote(y_out.at[h], y_in.at[h], y_send.at[h, 0], y_recv.at[h, 0], to_side),
            remote(y_out_top.at[h], y_in_top.at[h], y_send.at[h, 1], y_recv.at[h, 1], to_side),
        )

    def last_pass(i, carry):
        kind, h = i // 2, lax.rem(i, 2)
        place = kind // 2
        pole = jnp.where(place == 0, 1 - side, side) * 2 + jnp.where(lax.rem(kind, 2) == 0, 1 - core, core)
        rows = pl.ds(h * n_half, n_half)
        left = win[1, pole, rows].reshape(n_half * share, group)
        total = y[pole, rows].reshape(n_half * share, NS * width)
        total = (total + jnp.dot(left, al[1], preferred_element_type=jnp.float32)) * -weight
        columns, parts = [], []
        for k in range(NS):
            column = total[:, k * width : (k + 1) * width]
            for m in range(k):
                for piece in parts[m]:
                    column = column - jnp.dot(piece, fac[pair_index(k, m)], preferred_element_type=jnp.float32)
            columns.append(column)
            parts.append(split(column))
            y[pole, rows, :, k * width : (k + 1) * width] = column.reshape(n_half, share, width)

        @pl.when(lax.rem(kind, 2) == 0)
        def _():
            core_copy(place, h).start()

        @pl.when(kind == 1)
        def _():
            core_copy(0, h).wait_recv()
            for at in range(n_half):
                code, top = code_of(y[pole, h * n_half + at] + core_in[0, h * n_half + at])
                y_out[h, at] = code
                y_out_top[h, at] = top
            for copy in y_copy(h):
                copy.start()

        @pl.when(i == 3)
        def _():
            for step in early:
                pass_on(step, 1)

        return carry

    lax.fori_loop(0, 8, last_pass, 0)
    mine = side * 2 + core

    def z_copy(at, slot):
        return (
            remote(z_out.at[at], z_in.at[slot], z_send.at[at, 0], z_recv.at[slot, 0], {"row": at}),
            remote(z_out_top.at[at], z_in_top.at[slot], z_send.at[at, 1], z_recv.at[slot, 1], {"row": at}),
        )

    def finish(h):
        core_copy(1, h).wait_recv()
        for copy in y_copy(h):
            copy.wait_recv()
        for at in range(n_half):
            row = h * n_half + at
            total = y[mine, row] + core_in[1, row] + value_of(y_in[h, at], y_in_top[h, at])
            core_in[1, row] = total
            code, top = code_of(total)
            z_out[row] = code
            z_out_top[row] = top

            @pl.when(r != row)
            def _(row=row):
                for copy in z_copy(row, r):
                    copy.start()

    def gather_inner(step, carry):
        block = block_at(step)

        @pl.when(step == 1)
        def _():
            for later in range(3, n_row):
                pass_on(later, 0)

        @pl.when(step > 0)
        def _():
            @pl.when((r == 0) | (r == n_row - 1))
            def _():
                for j in range(2):
                    own_copy(block, j, 1).wait_recv()

            reorder(1, own_slab.at[block], block, c)

        slot = jnp.minimum(step, 1)
        for m in range(NS):
            column = jnp.concatenate(
                [y[pole, block, :, m * width : (m + 1) * width] for pole in range(n_pole)]
            )
            pieces = split(column)
            for k in range(m, NS):
                rows = al[slot, :, k * width : (k + 1) * width]
                for piece in pieces:
                    inner[k * (k + 1) // 2 + m] += lax.dot_general(
                        rows, piece, (((0,), (0,)), ((), ())), preferred_element_type=jnp.float32
                    )

        @pl.when(step == n_row - 2)
        def _():
            for later in range(3, n_row):
                pass_on(later, 1)
            finish(0)
            finish(1)

        return carry

    lax.fori_loop(0, n_row, gather_inner, 0)

    spread[...] = jnp.zeros_like(spread)
    spread[:, pl.ds(pl.multiple_of(r * part, part), part)] = diag_ref[...] * (weight * (1.0 / n_col))
    wide = [fac[e].astype(jnp.float32) for e in range(fac.shape[0])]
    diagonals, crossed = [], {}

    def inverse_block(m, n):
        if m == n:
            return diagonals[m]
        return crossed[m, n] if m < n else crossed[n, m].T

    for k in range(NS):
        diagonal = spread[k] - inner[k * (k + 1) // 2 + k]
        for m in range(k):
            y_block = inner[k * (k + 1) // 2 + m].T
            for n in range(k):
                y_block = y_block + precise(inverse_block(m, n), wide[pair_index(k, n)])
            crossed[m, k] = -y_block
            diagonal = diagonal + precise(wide[pair_index(k, m)].T, y_block)
        diagonals.append(diagonal)
        blocks = diagonal.reshape(n_row, n_pole, depth, width)
        for pole in range(n_pole):
            g_all[pole, :, :, k * width : (k + 1) * width] = blocks[:, pole]

    def gc_copy(at):
        return remote(g_all.at[at * 2 + 1 - core], g_core.at[at], gc_send.at[at], gc_recv.at[at], to_core)

    for at in range(2):
        gc_copy(at).start()
    gc_copy(1 - side).wait_recv()
    away = g_all[(1 - side) * 2 + core] + g_core[1 - side]
    g_out[...], g_out_top[...] = code_of(away.reshape(n_row * depth, NS * width))

    def gy_copies():
        return (
            remote(g_out, g_in, gy_send.at[0], gy_recv.at[0], to_side),
            remote(g_out_top, g_in_top, gy_send.at[1], gy_recv.at[1], to_side),
        )

    for copy in gy_copies():
        copy.start()
    gc_copy(side).wait_recv()
    for copy in gy_copies():
        copy.wait_recv()
    come = value_of(g_in[...], g_in_top[...]).reshape(n_row, depth, NS * width)
    g_sum[...] = g_all[mine] + g_core[side] + come
    for at in range(n_row):
        gz_out[at], gz_out_top[at] = code_of(g_sum[at])

    def gz_copy(at, slot):
        return (
            remote(gz_out.at[at], gz_in.at[slot], gz_send.at[at, 0], gz_recv.at[slot, 0], {"row": at}),
            remote(gz_out_top.at[at], gz_in_top.at[slot], gz_send.at[at, 1], gz_recv.at[slot, 1], {"row": at}),
        )

    for at in others():
        for copy in gz_copy(at, r):
            copy.start()

    total = core_in[1, r]
    for at in others():
        for copy in z_copy(at, at):
            copy.wait_recv()
        total = total + value_of(z_in[at], z_in_top[at])
    for k in range(NS):
        columns_ref[k] = total[:, k * width : (k + 1) * width]

    total = g_sum[r]
    for at in others():
        for copy in gz_copy(at, at):
            copy.wait_recv()
        total = total + value_of(gz_in[at], gz_in_top[at])
    g_last[...] = total
    gx_copy = remote(g_last, g_x, gx_send, gx_recv, to_col)
    gx_copy.start()
    gx_copy.wait_recv()
    total = total + g_x[...]
    for k in range(NS):
        diagonal_ref[k] = total[:, k * width : (k + 1) * width]

    for at in range(2):
        x_copy(at).wait_send()
        gc_copy(at).wait_send()
        for h in range(2):
            core_copy(at, h).wait_send()
        for copy in y_copy(at):
            copy.wait_send()
    for copy in gy_copies():
        copy.wait_send()
    gx_copy.wait_send()
    for at in others():
        for copy in small_copy(at) + z_copy(at, r) + gz_copy(at, r):
            copy.wait_send()
    for j in range(2):
        for right in (1, 0):
            @pl.when(r < n_row - 1 if right else r > 0)
            def _(right=right, j=j):
                own_copy(r, j, right, j == 0).wait_send()

        for step in range(1, n_row):
            @pl.when(passes_on())
            def _(step=step, j=j):
                block = block_at(step)

                @pl.when(block < r)
                def _():
                    own_copy(block, j, 1).wait_send()

                @pl.when(block > r)
                def _():
                    own_copy(block, j, 0).wait_send()


def fused(window, panels, row_map, panel_root, upper_blocks, diag_inverse, weights, pole_order):
    n_row, n_col, n_pole = (lax.axis_size(name) for name in ("row", "col", "pole"))
    slab = panels[0, 0]
    width = slab.shape[1]
    group = window.shape[1] // n_row
    share = group // n_pole
    depth = width // (n_row * n_pole)
    pairs = upper_blocks.shape[1]
    total = NS * width
    rows = window[0].reshape(n_row, n_pole, share, n_col * group)
    smem, vmem, hbm = (pl.BlockSpec(memory_space=m) for m in (pltpu.SMEM, pltpu.VMEM, pl.ANY))
    bf16, f32, i16, i32 = jnp.bfloat16, jnp.float32, jnp.int16, jnp.int32
    dma = pltpu.SemaphoreType.DMA
    columns, diagonal = pl.pallas_call(
        fused_kernel,
        out_shape=(
            jax.ShapeDtypeStruct((NS, share, width), f32),
            jax.ShapeDtypeStruct((NS, depth, width), f32),
        ),
        in_specs=[smem, smem, smem, hbm, hbm, vmem, vmem, vmem],
        out_specs=(vmem, vmem),
        scratch_shapes=[
            pltpu.VMEM((n_col, n_pole, n_row, share, group), bf16),
            pltpu.VMEM((n_row, n_col, group, width), bf16),
            pltpu.VMEM((n_col, group, width), bf16),
            pltpu.VMEM((n_row, NS, n_col * group), i32),
            pltpu.VMEM((pairs, width, width), bf16),
            pltpu.VMEM((2, group, total), bf16),
            pltpu.VMEM((n_pole, n_row, share, total), f32),
            pltpu.VMEM((2, n_row, share, total), f32),
            pltpu.VMEM((2, n_row // 2, share, total), i16),
            pltpu.VMEM((2, n_row // 2, 1, total), f32),
            pltpu.VMEM((2, n_row // 2, share, total), i16),
            pltpu.VMEM((2, n_row // 2, 1, total), f32),
            pltpu.VMEM((n_row, share, total), i16),
            pltpu.VMEM((n_row, 1, total), f32),
            pltpu.VMEM((n_row, share, total), i16),
            pltpu.VMEM((n_row, 1, total), f32),
            pltpu.VMEM((NS * (NS + 1) // 2, width, width), f32),
            pltpu.VMEM((NS, width, width), f32),
            pltpu.VMEM((n_pole, n_row, depth, total), f32),
            pltpu.VMEM((2, n_row, depth, total), f32),
            pltpu.VMEM((n_row * depth, total), i16),
            pltpu.VMEM((1, total), f32),
            pltpu.VMEM((n_row * depth, total), i16),
            pltpu.VMEM((1, total), f32),
            pltpu.VMEM((n_row, depth, total), f32),
            pltpu.VMEM((n_row, depth, total), i16),
            pltpu.VMEM((n_row, 1, total), f32),
            pltpu.VMEM((n_row, depth, total), i16),
            pltpu.VMEM((n_row, 1, total), f32),
            pltpu.VMEM((depth, total), f32),
            pltpu.VMEM((depth, total), f32),
            dma((2,)), dma((2,)), dma((2,)), dma((n_col, n_pole)),
            dma((n_row, 2, 2)), dma((n_row, 2)), dma((n_row, 2)), dma((n_row, 2)),
            dma((2, 2)), dma((2, 2)), dma((2, 2)), dma((2, 2)), dma((n_row, 2)), dma((n_row, 2)),
            dma((2,)), dma((2,)), dma((2,)), dma((2,)), dma((n_row, 2)), dma((n_row, 2)), dma, dma,
        ],
        compiler_params=pltpu.CompilerParams(
            collective_id=0, has_side_effects=True, vmem_limit_bytes=67043328
        ),
        name="fused",
    )(weights, pole_order, panel_root, rows, slab, row_map, upper_blocks[0], diag_inverse[0])
    return columns[:, None], diagonal


def fits(mesh, window, upper_blocks):
    n_row, n_col, n_pole = (mesh.shape[name] for name in ("row", "col", "pole"))
    share = window.shape[1] // (n_row * n_col * n_pole)
    depth = upper_blocks.shape[3] // (n_row * n_pole)
    return n_col == 2 and n_pole == 4 and n_row % 2 == 0 and share % 128 == 0 and depth % 8 == 0


def solution(mesh):
    step = jax.shard_map(
        staged,
        mesh=mesh,
        in_specs=(
            P("pole", "col", "row"),
            P("pole", "col", "row", None),
            P(None, "row"),
            P("pole", None),
            P("pole", None, "row", None),
            P("pole", None, "row", None),
            P(),
            P("pole"),
        ),
        out_specs=(P(None, "col", ("row", "pole"), None), P(None, ("row", "pole"), None)),
        check_vma=False,
    )
    staged_step = step
    fused_step = jax.shard_map(
        fused,
        mesh=mesh,
        in_specs=(
            P("pole", "col", "row"),
            P("pole", "col", "row", None),
            P(None, "row"),
            P("pole", None),
            P("pole", None, "row", None),
            P("pole", None, "row", None),
            P(),
            P("pole"),
        ),
        out_specs=(P(None, "col", ("row", "pole"), None), P(None, ("row", "pole"), None)),
        check_vma=False,
    )

    def chosen(window, panels, row_map, panel_root, upper_blocks, *rest):
        one = fused_step if fits(mesh, window, upper_blocks) else staged_step
        return one(window, panels, row_map, panel_root, upper_blocks, *rest)

    return chosen
```

```python
import jax
import jax.numpy as jnp
from jax import lax
from jax.experimental import pallas as pl
from jax.experimental.pallas import tpu as pltpu
from jax.sharding import PartitionSpec as P


NS = 3
CHUNKS = 2


def precise(left, right):
    return jnp.dot(left, right, precision=lax.Precision.HIGHEST, preferred_element_type=jnp.float32)


def pair_index(current, earlier):
    return current * (current - 1) // 2 + earlier


def split(value):
    high = value.astype(jnp.bfloat16)
    return high, (value - high.astype(jnp.float32)).astype(jnp.bfloat16)


def pick(stacked, index, axis=0):
    return lax.dynamic_index_in_dim(stacked, index, axis, keepdims=False)


def swap(block, axis_name, bit):
    size = lax.axis_size(axis_name)
    return lax.ppermute(block, axis_name, [(i, i ^ bit) for i in range(size)])


def shift(block, axis_name, distance):
    size = lax.axis_size(axis_name)
    return lax.ppermute(block, axis_name, [(i, (i + distance) % size) for i in range(size)])


def encode(value):
    top = jnp.maximum(jnp.max(jnp.abs(value), axis=-1), 1e-30)
    return jnp.round(value * (32000.0 / top)[..., None]).astype(jnp.int16), top


def decode(code, top):
    return code.astype(jnp.float32) * (top * (1.0 / 32000.0))[..., None]


def halving_sum(blocks, axis_name, bit):
    size = lax.axis_size(axis_name)
    index = lax.axis_index(axis_name)
    while bit < size:
        side = (index // bit) % 2
        paired = blocks.reshape((blocks.shape[0], blocks.shape[1] // 2, 2) + blocks.shape[2:])
        blocks = pick(paired, side, 2) + swap(pick(paired, 1 - side, 2), axis_name, bit)
        bit *= 2
    return blocks[:, 0]


def shift_sum(blocks, axis_name):
    size = lax.axis_size(axis_name)
    index = lax.axis_index(axis_name)
    total = pick(blocks, index)
    arrived = []
    for distance in range(1, size):
        arrived.append(shift(pick(blocks, (index + distance) % size), axis_name, distance))
    return sum(arrived, total)


def coded_sum(blocks, axis_name):
    size = lax.axis_size(axis_name)
    index = lax.axis_index(axis_name)
    total = pick(blocks, index)
    code, top = encode(blocks)
    arrived = []
    for distance in range(1, size):
        at = (index + distance) % size
        sent = shift(pick(code, at), axis_name, distance)
        arrived.append(decode(sent, shift(pick(top, at), axis_name, distance)))
    return sum(arrived, total)


def shift_gather(block, axis_name):
    size = lax.axis_size(axis_name)
    blocks = [block]
    for distance in range(1, size):
        blocks.append(shift(block, axis_name, distance))
    return blocks


def reorder_kernel(slab_ref, map_ref, rows_ref, out_ref):
    size = rows_ref.shape[2]
    chosen = lax.broadcasted_iota(jnp.int32, (size, size), 0) == map_ref[0, 0]
    out_ref[...] = lax.dot_general(
        jnp.where(chosen, 1.0, 0.0).astype(rows_ref.dtype),
        rows_ref[0, 0],
        (((0,), (0,)), ((), ())),
        preferred_element_type=jnp.float32,
    ).astype(out_ref.dtype)


def reorder(slab_index, maps, sources):
    _, groups, group, width = sources.shape
    return pl.pallas_call(
        reorder_kernel,
        out_shape=jax.ShapeDtypeStruct((groups * group, NS * width), sources.dtype),
        grid_spec=pltpu.PrefetchScalarGridSpec(
            num_scalar_prefetch=1,
            grid=(groups, NS),
            in_specs=[
                pl.BlockSpec((1, 1, 1, group), lambda a, k, slabs: (a, k, 0, 0)),
                pl.BlockSpec((1, 1, group, width), lambda a, k, slabs: (slabs[k], a, 0, 0)),
            ],
            out_specs=pl.BlockSpec((group, width), lambda a, k, slabs: (a, k)),
        ),
        cost_estimate=pl.CostEstimate(
            flops=2 * groups * NS * group * group * width,
            bytes_accessed=4 * groups * NS * group * width,
            transcendentals=0,
        ),
    )(slab_index, maps[:, :, None], sources)


def window_kernel(core_ref, weight_ref, window_ref, aligned_ref, factor_ref, away_ref, keep_ref):
    width = factor_ref.shape[2]
    half = pl.num_programs(0) // 2
    y_window = jnp.dot(window_ref[0], aligned_ref[...], preferred_element_type=jnp.float32)
    y_window = y_window * weight_ref[0]
    columns, parts = [], []
    for k in range(NS):
        column = y_window[:, k * width : (k + 1) * width]
        for m in range(k):
            for part in parts[m]:
                column = column - jnp.dot(
                    part, factor_ref[pair_index(k, m)], preferred_element_type=jnp.float32
                )
        columns.append(column)
        parts.append(split(column))

    @pl.when(pl.program_id(0) < half)
    def _():
        for k in range(NS):
            away_ref[0, 0, :, k * width : (k + 1) * width] = columns[k]

    @pl.when(pl.program_id(0) >= half)
    def _():
        for k in range(NS):
            keep_ref[0, 0, :, k * width : (k + 1) * width] = columns[k]


def window_columns(place, scale, window_rows, aligned, factors, other, n_row, n_pole):
    share = window_rows.shape[1]
    side = n_pole // 4
    half = n_row * side
    depth, total = aligned.shape

    def window_at(i, place_ref):
        j = i % half
        core = jnp.where(i < half, 1 - place_ref[1], place_ref[1])
        second = 1 - place_ref[2] if other else place_ref[2]
        return (j // side) * n_pole + (j % side) * 4 + second * 2 + core, 0, 0

    def away_at(i, place_ref):
        j = jnp.minimum(i, half - 1)
        return j // side, j % side, 0, 0

    def keep_at(i, place_ref):
        j = jnp.maximum(i - half, 0)
        return j // side, j % side, 0, 0

    shape = jax.ShapeDtypeStruct((n_row, side, share, total), jnp.float32)
    return pl.pallas_call(
        window_kernel,
        out_shape=(shape, shape),
        grid_spec=pltpu.PrefetchScalarGridSpec(
            num_scalar_prefetch=1,
            grid=(2 * half,),
            in_specs=[
                pl.BlockSpec(memory_space=pltpu.SMEM),
                pl.BlockSpec((1, share, depth), window_at),
                pl.BlockSpec((depth, total), lambda i, c: (0, 0)),
                pl.BlockSpec(factors.shape, lambda i, c: (0, 0, 0)),
            ],
            out_specs=(
                pl.BlockSpec((1, 1, share, total), away_at),
                pl.BlockSpec((1, 1, share, total), keep_at),
            ),
        ),
        cost_estimate=pl.CostEstimate(
            flops=4 * half * share * depth * total,
            bytes_accessed=4 * half * share * (depth + 2 * total),
            transcendentals=0,
        ),
    )(place, scale, window_rows, aligned, factors)


def inner_kernel(place_ref, own_away_ref, own_keep_ref, away_ref, keep_ref, sum_ref):
    width = sum_ref.shape[1]

    @pl.when((pl.program_id(0) == 0) & (pl.program_id(1) == 0))
    def _():
        sum_ref[...] = jnp.zeros_like(sum_ref)

    for own_ref, term_ref in ((own_away_ref, away_ref), (own_keep_ref, keep_ref)):
        for m in range(NS):
            for part in split(term_ref[0, 0, :, m * width : (m + 1) * width]):
                for k in range(m, NS):
                    sum_ref[k * (k + 1) // 2 + m] += lax.dot_general(
                        own_ref[0, 0, :, k * width : (k + 1) * width],
                        part,
                        (((0,), (0,)), ((), ())),
                        preferred_element_type=jnp.float32,
                    )


def inner_products(place, own, away, keep, other, width):
    n_row, side, share, total = away.shape
    n_pole = 4 * side

    def own_at(flip):
        def at(d, j, place_ref):
            core = 1 - place_ref[1] if flip else place_ref[1]
            second = 1 - place_ref[2] if other else place_ref[2]
            return d, j * 4 + second * 2 + core, 0, 0

        return at

    def term_at(d, j, place_ref):
        return (place_ref[0] - d + n_row) % n_row, j, 0, 0

    pairs = NS * (NS + 1) // 2
    return pl.pallas_call(
        inner_kernel,
        out_shape=jax.ShapeDtypeStruct((pairs, width, width), jnp.float32),
        grid_spec=pltpu.PrefetchScalarGridSpec(
            num_scalar_prefetch=1,
            grid=(n_row, side),
            in_specs=[
                pl.BlockSpec((1, 1, share, total), own_at(True)),
                pl.BlockSpec((1, 1, share, total), own_at(False)),
                pl.BlockSpec((1, 1, share, total), term_at),
                pl.BlockSpec((1, 1, share, total), term_at),
            ],
            out_specs=pl.BlockSpec((pairs, width, width), lambda d, j, p: (0, 0, 0)),
        ),
        cost_estimate=pl.CostEstimate(
            flops=2 * n_row * n_pole * share * pairs * width * width,
            bytes_accessed=3 * n_row * n_pole * share * total,
            transcendentals=0,
        ),
    )(place, own, own, away, keep)


def staged(window, panels, row_map, panel_root, upper_blocks, diag_inverse, weights, pole_order):
    n_row, n_col, n_pole = (lax.axis_size(name) for name in ("row", "col", "pole"))
    row_index, col_index = lax.axis_index("row"), lax.axis_index("col")
    window_block = window[0]
    slab = panels[0, 0]
    width = slab.shape[1]
    group = window_block.shape[0] // n_row
    share = group // n_pole
    pole_weight = jnp.sum(jnp.where(jnp.arange(weights.shape[0]) == pole_order[0], weights, 0.0))
    pole_index = lax.axis_index("pole")
    core, second = pole_index % 2, (pole_index // 2) % 2
    place = jnp.stack([row_index, core, second]).astype(jnp.int32)
    slab_index = (col_index - panel_root[0] + n_col) % n_col
    local_map = row_map % group
    own_start = col_index * group

    slabs = [slab]
    for distance in range(1, n_col):
        slabs.append(shift(slab, "col", distance))
    own_map = lax.dynamic_slice_in_dim(local_map, own_start, group, 1)
    packed_map = jnp.concatenate([own_map // 32, own_map % 32]).astype(jnp.bfloat16).reshape(-1)
    packed_map = jnp.pad(packed_map, (0, -packed_map.shape[0] % width)).reshape(-1, width)
    part_rows = upper_blocks.shape[2]
    pairs = upper_blocks.shape[1]
    gathered = shift_gather(jnp.concatenate([upper_blocks[0].reshape(-1, width), packed_map]), "row")
    own_slab = [shift_gather(lax.dynamic_slice_in_dim(slab, own_start, group, 0), "row")]
    factors = jnp.zeros((pairs, part_rows * n_row, width), upper_blocks.dtype)
    maps = []
    for back, g in enumerate(gathered):
        at = (row_index - back + n_row) % n_row
        factors = lax.dynamic_update_slice_in_dim(
            factors, g[: pairs * part_rows].reshape(pairs, part_rows, width), at * part_rows, 1
        )
        flat = g[pairs * part_rows :].reshape(-1)[: 2 * NS * group].astype(jnp.int32)
        maps.append((flat[: NS * group] * 32 + flat[NS * group :]).reshape(NS, group))

    stacked_slabs = jnp.stack(slabs).reshape(n_col, n_col, group, width)
    stacked_map = jnp.stack([local_map[:, c * group : (c + 1) * group] for c in range(n_col)])
    aligned = reorder(slab_index, stacked_map, stacked_slabs)
    own_slab += [shift_gather(lax.dynamic_slice_in_dim(other, own_start, group, 0), "row") for other in slabs[1:]]

    window_rows = window_block.reshape(n_row * n_pole, share, window_block.shape[1])
    scale = (-pole_weight).reshape(1)
    first_away, first_keep = window_columns(
        place, scale, window_rows, aligned, factors, True, n_row, n_pole
    )
    last_away, last_keep = window_columns(
        place, scale, window_rows, aligned, factors, False, n_row, n_pole
    )
    first_come = swap(first_away, "pole", 1)
    last_come = swap(last_away, "pole", 1)
    step = share // CHUNKS if share % (8 * CHUNKS) == 0 else share
    pieces = [slice(at, at + step) for at in range(0, share, step)]
    sent = [first_keep[:, :, piece] + first_come[:, :, piece] for piece in pieces]
    kept = [last_keep[:, :, piece] + last_come[:, :, piece] for piece in pieces]
    _, own_slab = lax.optimization_barrier((sent, own_slab))
    column_parts = []
    for away, keep in zip(sent, kept):
        code, top = encode(away)
        code = swap(code, "pole", 2)
        top = swap(top, "pole", 2)
        total = keep + decode(code, top)
        column_parts.append(coded_sum(halving_sum(total, "pole", 4), "row"))
    summed_columns = jnp.stack(
        [
            jnp.concatenate([part[:, k * width : (k + 1) * width] for part in column_parts])
            for k in range(NS)
        ]
    )

    stacked_own = jnp.stack([jnp.stack(blocks) for blocks in own_slab])
    own = reorder(slab_index, jnp.stack(maps), stacked_own)
    own = own.reshape(n_row, n_pole, share, NS * width)
    products = inner_products(place, own, first_away, first_keep, True, width)
    products += inner_products(place, own, last_away, last_keep, False, width)
    inner = {(k, m): products[k * (k + 1) // 2 + m] for k in range(NS) for m in range(k + 1)}

    wide = [factors[e].astype(jnp.float32) for e in range(pairs)]
    spread = jnp.zeros((NS, diag_inverse.shape[2] * n_row, width), jnp.float32)
    spread = lax.dynamic_update_slice_in_dim(
        spread, diag_inverse[0] * (pole_weight / n_col), row_index * diag_inverse.shape[2], 1
    )
    diagonals, crossed = [], {}

    def inverse_block(m, n):
        if m == n:
            return diagonals[m]
        return crossed[m, n] if m < n else crossed[n, m].T

    for k in range(NS):
        diagonal = spread[k] - inner[k, k]
        for m in range(k):
            y_block = inner[k, m].T
            for n in range(k):
                y_block = y_block + precise(inverse_block(m, n), wide[pair_index(k, n)])
            crossed[m, k] = -y_block
            diagonal = diagonal + precise(wide[pair_index(k, m)].T, y_block)
        diagonals.append(diagonal)
    blocks = jnp.concatenate(diagonals, axis=1).reshape(n_row, n_pole, -1, NS * width)
    summed_diagonals = shift_sum(halving_sum(blocks, "pole", 1), "row")
    bit = 1
    while bit < n_col:
        summed_diagonals = summed_diagonals + lax.ppermute(
            summed_diagonals, "col", [(i, i ^ bit) for i in range(n_col)]
        )
        bit *= 2
    summed_diagonals = summed_diagonals.reshape(-1, NS, width).transpose(1, 0, 2)
    return (summed_columns[:, None], summed_diagonals)


MESH = pl.DeviceIdType.MESH
LEVELS = 32000.0
NEAREST = 12582912.0


def code_of(value):
    top = jnp.maximum(jnp.max(jnp.abs(value), axis=0, keepdims=True), 1e-30)
    nearest = (value * (LEVELS / top) + NEAREST) - NEAREST
    return nearest.astype(jnp.int32).astype(jnp.int16), top


def value_of(code, top):
    return code.astype(jnp.int32).astype(jnp.float32) * (top * (1.0 / LEVELS))


def fused_kernel(
    weights_ref, order_ref, root_ref, window_ref, slab_ref, map_ref, upper_ref, diag_ref,
    columns_ref, diagonal_ref,
    win, own_slab, far_slab, maps, fac, al, y, core_in, y_out, y_out_top, y_in, y_in_top,
    z_out, z_out_top, z_in, z_in_top, inner, spread, g_all, g_core, g_out, g_out_top, g_in, g_in_top,
    g_sum, gz_out, gz_out_top, gz_in, gz_in_top, g_x, g_last,
    x_send, x_recv, here, win_sem, own_send, own_recv, small_send, small_recv,
    core_send, core_recv, y_send, y_recv, z_send, z_recv,
    gc_send, gc_recv, gy_send, gy_recv, gz_send, gz_recv, gx_send, gx_recv,
):
    n_row, n_col, n_pole = (lax.axis_size(name) for name in ("row", "col", "pole"))
    r, c, p = (lax.axis_index(name) for name in ("row", "col", "pole"))
    side, core = p // 2, p % 2
    share, width = columns_ref.shape[1:]
    group = share * n_pole
    depth = diagonal_ref.shape[1]
    part = upper_ref.shape[1]
    to_col, to_core, to_side = {"col": 1 - c}, {"pole": side * 2 + 1 - core}, {"pole": (1 - side) * 2 + core}

    def remote(src, dst, send, recv, device):
        return pltpu.make_async_remote_copy(
            src_ref=src, dst_ref=dst, send_sem=send, recv_sem=recv, device_id=device, device_id_type=MESH
        )

    def half(at):
        return pl.ds(pl.multiple_of(at * group, group), group)

    def others():
        return [lax.rem(r + distance, n_row) for distance in range(1, n_row)]

    barrier = pltpu.get_barrier_semaphore()
    for device in [to_col, to_core, to_side] + [{"row": at} for at in others()]:
        pl.semaphore_signal(barrier, inc=1, device_id=device, device_id_type=MESH)
    pl.semaphore_wait(barrier, 2 + n_row)

    def x_copy(at):
        src, dst = ((half(1 - c), own_slab.at[r, 1]), (half(c), far_slab.at[1]))[at]
        return remote(slab_ref.at[src], dst, x_send.at[at], x_recv.at[at], to_col)

    def own_copy(block, j, right, first=False):
        src = slab_ref.at[half(c)] if first else own_slab.at[block, j]
        return remote(
            src, own_slab.at[block, j], own_send.at[block, j, 1 - right], own_recv.at[block, j],
            {"row": r + 1 if right else r - 1},
        )

    def small_copy(at):
        rows = pl.ds(pl.multiple_of(r * part, part), part)
        return (
            remote(upper_ref, fac.at[:, rows], small_send.at[at, 0], small_recv.at[r, 0], {"row": at}),
            remote(
                map_ref.at[:, half(c)], maps.at[r, :, half(c)], small_send.at[at, 1], small_recv.at[r, 1],
                {"row": at},
            ),
        )

    def small_arrival(at):
        rows = pl.ds(pl.multiple_of(at * part, part), part)
        return (
            remote(upper_ref, fac.at[:, rows], small_send.at[at, 0], small_recv.at[at, 0], {"row": at}),
            remote(
                map_ref.at[:, half(c)], maps.at[at, :, half(c)], small_send.at[at, 1], small_recv.at[at, 1],
                {"row": at},
            ),
        )

    def both_ways(j, first):
        for right in (1, 0):
            @pl.when(r < n_row - 1 if right else r > 0)
            def _(right=right):
                own_copy(r, j, right, first).start()

    x_copy(0).start()
    both_ways(0, True)
    x_copy(1).start()
    for at in others():
        for copy in small_copy(at):
            copy.start()
    locals_ = [
        pltpu.make_async_copy(slab_ref.at[half(c)], own_slab.at[r, 0], here.at[0]),
        pltpu.make_async_copy(slab_ref.at[half(1 - c)], far_slab.at[0], here.at[1]),
    ]
    loads = []
    for slot, at in ((0, c), (1, 1 - c)):
        for pole in range(n_pole):
            loads.append(
                pltpu.make_async_copy(
                    window_ref.at[:, pole, :, half(at)], win.at[slot, pole], win_sem.at[slot, pole]
                )
            )
    for copy in locals_ + loads:
        copy.start()

    maps[r] = map_ref[...]
    fac[:, pl.ds(pl.multiple_of(r * part, part), part)] = upper_ref[...]
    weight = jnp.float32(0.0)
    for at in range(weights_ref.shape[0]):
        weight += jnp.where(order_ref[0] == at, weights_ref[at], 0.0)
    inner[...] = jnp.zeros_like(inner)

    def reorder(slot, source, block, at):
        def one(k, carry):
            row = maps[block, pl.ds(k, 1), half(at)] - (block * n_col + at) * group
            chosen = lax.broadcasted_iota(jnp.int32, (group, group), 0) == row
            column = lax.rem(root_ref[0, k] + n_col - c, n_col)
            rows = source[0]
            for j in range(1, n_col):
                rows = jnp.where(column == j, source[j], rows)
            placed = lax.dot_general(
                jnp.where(chosen, 1.0, 0.0).astype(rows.dtype), rows, (((0,), (0,)), ((), ())),
                preferred_element_type=jnp.float32,
            )
            al[slot, :, pl.ds(pl.multiple_of(k * width, width), width)] = placed.astype(al.dtype)
            return carry

        lax.fori_loop(0, NS, one, 0)

    near = jnp.minimum(r, n_row - 1 - r)
    toward = jnp.where(r < n_row - 1 - r, 1, -1)

    def block_at(step):
        odd = lax.rem(step, 2)
        zigzag = r + (2 * odd - 1) * ((step + 1) // 2)
        return jnp.where(step <= 2 * near, zigzag, r + toward * (step - near))

    def passes_on():
        return (r > 0) & (r < n_row - 1)

    def pass_on(step, j):
        @pl.when(passes_on())
        def _():
            block = block_at(step)
            own_copy(block, j, 1).wait_recv()

            @pl.when(block < r)
            def _():
                own_copy(block, j, 1).start()

            @pl.when(block > r)
            def _():
                own_copy(block, j, 0).start()

    x_copy(0).wait_recv()
    both_ways(1, False)
    for copy in locals_:
        copy.wait()
    early = range(1, min(3, n_row))
    reorder(0, own_slab.at[r], r, c)
    for step in early:
        pass_on(step, 0)
    for copy in loads[:n_pole]:
        copy.wait()

    def first_pass(pole, carry):
        left = win[0, pole].reshape(n_row * share, group)
        y[pole] = jnp.dot(left, al[0], preferred_element_type=jnp.float32).reshape(n_row, share, NS * width)
        return carry

    lax.fori_loop(0, n_pole, first_pass, 0)
    x_copy(1).wait_recv()
    reorder(1, far_slab, r, 1 - c)
    for copy in loads[n_pole:]:
        copy.wait()
    for at in others():
        for copy in small_arrival(at):
            copy.wait_recv()

    n_half = n_row // 2

    def core_copy(place, h):
        pole = jnp.where(place == 0, 1 - side, side) * 2 + 1 - core
        rows = pl.ds(h * n_half, n_half)
        return remote(
            y.at[pole, rows], core_in.at[place, rows], core_send.at[place, h], core_recv.at[place, h], to_core
        )

    def y_copy(h):
        return (
            remote(y_out.at[h], y_in.at[h], y_send.at[h, 0], y_recv.at[h, 0], to_side),
            remote(y_out_top.at[h], y_in_top.at[h], y_send.at[h, 1], y_recv.at[h, 1], to_side),
        )

    low = r < n_half
    far_half = jnp.where(low, 1, 0)

    def last_pass(i, carry):
        kind = i // 2
        h = jnp.where(lax.rem(i, 2) == 0, far_half, 1 - far_half)
        place = kind // 2
        pole = jnp.where(place == 0, 1 - side, side) * 2 + jnp.where(lax.rem(kind, 2) == 0, 1 - core, core)
        rows = pl.ds(h * n_half, n_half)
        left = win[1, pole, rows].reshape(n_half * share, group)
        total = y[pole, rows].reshape(n_half * share, NS * width)
        total = (total + jnp.dot(left, al[1], preferred_element_type=jnp.float32)) * -weight
        columns, parts = [], []
        for k in range(NS):
            column = total[:, k * width : (k + 1) * width]
            for m in range(k):
                for piece in parts[m]:
                    column = column - jnp.dot(piece, fac[pair_index(k, m)], preferred_element_type=jnp.float32)
            columns.append(column)
            parts.append(split(column))
            y[pole, rows, :, k * width : (k + 1) * width] = column.reshape(n_half, share, width)

        @pl.when(lax.rem(kind, 2) == 0)
        def _():
            core_copy(place, h).start()

        @pl.when(kind == 1)
        def _():
            core_copy(0, h).wait_recv()
            for at in range(n_half):
                code, top = code_of(y[pole, h * n_half + at] + core_in[0, h * n_half + at])
                y_out[h, at] = code
                y_out_top[h, at] = top
            for copy in y_copy(h):
                copy.start()

        @pl.when(i == 3)
        def _():
            for step in early:
                pass_on(step, 1)

        return carry

    lax.fori_loop(0, 8, last_pass, 0)
    mine = side * 2 + core

    def z_copy(at, way):
        device = {"row": r + 1 - 2 * way}
        return (
            remote(z_out.at[at], z_in.at[way, at], z_send.at[at, 0], z_recv.at[way, at, 0], device),
            remote(z_out_top.at[at], z_in_top.at[way, at], z_send.at[at, 1], z_recv.at[way, at, 1], device),
        )

    def finish(h):
        core_copy(1, h).wait_recv()
        for copy in y_copy(h):
            copy.wait_recv()
        for at in range(n_half):
            row = h * n_half + at
            core_in[1, row] = y[mine, row] + core_in[1, row] + value_of(y_in[h, at], y_in_top[h, at])

    def add_come(at, way):
        @pl.when(jnp.where(way == 0, r, n_row - 1 - r) > 0)
        def _():
            for copy in z_copy(at, way):
                copy.wait_recv()
            core_in[1, at] = core_in[1, at] + value_of(z_in[way, at], z_in_top[way, at])

    def forward(at, way):
        @pl.when(jnp.where(way == 0, at - r, r - at) > 0)
        def _():
            add_come(at, way)
            z_out[at], z_out_top[at] = code_of(core_in[1, at])
            for copy in z_copy(at, way):
                copy.start()

    def far(n):
        forward(jnp.where(low, n_row - 1 - n, n), jnp.where(low, 0, 1))

    def close(n):
        forward(jnp.where(low, n, n_row - 1 - n), jnp.where(low, 1, 0))

    def gather_inner(step, carry):
        block = block_at(step)

        @pl.when(step == 1)
        def _():
            for later in range(3, n_row):
                pass_on(later, 0)

        @pl.when(step > 0)
        def _():
            @pl.when((r == 0) | (r == n_row - 1))
            def _():
                for j in range(2):
                    own_copy(block, j, 1).wait_recv()

            reorder(1, own_slab.at[block], block, c)

        slot = jnp.minimum(step, 1)
        for m in range(NS):
            column = jnp.concatenate(
                [y[pole, block, :, m * width : (m + 1) * width] for pole in range(n_pole)]
            )
            pieces = split(column)
            for k in range(m, NS):
                rows = al[slot, :, k * width : (k + 1) * width]
                for piece in pieces:
                    inner[k * (k + 1) // 2 + m] += lax.dot_general(
                        rows, piece, (((0,), (0,)), ((), ())), preferred_element_type=jnp.float32
                    )

        @pl.when(step == n_row - 2)
        def _():
            for later in range(3, n_row):
                pass_on(later, 1)
            finish(far_half)

            @pl.when(jnp.logical_not(passes_on()))
            def _():
                for n in range(n_half):
                    far(n)
                finish(1 - far_half)
                for n in range(n_half, n_row - 1):
                    far(n)

        return carry

    lax.fori_loop(0, n_row, gather_inner, 0)

    @pl.when(passes_on())
    def _():
        far(0)
        finish(1 - far_half)
        for n in range(1, n_row - 1):
            far(n)
        for n in range(n_row - 1):
            close(n)


    spread[...] = jnp.zeros_like(spread)
    spread[:, pl.ds(pl.multiple_of(r * part, part), part)] = diag_ref[...] * (weight * (1.0 / n_col))
    wide = [fac[e].astype(jnp.float32) for e in range(fac.shape[0])]
    diagonals, crossed = [], {}

    def inverse_block(m, n):
        if m == n:
            return diagonals[m]
        return crossed[m, n] if m < n else crossed[n, m].T

    for k in range(NS):
        diagonal = spread[k] - inner[k * (k + 1) // 2 + k]
        for m in range(k):
            y_block = inner[k * (k + 1) // 2 + m].T
            for n in range(k):
                y_block = y_block + precise(inverse_block(m, n), wide[pair_index(k, n)])
            crossed[m, k] = -y_block
            diagonal = diagonal + precise(wide[pair_index(k, m)].T, y_block)
        diagonals.append(diagonal)
        blocks = diagonal.reshape(n_row, n_pole, depth, width)
        for pole in range(n_pole):
            g_all[pole, :, :, k * width : (k + 1) * width] = blocks[:, pole]

    def gc_copy(at):
        return remote(g_all.at[at * 2 + 1 - core], g_core.at[at], gc_send.at[at], gc_recv.at[at], to_core)

    for at in range(2):
        gc_copy(at).start()
    gc_copy(1 - side).wait_recv()
    away = g_all[(1 - side) * 2 + core] + g_core[1 - side]
    g_out[...], g_out_top[...] = code_of(away.reshape(n_row * depth, NS * width))

    def gy_copies():
        return (
            remote(g_out, g_in, gy_send.at[0], gy_recv.at[0], to_side),
            remote(g_out_top, g_in_top, gy_send.at[1], gy_recv.at[1], to_side),
        )

    for copy in gy_copies():
        copy.start()
    gc_copy(side).wait_recv()
    for copy in gy_copies():
        copy.wait_recv()
    come = value_of(g_in[...], g_in_top[...]).reshape(n_row, depth, NS * width)
    g_sum[...] = g_all[mine] + g_core[side] + come
    for at in range(n_row):
        gz_out[at], gz_out_top[at] = code_of(g_sum[at])

    def gz_copy(at, slot):
        return (
            remote(gz_out.at[at], gz_in.at[slot], gz_send.at[at, 0], gz_recv.at[slot, 0], {"row": at}),
            remote(gz_out_top.at[at], gz_in_top.at[slot], gz_send.at[at, 1], gz_recv.at[slot, 1], {"row": at}),
        )

    for at in others():
        for copy in gz_copy(at, r):
            copy.start()

    for way in range(2):
        add_come(r, way)
    total = core_in[1, r]
    for k in range(NS):
        columns_ref[k] = total[:, k * width : (k + 1) * width]

    total = g_sum[r]
    for at in others():
        for copy in gz_copy(at, at):
            copy.wait_recv()
        total = total + value_of(gz_in[at], gz_in_top[at])
    g_last[...] = total
    gx_copy = remote(g_last, g_x, gx_send, gx_recv, to_col)
    gx_copy.start()
    gx_copy.wait_recv()
    total = total + g_x[...]
    for k in range(NS):
        diagonal_ref[k] = total[:, k * width : (k + 1) * width]

    for at in range(2):
        x_copy(at).wait_send()
        gc_copy(at).wait_send()
        for h in range(2):
            core_copy(at, h).wait_send()
        for copy in y_copy(at):
            copy.wait_send()
    for copy in gy_copies():
        copy.wait_send()
    gx_copy.wait_send()
    for at in others():
        for copy in small_copy(at) + z_copy(at, 0) + gz_copy(at, r):
            copy.wait_send()
    for j in range(2):
        for right in (1, 0):
            @pl.when(r < n_row - 1 if right else r > 0)
            def _(right=right, j=j):
                own_copy(r, j, right, j == 0).wait_send()

        for step in range(1, n_row):
            @pl.when(passes_on())
            def _(step=step, j=j):
                block = block_at(step)

                @pl.when(block < r)
                def _():
                    own_copy(block, j, 1).wait_send()

                @pl.when(block > r)
                def _():
                    own_copy(block, j, 0).wait_send()


def fused(window, panels, row_map, panel_root, upper_blocks, diag_inverse, weights, pole_order):
    n_row, n_col, n_pole = (lax.axis_size(name) for name in ("row", "col", "pole"))
    slab = panels[0, 0]
    width = slab.shape[1]
    group = window.shape[1] // n_row
    share = group // n_pole
    depth = width // (n_row * n_pole)
    pairs = upper_blocks.shape[1]
    total = NS * width
    rows = window[0].reshape(n_row, n_pole, share, n_col * group)
    smem, vmem, hbm = (pl.BlockSpec(memory_space=m) for m in (pltpu.SMEM, pltpu.VMEM, pl.ANY))
    bf16, f32, i16, i32 = jnp.bfloat16, jnp.float32, jnp.int16, jnp.int32
    dma = pltpu.SemaphoreType.DMA
    columns, diagonal = pl.pallas_call(
        fused_kernel,
        out_shape=(
            jax.ShapeDtypeStruct((NS, share, width), f32),
            jax.ShapeDtypeStruct((NS, depth, width), f32),
        ),
        in_specs=[smem, smem, smem, hbm, hbm, vmem, vmem, vmem],
        out_specs=(vmem, vmem),
        scratch_shapes=[
            pltpu.VMEM((n_col, n_pole, n_row, share, group), bf16),
            pltpu.VMEM((n_row, n_col, group, width), bf16),
            pltpu.VMEM((n_col, group, width), bf16),
            pltpu.VMEM((n_row, NS, n_col * group), i32),
            pltpu.VMEM((pairs, width, width), bf16),
            pltpu.VMEM((2, group, total), bf16),
            pltpu.VMEM((n_pole, n_row, share, total), f32),
            pltpu.VMEM((2, n_row, share, total), f32),
            pltpu.VMEM((2, n_row // 2, share, total), i16),
            pltpu.VMEM((2, n_row // 2, 1, total), f32),
            pltpu.VMEM((2, n_row // 2, share, total), i16),
            pltpu.VMEM((2, n_row // 2, 1, total), f32),
            pltpu.VMEM((n_row, share, total), i16),
            pltpu.VMEM((n_row, 1, total), f32),
            pltpu.VMEM((2, n_row, share, total), i16),
            pltpu.VMEM((2, n_row, 1, total), f32),
            pltpu.VMEM((NS * (NS + 1) // 2, width, width), f32),
            pltpu.VMEM((NS, width, width), f32),
            pltpu.VMEM((n_pole, n_row, depth, total), f32),
            pltpu.VMEM((2, n_row, depth, total), f32),
            pltpu.VMEM((n_row * depth, total), i16),
            pltpu.VMEM((1, total), f32),
            pltpu.VMEM((n_row * depth, total), i16),
            pltpu.VMEM((1, total), f32),
            pltpu.VMEM((n_row, depth, total), f32),
            pltpu.VMEM((n_row, depth, total), i16),
            pltpu.VMEM((n_row, 1, total), f32),
            pltpu.VMEM((n_row, depth, total), i16),
            pltpu.VMEM((n_row, 1, total), f32),
            pltpu.VMEM((depth, total), f32),
            pltpu.VMEM((depth, total), f32),
            dma((2,)), dma((2,)), dma((2,)), dma((n_col, n_pole)),
            dma((n_row, 2, 2)), dma((n_row, 2)), dma((n_row, 2)), dma((n_row, 2)),
            dma((2, 2)), dma((2, 2)), dma((2, 2)), dma((2, 2)), dma((n_row, 2)), dma((2, n_row, 2)),
            dma((2,)), dma((2,)), dma((2,)), dma((2,)), dma((n_row, 2)), dma((n_row, 2)), dma, dma,
        ],
        compiler_params=pltpu.CompilerParams(
            collective_id=0, has_side_effects=True, vmem_limit_bytes=67043328
        ),
        name="fused",
    )(weights, pole_order, panel_root, rows, slab, row_map, upper_blocks[0], diag_inverse[0])
    return columns[:, None], diagonal


def fits(mesh, window, upper_blocks):
    n_row, n_col, n_pole = (mesh.shape[name] for name in ("row", "col", "pole"))
    share = window.shape[1] // (n_row * n_col * n_pole)
    depth = upper_blocks.shape[3] // (n_row * n_pole)
    return n_col == 2 and n_pole == 4 and n_row % 2 == 0 and share % 128 == 0 and depth % 8 == 0


def solution(mesh):
    step = jax.shard_map(
        staged,
        mesh=mesh,
        in_specs=(
            P("pole", "col", "row"),
            P("pole", "col", "row", None),
            P(None, "row"),
            P("pole", None),
            P("pole", None, "row", None),
            P("pole", None, "row", None),
            P(),
            P("pole"),
        ),
        out_specs=(P(None, "col", ("row", "pole"), None), P(None, ("row", "pole"), None)),
        check_vma=False,
    )
    staged_step = step
    fused_step = jax.shard_map(
        fused,
        mesh=mesh,
        in_specs=(
            P("pole", "col", "row"),
            P("pole", "col", "row", None),
            P(None, "row"),
            P("pole", None),
            P("pole", None, "row", None),
            P("pole", None, "row", None),
            P(),
            P("pole"),
        ),
        out_specs=(P(None, "col", ("row", "pole"), None), P(None, ("row", "pole"), None)),
        check_vma=False,
    )

    def chosen(window, panels, row_map, panel_root, upper_blocks, *rest):
        one = fused_step if fits(mesh, window, upper_blocks) else staged_step
        return one(window, panels, row_map, panel_root, upper_blocks, *rest)

    return chosen
```

```python
import jax
import jax.numpy as jnp
from jax import lax
from jax.experimental import pallas as pl
from jax.experimental.pallas import tpu as pltpu
from jax.sharding import PartitionSpec as P


NS = 3
CHUNKS = 2


def precise(left, right):
    return jnp.dot(left, right, precision=lax.Precision.HIGHEST, preferred_element_type=jnp.float32)


def pair_index(current, earlier):
    return current * (current - 1) // 2 + earlier


def split(value):
    high = value.astype(jnp.bfloat16)
    return high, (value - high.astype(jnp.float32)).astype(jnp.bfloat16)


def pick(stacked, index, axis=0):
    return lax.dynamic_index_in_dim(stacked, index, axis, keepdims=False)


def swap(block, axis_name, bit):
    size = lax.axis_size(axis_name)
    return lax.ppermute(block, axis_name, [(i, i ^ bit) for i in range(size)])


def shift(block, axis_name, distance):
    size = lax.axis_size(axis_name)
    return lax.ppermute(block, axis_name, [(i, (i + distance) % size) for i in range(size)])


def encode(value):
    top = jnp.maximum(jnp.max(jnp.abs(value), axis=-1), 1e-30)
    return jnp.round(value * (32000.0 / top)[..., None]).astype(jnp.int16), top


def decode(code, top):
    return code.astype(jnp.float32) * (top * (1.0 / 32000.0))[..., None]


def halving_sum(blocks, axis_name, bit):
    size = lax.axis_size(axis_name)
    index = lax.axis_index(axis_name)
    while bit < size:
        side = (index // bit) % 2
        paired = blocks.reshape((blocks.shape[0], blocks.shape[1] // 2, 2) + blocks.shape[2:])
        blocks = pick(paired, side, 2) + swap(pick(paired, 1 - side, 2), axis_name, bit)
        bit *= 2
    return blocks[:, 0]


def shift_sum(blocks, axis_name):
    size = lax.axis_size(axis_name)
    index = lax.axis_index(axis_name)
    total = pick(blocks, index)
    arrived = []
    for distance in range(1, size):
        arrived.append(shift(pick(blocks, (index + distance) % size), axis_name, distance))
    return sum(arrived, total)


def coded_sum(blocks, axis_name):
    size = lax.axis_size(axis_name)
    index = lax.axis_index(axis_name)
    total = pick(blocks, index)
    code, top = encode(blocks)
    arrived = []
    for distance in range(1, size):
        at = (index + distance) % size
        sent = shift(pick(code, at), axis_name, distance)
        arrived.append(decode(sent, shift(pick(top, at), axis_name, distance)))
    return sum(arrived, total)


def shift_gather(block, axis_name):
    size = lax.axis_size(axis_name)
    blocks = [block]
    for distance in range(1, size):
        blocks.append(shift(block, axis_name, distance))
    return blocks


def reorder_kernel(slab_ref, map_ref, rows_ref, out_ref):
    size = rows_ref.shape[2]
    chosen = lax.broadcasted_iota(jnp.int32, (size, size), 0) == map_ref[0, 0]
    out_ref[...] = lax.dot_general(
        jnp.where(chosen, 1.0, 0.0).astype(rows_ref.dtype),
        rows_ref[0, 0],
        (((0,), (0,)), ((), ())),
        preferred_element_type=jnp.float32,
    ).astype(out_ref.dtype)


def reorder(slab_index, maps, sources):
    _, groups, group, width = sources.shape
    return pl.pallas_call(
        reorder_kernel,
        out_shape=jax.ShapeDtypeStruct((groups * group, NS * width), sources.dtype),
        grid_spec=pltpu.PrefetchScalarGridSpec(
            num_scalar_prefetch=1,
            grid=(groups, NS),
            in_specs=[
                pl.BlockSpec((1, 1, 1, group), lambda a, k, slabs: (a, k, 0, 0)),
                pl.BlockSpec((1, 1, group, width), lambda a, k, slabs: (slabs[k], a, 0, 0)),
            ],
            out_specs=pl.BlockSpec((group, width), lambda a, k, slabs: (a, k)),
        ),
        cost_estimate=pl.CostEstimate(
            flops=2 * groups * NS * group * group * width,
            bytes_accessed=4 * groups * NS * group * width,
            transcendentals=0,
        ),
    )(slab_index, maps[:, :, None], sources)


def window_kernel(core_ref, weight_ref, window_ref, aligned_ref, factor_ref, away_ref, keep_ref):
    width = factor_ref.shape[2]
    half = pl.num_programs(0) // 2
    y_window = jnp.dot(window_ref[0], aligned_ref[...], preferred_element_type=jnp.float32)
    y_window = y_window * weight_ref[0]
    columns, parts = [], []
    for k in range(NS):
        column = y_window[:, k * width : (k + 1) * width]
        for m in range(k):
            for part in parts[m]:
                column = column - jnp.dot(
                    part, factor_ref[pair_index(k, m)], preferred_element_type=jnp.float32
                )
        columns.append(column)
        parts.append(split(column))

    @pl.when(pl.program_id(0) < half)
    def _():
        for k in range(NS):
            away_ref[0, 0, :, k * width : (k + 1) * width] = columns[k]

    @pl.when(pl.program_id(0) >= half)
    def _():
        for k in range(NS):
            keep_ref[0, 0, :, k * width : (k + 1) * width] = columns[k]


def window_columns(place, scale, window_rows, aligned, factors, other, n_row, n_pole):
    share = window_rows.shape[1]
    side = n_pole // 4
    half = n_row * side
    depth, total = aligned.shape

    def window_at(i, place_ref):
        j = i % half
        core = jnp.where(i < half, 1 - place_ref[1], place_ref[1])
        second = 1 - place_ref[2] if other else place_ref[2]
        return (j // side) * n_pole + (j % side) * 4 + second * 2 + core, 0, 0

    def away_at(i, place_ref):
        j = jnp.minimum(i, half - 1)
        return j // side, j % side, 0, 0

    def keep_at(i, place_ref):
        j = jnp.maximum(i - half, 0)
        return j // side, j % side, 0, 0

    shape = jax.ShapeDtypeStruct((n_row, side, share, total), jnp.float32)
    return pl.pallas_call(
        window_kernel,
        out_shape=(shape, shape),
        grid_spec=pltpu.PrefetchScalarGridSpec(
            num_scalar_prefetch=1,
            grid=(2 * half,),
            in_specs=[
                pl.BlockSpec(memory_space=pltpu.SMEM),
                pl.BlockSpec((1, share, depth), window_at),
                pl.BlockSpec((depth, total), lambda i, c: (0, 0)),
                pl.BlockSpec(factors.shape, lambda i, c: (0, 0, 0)),
            ],
            out_specs=(
                pl.BlockSpec((1, 1, share, total), away_at),
                pl.BlockSpec((1, 1, share, total), keep_at),
            ),
        ),
        cost_estimate=pl.CostEstimate(
            flops=4 * half * share * depth * total,
            bytes_accessed=4 * half * share * (depth + 2 * total),
            transcendentals=0,
        ),
    )(place, scale, window_rows, aligned, factors)


def inner_kernel(place_ref, own_away_ref, own_keep_ref, away_ref, keep_ref, sum_ref):
    width = sum_ref.shape[1]

    @pl.when((pl.program_id(0) == 0) & (pl.program_id(1) == 0))
    def _():
        sum_ref[...] = jnp.zeros_like(sum_ref)

    for own_ref, term_ref in ((own_away_ref, away_ref), (own_keep_ref, keep_ref)):
        for m in range(NS):
            for part in split(term_ref[0, 0, :, m * width : (m + 1) * width]):
                for k in range(m, NS):
                    sum_ref[k * (k + 1) // 2 + m] += lax.dot_general(
                        own_ref[0, 0, :, k * width : (k + 1) * width],
                        part,
                        (((0,), (0,)), ((), ())),
                        preferred_element_type=jnp.float32,
                    )


def inner_products(place, own, away, keep, other, width):
    n_row, side, share, total = away.shape
    n_pole = 4 * side

    def own_at(flip):
        def at(d, j, place_ref):
            core = 1 - place_ref[1] if flip else place_ref[1]
            second = 1 - place_ref[2] if other else place_ref[2]
            return d, j * 4 + second * 2 + core, 0, 0

        return at

    def term_at(d, j, place_ref):
        return (place_ref[0] - d + n_row) % n_row, j, 0, 0

    pairs = NS * (NS + 1) // 2
    return pl.pallas_call(
        inner_kernel,
        out_shape=jax.ShapeDtypeStruct((pairs, width, width), jnp.float32),
        grid_spec=pltpu.PrefetchScalarGridSpec(
            num_scalar_prefetch=1,
            grid=(n_row, side),
            in_specs=[
                pl.BlockSpec((1, 1, share, total), own_at(True)),
                pl.BlockSpec((1, 1, share, total), own_at(False)),
                pl.BlockSpec((1, 1, share, total), term_at),
                pl.BlockSpec((1, 1, share, total), term_at),
            ],
            out_specs=pl.BlockSpec((pairs, width, width), lambda d, j, p: (0, 0, 0)),
        ),
        cost_estimate=pl.CostEstimate(
            flops=2 * n_row * n_pole * share * pairs * width * width,
            bytes_accessed=3 * n_row * n_pole * share * total,
            transcendentals=0,
        ),
    )(place, own, own, away, keep)


def staged(window, panels, row_map, panel_root, upper_blocks, diag_inverse, weights, pole_order):
    n_row, n_col, n_pole = (lax.axis_size(name) for name in ("row", "col", "pole"))
    row_index, col_index = lax.axis_index("row"), lax.axis_index("col")
    window_block = window[0]
    slab = panels[0, 0]
    width = slab.shape[1]
    group = window_block.shape[0] // n_row
    share = group // n_pole
    pole_weight = jnp.sum(jnp.where(jnp.arange(weights.shape[0]) == pole_order[0], weights, 0.0))
    pole_index = lax.axis_index("pole")
    core, second = pole_index % 2, (pole_index // 2) % 2
    place = jnp.stack([row_index, core, second]).astype(jnp.int32)
    slab_index = (col_index - panel_root[0] + n_col) % n_col
    local_map = row_map % group
    own_start = col_index * group

    slabs = [slab]
    for distance in range(1, n_col):
        slabs.append(shift(slab, "col", distance))
    own_map = lax.dynamic_slice_in_dim(local_map, own_start, group, 1)
    packed_map = jnp.concatenate([own_map // 32, own_map % 32]).astype(jnp.bfloat16).reshape(-1)
    packed_map = jnp.pad(packed_map, (0, -packed_map.shape[0] % width)).reshape(-1, width)
    part_rows = upper_blocks.shape[2]
    pairs = upper_blocks.shape[1]
    gathered = shift_gather(jnp.concatenate([upper_blocks[0].reshape(-1, width), packed_map]), "row")
    own_slab = [shift_gather(lax.dynamic_slice_in_dim(slab, own_start, group, 0), "row")]
    factors = jnp.zeros((pairs, part_rows * n_row, width), upper_blocks.dtype)
    maps = []
    for back, g in enumerate(gathered):
        at = (row_index - back + n_row) % n_row
        factors = lax.dynamic_update_slice_in_dim(
            factors, g[: pairs * part_rows].reshape(pairs, part_rows, width), at * part_rows, 1
        )
        flat = g[pairs * part_rows :].reshape(-1)[: 2 * NS * group].astype(jnp.int32)
        maps.append((flat[: NS * group] * 32 + flat[NS * group :]).reshape(NS, group))

    stacked_slabs = jnp.stack(slabs).reshape(n_col, n_col, group, width)
    stacked_map = jnp.stack([local_map[:, c * group : (c + 1) * group] for c in range(n_col)])
    aligned = reorder(slab_index, stacked_map, stacked_slabs)
    own_slab += [shift_gather(lax.dynamic_slice_in_dim(other, own_start, group, 0), "row") for other in slabs[1:]]

    window_rows = window_block.reshape(n_row * n_pole, share, window_block.shape[1])
    scale = (-pole_weight).reshape(1)
    first_away, first_keep = window_columns(
        place, scale, window_rows, aligned, factors, True, n_row, n_pole
    )
    last_away, last_keep = window_columns(
        place, scale, window_rows, aligned, factors, False, n_row, n_pole
    )
    first_come = swap(first_away, "pole", 1)
    last_come = swap(last_away, "pole", 1)
    step = share // CHUNKS if share % (8 * CHUNKS) == 0 else share
    pieces = [slice(at, at + step) for at in range(0, share, step)]
    sent = [first_keep[:, :, piece] + first_come[:, :, piece] for piece in pieces]
    kept = [last_keep[:, :, piece] + last_come[:, :, piece] for piece in pieces]
    _, own_slab = lax.optimization_barrier((sent, own_slab))
    column_parts = []
    for away, keep in zip(sent, kept):
        code, top = encode(away)
        code = swap(code, "pole", 2)
        top = swap(top, "pole", 2)
        total = keep + decode(code, top)
        column_parts.append(coded_sum(halving_sum(total, "pole", 4), "row"))
    summed_columns = jnp.stack(
        [
            jnp.concatenate([part[:, k * width : (k + 1) * width] for part in column_parts])
            for k in range(NS)
        ]
    )

    stacked_own = jnp.stack([jnp.stack(blocks) for blocks in own_slab])
    own = reorder(slab_index, jnp.stack(maps), stacked_own)
    own = own.reshape(n_row, n_pole, share, NS * width)
    products = inner_products(place, own, first_away, first_keep, True, width)
    products += inner_products(place, own, last_away, last_keep, False, width)
    inner = {(k, m): products[k * (k + 1) // 2 + m] for k in range(NS) for m in range(k + 1)}

    wide = [factors[e].astype(jnp.float32) for e in range(pairs)]
    spread = jnp.zeros((NS, diag_inverse.shape[2] * n_row, width), jnp.float32)
    spread = lax.dynamic_update_slice_in_dim(
        spread, diag_inverse[0] * (pole_weight / n_col), row_index * diag_inverse.shape[2], 1
    )
    diagonals, crossed = [], {}

    def inverse_block(m, n):
        if m == n:
            return diagonals[m]
        return crossed[m, n] if m < n else crossed[n, m].T

    for k in range(NS):
        diagonal = spread[k] - inner[k, k]
        for m in range(k):
            y_block = inner[k, m].T
            for n in range(k):
                y_block = y_block + precise(inverse_block(m, n), wide[pair_index(k, n)])
            crossed[m, k] = -y_block
            diagonal = diagonal + precise(wide[pair_index(k, m)].T, y_block)
        diagonals.append(diagonal)
    blocks = jnp.concatenate(diagonals, axis=1).reshape(n_row, n_pole, -1, NS * width)
    summed_diagonals = shift_sum(halving_sum(blocks, "pole", 1), "row")
    bit = 1
    while bit < n_col:
        summed_diagonals = summed_diagonals + lax.ppermute(
            summed_diagonals, "col", [(i, i ^ bit) for i in range(n_col)]
        )
        bit *= 2
    summed_diagonals = summed_diagonals.reshape(-1, NS, width).transpose(1, 0, 2)
    return (summed_columns[:, None], summed_diagonals)


MESH = pl.DeviceIdType.MESH
LEVELS = 32000.0
NEAREST = 12582912.0


def code_of(value):
    top = jnp.maximum(jnp.max(jnp.abs(value), axis=0, keepdims=True), 1e-30)
    nearest = (value * (LEVELS / top) + NEAREST) - NEAREST
    return nearest.astype(jnp.int32).astype(jnp.int16), top


def value_of(code, top):
    return code.astype(jnp.int32).astype(jnp.float32) * (top * (1.0 / LEVELS))


def fused_kernel(
    weights_ref, order_ref, root_ref, window_ref, slab_ref, map_ref, upper_ref, diag_ref,
    columns_ref, diagonal_ref,
    win, own_slab, far_slab, maps, fac, al, y, core_in, y_out, y_out_top, y_in, y_in_top,
    z_out, z_out_top, z_in, z_in_top, inner, spread, g_all, g_core, g_out, g_out_top, g_in, g_in_top,
    g_sum, gz_out, gz_out_top, gz_in, gz_in_top, g_x, g_last,
    x_send, x_recv, here, win_sem, own_send, own_recv, small_send, small_recv, share_send, share_recv,
    core_send, core_recv, y_send, y_recv, z_send, z_recv,
    gc_send, gc_recv, gy_send, gy_recv, gz_send, gz_recv, gx_send, gx_recv,
):
    n_row, n_col, n_pole = (lax.axis_size(name) for name in ("row", "col", "pole"))
    r, c, p = (lax.axis_index(name) for name in ("row", "col", "pole"))
    side, core = p // 2, p % 2
    share, width = columns_ref.shape[1:]
    group = share * n_pole
    depth = diagonal_ref.shape[1]
    part = upper_ref.shape[1]
    to_col, to_core, to_side = {"col": 1 - c}, {"pole": side * 2 + 1 - core}, {"pole": (1 - side) * 2 + core}

    def remote(src, dst, send, recv, device):
        return pltpu.make_async_remote_copy(
            src_ref=src, dst_ref=dst, send_sem=send, recv_sem=recv, device_id=device, device_id_type=MESH
        )

    def half(at):
        return pl.ds(pl.multiple_of(at * group, group), group)

    def others():
        return [lax.rem(r + distance, n_row) for distance in range(1, n_row)]

    barrier = pltpu.get_barrier_semaphore()
    for device in [to_col, to_core, to_side] + [{"row": at} for at in others()]:
        pl.semaphore_signal(barrier, inc=1, device_id=device, device_id_type=MESH)
    pl.semaphore_wait(barrier, 2 + n_row)

    def x_copy(at):
        src, dst = ((half(1 - c), own_slab.at[r, 1]), (half(c), far_slab.at[1]))[at]
        return remote(slab_ref.at[src], dst, x_send.at[at], x_recv.at[at], to_col)

    def own_copy(block, j, right, first=False):
        src = slab_ref.at[half(c)] if first else own_slab.at[block, j]
        return remote(
            src, own_slab.at[block, j], own_send.at[block, j, 1 - right], own_recv.at[block, j],
            {"row": r + 1 if right else r - 1},
        )

    piece = part // n_col

    def small_copy(at, sender):
        mine_at = pl.ds(pl.multiple_of(c * piece, piece), piece)
        rows = pl.ds(pl.multiple_of(sender * part + c * piece, piece), piece)
        return (
            remote(
                upper_ref.at[:, mine_at], fac.at[:, rows], small_send.at[at, 0], small_recv.at[sender, 0],
                {"row": at},
            ),
            remote(
                map_ref.at[:, half(c)], maps.at[sender, :, half(c)], small_send.at[at, 1],
                small_recv.at[sender, 1], {"row": at},
            ),
        )

    def share_copy(at, column):
        rows = pl.ds(pl.multiple_of(at * part + column * piece, piece), piece)
        return remote(fac.at[:, rows], fac.at[:, rows], share_send.at[at], share_recv.at[at], to_col)

    def both_ways(j, first):
        for right in (1, 0):
            @pl.when(r < n_row - 1 if right else r > 0)
            def _(right=right):
                own_copy(r, j, right, first).start()

    x_copy(0).start()
    both_ways(0, True)
    x_copy(1).start()
    for at in others():
        for copy in small_copy(at, r):
            copy.start()
    locals_ = [
        pltpu.make_async_copy(slab_ref.at[half(c)], own_slab.at[r, 0], here.at[0]),
        pltpu.make_async_copy(slab_ref.at[half(1 - c)], far_slab.at[0], here.at[1]),
    ]
    loads = []
    for slot, at in ((0, c), (1, 1 - c)):
        for pole in range(n_pole):
            loads.append(
                pltpu.make_async_copy(
                    window_ref.at[:, pole, :, half(at)], win.at[slot, pole], win_sem.at[slot, pole]
                )
            )
    for copy in locals_ + loads:
        copy.start()

    maps[r] = map_ref[...]
    fac[:, pl.ds(pl.multiple_of(r * part, part), part)] = upper_ref[...]
    weight = jnp.float32(0.0)
    for at in range(weights_ref.shape[0]):
        weight += jnp.where(order_ref[0] == at, weights_ref[at], 0.0)
    inner[...] = jnp.zeros_like(inner)

    def reorder(slot, source, block, at):
        def one(k, carry):
            row = maps[block, pl.ds(k, 1), half(at)] - (block * n_col + at) * group
            chosen = lax.broadcasted_iota(jnp.int32, (group, group), 0) == row
            column = lax.rem(root_ref[0, k] + n_col - c, n_col)
            rows = source[0]
            for j in range(1, n_col):
                rows = jnp.where(column == j, source[j], rows)
            placed = lax.dot_general(
                jnp.where(chosen, 1.0, 0.0).astype(rows.dtype), rows, (((0,), (0,)), ((), ())),
                preferred_element_type=jnp.float32,
            )
            al[slot, :, pl.ds(pl.multiple_of(k * width, width), width)] = placed.astype(al.dtype)
            return carry

        lax.fori_loop(0, NS, one, 0)

    near = jnp.minimum(r, n_row - 1 - r)
    toward = jnp.where(r < n_row - 1 - r, 1, -1)

    def block_at(step):
        odd = lax.rem(step, 2)
        zigzag = r + (2 * odd - 1) * ((step + 1) // 2)
        return jnp.where(step <= 2 * near, zigzag, r + toward * (step - near))

    def passes_on():
        return (r > 0) & (r < n_row - 1)

    def pass_on(step, j):
        @pl.when(passes_on())
        def _():
            block = block_at(step)
            own_copy(block, j, 1).wait_recv()

            @pl.when(block < r)
            def _():
                own_copy(block, j, 1).start()

            @pl.when(block > r)
            def _():
                own_copy(block, j, 0).start()

    x_copy(0).wait_recv()
    both_ways(1, False)
    for copy in locals_:
        copy.wait()
    early = range(1, min(3, n_row))
    reorder(0, own_slab.at[r], r, c)
    for step in early:
        pass_on(step, 0)
    for copy in loads[:n_pole]:
        copy.wait()

    def first_pass(pole, carry):
        left = win[0, pole].reshape(n_row * share, group)
        y[pole] = jnp.dot(left, al[0], preferred_element_type=jnp.float32).reshape(n_row, share, NS * width)
        return carry

    lax.fori_loop(0, n_pole, first_pass, 0)
    for at in others():
        for copy in small_copy(at, at):
            copy.wait_recv()
        share_copy(at, c).start()
    x_copy(1).wait_recv()
    reorder(1, far_slab, r, 1 - c)
    for copy in loads[n_pole:]:
        copy.wait()
    for at in others():
        share_copy(at, 1 - c).wait_recv()

    n_half = n_row // 2

    def core_copy(place, h):
        pole = jnp.where(place == 0, 1 - side, side) * 2 + 1 - core
        rows = pl.ds(h * n_half, n_half)
        return remote(
            y.at[pole, rows], core_in.at[place, rows], core_send.at[place, h], core_recv.at[place, h], to_core
        )

    def y_copy(h):
        return (
            remote(y_out.at[h], y_in.at[h], y_send.at[h, 0], y_recv.at[h, 0], to_side),
            remote(y_out_top.at[h], y_in_top.at[h], y_send.at[h, 1], y_recv.at[h, 1], to_side),
        )

    low = r < n_half
    far_half = jnp.where(low, 1, 0)

    def last_pass(i, carry):
        kind = i // 2
        h = jnp.where(lax.rem(i, 2) == 0, far_half, 1 - far_half)
        place = kind // 2
        pole = jnp.where(place == 0, 1 - side, side) * 2 + jnp.where(lax.rem(kind, 2) == 0, 1 - core, core)
        rows = pl.ds(h * n_half, n_half)
        left = win[1, pole, rows].reshape(n_half * share, group)
        total = y[pole, rows].reshape(n_half * share, NS * width)
        total = (total + jnp.dot(left, al[1], preferred_element_type=jnp.float32)) * -weight
        columns, parts = [], []
        for k in range(NS):
            column = total[:, k * width : (k + 1) * width]
            for m in range(k):
                for piece in parts[m]:
                    column = column - jnp.dot(piece, fac[pair_index(k, m)], preferred_element_type=jnp.float32)
            columns.append(column)
            parts.append(split(column))
            y[pole, rows, :, k * width : (k + 1) * width] = column.reshape(n_half, share, width)

        @pl.when(lax.rem(kind, 2) == 0)
        def _():
            core_copy(place, h).start()

        @pl.when(kind == 1)
        def _():
            core_copy(0, h).wait_recv()
            for at in range(n_half):
                code, top = code_of(y[pole, h * n_half + at] + core_in[0, h * n_half + at])
                y_out[h, at] = code
                y_out_top[h, at] = top
            for copy in y_copy(h):
                copy.start()

        @pl.when(i == 3)
        def _():
            for step in early:
                pass_on(step, 1)

        return carry

    lax.fori_loop(0, 8, last_pass, 0)
    mine = side * 2 + core

    def z_copy(at, way):
        device = {"row": r + 1 - 2 * way}
        return (
            remote(z_out.at[at], z_in.at[way, at], z_send.at[at, 0], z_recv.at[way, at, 0], device),
            remote(z_out_top.at[at], z_in_top.at[way, at], z_send.at[at, 1], z_recv.at[way, at, 1], device),
        )

    def finish(h):
        core_copy(1, h).wait_recv()
        for copy in y_copy(h):
            copy.wait_recv()
        for at in range(n_half):
            row = h * n_half + at
            core_in[1, row] = y[mine, row] + core_in[1, row] + value_of(y_in[h, at], y_in_top[h, at])

    def add_come(at, way):
        @pl.when(jnp.where(way == 0, r, n_row - 1 - r) > 0)
        def _():
            for copy in z_copy(at, way):
                copy.wait_recv()
            core_in[1, at] = core_in[1, at] + value_of(z_in[way, at], z_in_top[way, at])

    def forward(at, way):
        @pl.when(jnp.where(way == 0, at - r, r - at) > 0)
        def _():
            add_come(at, way)
            z_out[at], z_out_top[at] = code_of(core_in[1, at])
            for copy in z_copy(at, way):
                copy.start()

    def far(n):
        forward(jnp.where(low, n_row - 1 - n, n), jnp.where(low, 0, 1))

    def close(n):
        forward(jnp.where(low, n, n_row - 1 - n), jnp.where(low, 1, 0))

    def gather_inner(step, carry):
        block = block_at(step)

        @pl.when(step == 1)
        def _():
            for later in range(3, n_row):
                pass_on(later, 0)

        @pl.when(step > 0)
        def _():
            @pl.when((r == 0) | (r == n_row - 1))
            def _():
                for j in range(2):
                    own_copy(block, j, 1).wait_recv()

            reorder(1, own_slab.at[block], block, c)

        slot = jnp.minimum(step, 1)
        for m in range(NS):
            column = jnp.concatenate(
                [y[pole, block, :, m * width : (m + 1) * width] for pole in range(n_pole)]
            )
            pieces = split(column)
            for k in range(m, NS):
                rows = al[slot, :, k * width : (k + 1) * width]
                for piece in pieces:
                    inner[k * (k + 1) // 2 + m] += lax.dot_general(
                        rows, piece, (((0,), (0,)), ((), ())), preferred_element_type=jnp.float32
                    )

        @pl.when(step == n_row - 2)
        def _():
            for later in range(3, n_row):
                pass_on(later, 1)
            finish(far_half)

            @pl.when(jnp.logical_not(passes_on()))
            def _():
                for n in range(n_half):
                    far(n)
                finish(1 - far_half)
                for n in range(n_half, n_row - 1):
                    far(n)

        return carry

    lax.fori_loop(0, n_row, gather_inner, 0)

    @pl.when(passes_on())
    def _():
        far(0)
        finish(1 - far_half)
        for n in range(1, n_row - 1):
            far(n)
        for n in range(n_row - 1):
            close(n)


    spread[...] = jnp.zeros_like(spread)
    spread[:, pl.ds(pl.multiple_of(r * part, part), part)] = diag_ref[...] * (weight * (1.0 / n_col))

    def times_factor(left, e):
        return sum(jnp.dot(piece, fac[e], preferred_element_type=jnp.float32) for piece in split(left))

    def factor_times(e, right):
        dims = (((0,), (0,)), ((), ()))
        return sum(
            lax.dot_general(fac[e], piece, dims, preferred_element_type=jnp.float32) for piece in split(right)
        )

    diagonals, crossed = [], {}

    def inverse_block(m, n):
        if m == n:
            return diagonals[m]
        return crossed[m, n] if m < n else crossed[n, m].T

    for k in range(NS):
        diagonal = spread[k] - inner[k * (k + 1) // 2 + k]
        for m in range(k):
            y_block = inner[k * (k + 1) // 2 + m].T
            for n in range(k):
                y_block = y_block + times_factor(inverse_block(m, n), pair_index(k, n))
            crossed[m, k] = -y_block
            diagonal = diagonal + factor_times(pair_index(k, m), y_block)
        diagonals.append(diagonal)
        blocks = diagonal.reshape(n_row, n_pole, depth, width)
        for pole in range(n_pole):
            g_all[pole, :, :, k * width : (k + 1) * width] = blocks[:, pole]

    def gc_copy(at):
        return remote(g_all.at[at * 2 + 1 - core], g_core.at[at], gc_send.at[at], gc_recv.at[at], to_core)

    for at in range(2):
        gc_copy(at).start()
    gc_copy(1 - side).wait_recv()
    away = g_all[(1 - side) * 2 + core] + g_core[1 - side]
    g_out[...], g_out_top[...] = code_of(away.reshape(n_row * depth, NS * width))

    def gy_copies():
        return (
            remote(g_out, g_in, gy_send.at[0], gy_recv.at[0], to_side),
            remote(g_out_top, g_in_top, gy_send.at[1], gy_recv.at[1], to_side),
        )

    for copy in gy_copies():
        copy.start()
    gc_copy(side).wait_recv()
    for copy in gy_copies():
        copy.wait_recv()
    come = value_of(g_in[...], g_in_top[...]).reshape(n_row, depth, NS * width)
    g_sum[...] = g_all[mine] + g_core[side] + come
    for at in range(n_row):
        gz_out[at], gz_out_top[at] = code_of(g_sum[at])

    def gz_copy(at, slot):
        return (
            remote(gz_out.at[at], gz_in.at[slot], gz_send.at[at, 0], gz_recv.at[slot, 0], {"row": at}),
            remote(gz_out_top.at[at], gz_in_top.at[slot], gz_send.at[at, 1], gz_recv.at[slot, 1], {"row": at}),
        )

    for at in others():
        for copy in gz_copy(at, r):
            copy.start()

    for way in range(2):
        add_come(r, way)
    total = core_in[1, r]
    for k in range(NS):
        columns_ref[k] = total[:, k * width : (k + 1) * width]

    total = g_sum[r]
    for at in others():
        for copy in gz_copy(at, at):
            copy.wait_recv()
        total = total + value_of(gz_in[at], gz_in_top[at])
    g_last[...] = total
    gx_copy = remote(g_last, g_x, gx_send, gx_recv, to_col)
    gx_copy.start()
    gx_copy.wait_recv()
    total = total + g_x[...]
    for k in range(NS):
        diagonal_ref[k] = total[:, k * width : (k + 1) * width]

    for at in range(2):
        x_copy(at).wait_send()
        gc_copy(at).wait_send()
        for h in range(2):
            core_copy(at, h).wait_send()
        for copy in y_copy(at):
            copy.wait_send()
    for copy in gy_copies():
        copy.wait_send()
    gx_copy.wait_send()
    for at in others():
        share_copy(at, c).wait_send()
        for copy in small_copy(at, r) + z_copy(at, 0) + gz_copy(at, r):
            copy.wait_send()
    for j in range(2):
        for right in (1, 0):
            @pl.when(r < n_row - 1 if right else r > 0)
            def _(right=right, j=j):
                own_copy(r, j, right, j == 0).wait_send()

        for step in range(1, n_row):
            @pl.when(passes_on())
            def _(step=step, j=j):
                block = block_at(step)

                @pl.when(block < r)
                def _():
                    own_copy(block, j, 1).wait_send()

                @pl.when(block > r)
                def _():
                    own_copy(block, j, 0).wait_send()


def hand_on(columns_ref, diagonal_ref, columns_out, diagonal_out):
    columns_out[...] = columns_ref[...]
    diagonal_out[...] = diagonal_ref[...]


def fused(window, panels, row_map, panel_root, upper_blocks, diag_inverse, weights, pole_order):
    n_row, n_col, n_pole = (lax.axis_size(name) for name in ("row", "col", "pole"))
    slab = panels[0, 0]
    width = slab.shape[1]
    group = window.shape[1] // n_row
    share = group // n_pole
    depth = width // (n_row * n_pole)
    pairs = upper_blocks.shape[1]
    total = NS * width
    rows = window[0].reshape(n_row, n_pole, share, n_col * group)
    smem, vmem, hbm = (pl.BlockSpec(memory_space=m) for m in (pltpu.SMEM, pltpu.VMEM, pl.ANY))
    bf16, f32, i16, i32 = jnp.bfloat16, jnp.float32, jnp.int16, jnp.int32
    dma = pltpu.SemaphoreType.DMA
    columns, diagonal = pl.pallas_call(
        fused_kernel,
        out_shape=(
            jax.ShapeDtypeStruct((NS, share, width), f32),
            jax.ShapeDtypeStruct((NS, depth, width), f32),
        ),
        in_specs=[smem, smem, smem, hbm, hbm, vmem, vmem, vmem],
        out_specs=(vmem, vmem),
        scratch_shapes=[
            pltpu.VMEM((n_col, n_pole, n_row, share, group), bf16),
            pltpu.VMEM((n_row, n_col, group, width), bf16),
            pltpu.VMEM((n_col, group, width), bf16),
            pltpu.VMEM((n_row, NS, n_col * group), i32),
            pltpu.VMEM((pairs, width, width), bf16),
            pltpu.VMEM((2, group, total), bf16),
            pltpu.VMEM((n_pole, n_row, share, total), f32),
            pltpu.VMEM((2, n_row, share, total), f32),
            pltpu.VMEM((2, n_row // 2, share, total), i16),
            pltpu.VMEM((2, n_row // 2, 1, total), f32),
            pltpu.VMEM((2, n_row // 2, share, total), i16),
            pltpu.VMEM((2, n_row // 2, 1, total), f32),
            pltpu.VMEM((n_row, share, total), i16),
            pltpu.VMEM((n_row, 1, total), f32),
            pltpu.VMEM((2, n_row, share, total), i16),
            pltpu.VMEM((2, n_row, 1, total), f32),
            pltpu.VMEM((NS * (NS + 1) // 2, width, width), f32),
            pltpu.VMEM((NS, width, width), f32),
            pltpu.VMEM((n_pole, n_row, depth, total), f32),
            pltpu.VMEM((2, n_row, depth, total), f32),
            pltpu.VMEM((n_row * depth, total), i16),
            pltpu.VMEM((1, total), f32),
            pltpu.VMEM((n_row * depth, total), i16),
            pltpu.VMEM((1, total), f32),
            pltpu.VMEM((n_row, depth, total), f32),
            pltpu.VMEM((n_row, depth, total), i16),
            pltpu.VMEM((n_row, 1, total), f32),
            pltpu.VMEM((n_row, depth, total), i16),
            pltpu.VMEM((n_row, 1, total), f32),
            pltpu.VMEM((depth, total), f32),
            pltpu.VMEM((depth, total), f32),
            dma((2,)), dma((2,)), dma((2,)), dma((n_col, n_pole)),
            dma((n_row, 2, 2)), dma((n_row, 2)), dma((n_row, 2)), dma((n_row, 2)), dma((n_row,)), dma((n_row,)),
            dma((2, 2)), dma((2, 2)), dma((2, 2)), dma((2, 2)), dma((n_row, 2)), dma((2, n_row, 2)),
            dma((2,)), dma((2,)), dma((2,)), dma((2,)), dma((n_row, 2)), dma((n_row, 2)), dma, dma,
        ],
        compiler_params=pltpu.CompilerParams(
            collective_id=0, has_side_effects=True, vmem_limit_bytes=67043328
        ),
        name="fused",
    )(weights, pole_order, panel_root, rows, slab, row_map, upper_blocks[0], diag_inverse[0])
    columns, diagonal = pl.pallas_call(
        hand_on,
        out_shape=(
            jax.ShapeDtypeStruct(columns.shape, f32),
            jax.ShapeDtypeStruct(diagonal.shape, f32),
        ),
        in_specs=[vmem, vmem],
        out_specs=(vmem, vmem),
        compiler_params=pltpu.CompilerParams(vmem_limit_bytes=8 * 2**20),
        name="hand_on",
    )(columns, diagonal)
    return columns[:, None], diagonal


def fits(mesh, window, upper_blocks):
    n_row, n_col, n_pole = (mesh.shape[name] for name in ("row", "col", "pole"))
    share = window.shape[1] // (n_row * n_col * n_pole)
    depth = upper_blocks.shape[3] // (n_row * n_pole)
    return n_col == 2 and n_pole == 4 and n_row % 2 == 0 and share % 128 == 0 and depth % 8 == 0


def solution(mesh):
    step = jax.shard_map(
        staged,
        mesh=mesh,
        in_specs=(
            P("pole", "col", "row"),
            P("pole", "col", "row", None),
            P(None, "row"),
            P("pole", None),
            P("pole", None, "row", None),
            P("pole", None, "row", None),
            P(),
            P("pole"),
        ),
        out_specs=(P(None, "col", ("row", "pole"), None), P(None, ("row", "pole"), None)),
        check_vma=False,
    )
    staged_step = step
    fused_step = jax.shard_map(
        fused,
        mesh=mesh,
        in_specs=(
            P("pole", "col", "row"),
            P("pole", "col", "row", None),
            P(None, "row"),
            P("pole", None),
            P("pole", None, "row", None),
            P("pole", None, "row", None),
            P(),
            P("pole"),
        ),
        out_specs=(P(None, "col", ("row", "pole"), None), P(None, ("row", "pole"), None)),
        check_vma=False,
    )

    def chosen(window, panels, row_map, panel_root, upper_blocks, *rest):
        one = fused_step if fits(mesh, window, upper_blocks) else staged_step
        return one(window, panels, row_map, panel_root, upper_blocks, *rest)

    return chosen
```

```python
import jax
import jax.numpy as jnp
from jax import lax
from jax.experimental import pallas as pl
from jax.experimental.pallas import tpu as pltpu
from jax.sharding import PartitionSpec as P


NS = 3
CHUNKS = 2


def precise(left, right):
    return jnp.dot(left, right, precision=lax.Precision.HIGHEST, preferred_element_type=jnp.float32)


def pair_index(current, earlier):
    return current * (current - 1) // 2 + earlier


def split(value):
    high = value.astype(jnp.bfloat16)
    return high, (value - high.astype(jnp.float32)).astype(jnp.bfloat16)


def pick(stacked, index, axis=0):
    return lax.dynamic_index_in_dim(stacked, index, axis, keepdims=False)


def swap(block, axis_name, bit):
    size = lax.axis_size(axis_name)
    return lax.ppermute(block, axis_name, [(i, i ^ bit) for i in range(size)])


def shift(block, axis_name, distance):
    size = lax.axis_size(axis_name)
    return lax.ppermute(block, axis_name, [(i, (i + distance) % size) for i in range(size)])


def encode(value):
    top = jnp.maximum(jnp.max(jnp.abs(value), axis=-1), 1e-30)
    return jnp.round(value * (32000.0 / top)[..., None]).astype(jnp.int16), top


def decode(code, top):
    return code.astype(jnp.float32) * (top * (1.0 / 32000.0))[..., None]


def halving_sum(blocks, axis_name, bit):
    size = lax.axis_size(axis_name)
    index = lax.axis_index(axis_name)
    while bit < size:
        side = (index // bit) % 2
        paired = blocks.reshape((blocks.shape[0], blocks.shape[1] // 2, 2) + blocks.shape[2:])
        blocks = pick(paired, side, 2) + swap(pick(paired, 1 - side, 2), axis_name, bit)
        bit *= 2
    return blocks[:, 0]


def shift_sum(blocks, axis_name):
    size = lax.axis_size(axis_name)
    index = lax.axis_index(axis_name)
    total = pick(blocks, index)
    arrived = []
    for distance in range(1, size):
        arrived.append(shift(pick(blocks, (index + distance) % size), axis_name, distance))
    return sum(arrived, total)


def coded_sum(blocks, axis_name):
    size = lax.axis_size(axis_name)
    index = lax.axis_index(axis_name)
    total = pick(blocks, index)
    code, top = encode(blocks)
    arrived = []
    for distance in range(1, size):
        at = (index + distance) % size
        sent = shift(pick(code, at), axis_name, distance)
        arrived.append(decode(sent, shift(pick(top, at), axis_name, distance)))
    return sum(arrived, total)


def shift_gather(block, axis_name):
    size = lax.axis_size(axis_name)
    blocks = [block]
    for distance in range(1, size):
        blocks.append(shift(block, axis_name, distance))
    return blocks


def reorder_kernel(slab_ref, map_ref, rows_ref, out_ref):
    size = rows_ref.shape[2]
    chosen = lax.broadcasted_iota(jnp.int32, (size, size), 0) == map_ref[0, 0]
    out_ref[...] = lax.dot_general(
        jnp.where(chosen, 1.0, 0.0).astype(rows_ref.dtype),
        rows_ref[0, 0],
        (((0,), (0,)), ((), ())),
        preferred_element_type=jnp.float32,
    ).astype(out_ref.dtype)


def reorder(slab_index, maps, sources):
    _, groups, group, width = sources.shape
    return pl.pallas_call(
        reorder_kernel,
        out_shape=jax.ShapeDtypeStruct((groups * group, NS * width), sources.dtype),
        grid_spec=pltpu.PrefetchScalarGridSpec(
            num_scalar_prefetch=1,
            grid=(groups, NS),
            in_specs=[
                pl.BlockSpec((1, 1, 1, group), lambda a, k, slabs: (a, k, 0, 0)),
                pl.BlockSpec((1, 1, group, width), lambda a, k, slabs: (slabs[k], a, 0, 0)),
            ],
            out_specs=pl.BlockSpec((group, width), lambda a, k, slabs: (a, k)),
        ),
        cost_estimate=pl.CostEstimate(
            flops=2 * groups * NS * group * group * width,
            bytes_accessed=4 * groups * NS * group * width,
            transcendentals=0,
        ),
    )(slab_index, maps[:, :, None], sources)


def window_kernel(core_ref, weight_ref, window_ref, aligned_ref, factor_ref, away_ref, keep_ref):
    width = factor_ref.shape[2]
    half = pl.num_programs(0) // 2
    y_window = jnp.dot(window_ref[0], aligned_ref[...], preferred_element_type=jnp.float32)
    y_window = y_window * weight_ref[0]
    columns, parts = [], []
    for k in range(NS):
        column = y_window[:, k * width : (k + 1) * width]
        for m in range(k):
            for part in parts[m]:
                column = column - jnp.dot(
                    part, factor_ref[pair_index(k, m)], preferred_element_type=jnp.float32
                )
        columns.append(column)
        parts.append(split(column))

    @pl.when(pl.program_id(0) < half)
    def _():
        for k in range(NS):
            away_ref[0, 0, :, k * width : (k + 1) * width] = columns[k]

    @pl.when(pl.program_id(0) >= half)
    def _():
        for k in range(NS):
            keep_ref[0, 0, :, k * width : (k + 1) * width] = columns[k]


def window_columns(place, scale, window_rows, aligned, factors, other, n_row, n_pole):
    share = window_rows.shape[1]
    side = n_pole // 4
    half = n_row * side
    depth, total = aligned.shape

    def window_at(i, place_ref):
        j = i % half
        core = jnp.where(i < half, 1 - place_ref[1], place_ref[1])
        second = 1 - place_ref[2] if other else place_ref[2]
        return (j // side) * n_pole + (j % side) * 4 + second * 2 + core, 0, 0

    def away_at(i, place_ref):
        j = jnp.minimum(i, half - 1)
        return j // side, j % side, 0, 0

    def keep_at(i, place_ref):
        j = jnp.maximum(i - half, 0)
        return j // side, j % side, 0, 0

    shape = jax.ShapeDtypeStruct((n_row, side, share, total), jnp.float32)
    return pl.pallas_call(
        window_kernel,
        out_shape=(shape, shape),
        grid_spec=pltpu.PrefetchScalarGridSpec(
            num_scalar_prefetch=1,
            grid=(2 * half,),
            in_specs=[
                pl.BlockSpec(memory_space=pltpu.SMEM),
                pl.BlockSpec((1, share, depth), window_at),
                pl.BlockSpec((depth, total), lambda i, c: (0, 0)),
                pl.BlockSpec(factors.shape, lambda i, c: (0, 0, 0)),
            ],
            out_specs=(
                pl.BlockSpec((1, 1, share, total), away_at),
                pl.BlockSpec((1, 1, share, total), keep_at),
            ),
        ),
        cost_estimate=pl.CostEstimate(
            flops=4 * half * share * depth * total,
            bytes_accessed=4 * half * share * (depth + 2 * total),
            transcendentals=0,
        ),
    )(place, scale, window_rows, aligned, factors)


def inner_kernel(place_ref, own_away_ref, own_keep_ref, away_ref, keep_ref, sum_ref):
    width = sum_ref.shape[1]

    @pl.when((pl.program_id(0) == 0) & (pl.program_id(1) == 0))
    def _():
        sum_ref[...] = jnp.zeros_like(sum_ref)

    for own_ref, term_ref in ((own_away_ref, away_ref), (own_keep_ref, keep_ref)):
        for m in range(NS):
            for part in split(term_ref[0, 0, :, m * width : (m + 1) * width]):
                for k in range(m, NS):
                    sum_ref[k * (k + 1) // 2 + m] += lax.dot_general(
                        own_ref[0, 0, :, k * width : (k + 1) * width],
                        part,
                        (((0,), (0,)), ((), ())),
                        preferred_element_type=jnp.float32,
                    )


def inner_products(place, own, away, keep, other, width):
    n_row, side, share, total = away.shape
    n_pole = 4 * side

    def own_at(flip):
        def at(d, j, place_ref):
            core = 1 - place_ref[1] if flip else place_ref[1]
            second = 1 - place_ref[2] if other else place_ref[2]
            return d, j * 4 + second * 2 + core, 0, 0

        return at

    def term_at(d, j, place_ref):
        return (place_ref[0] - d + n_row) % n_row, j, 0, 0

    pairs = NS * (NS + 1) // 2
    return pl.pallas_call(
        inner_kernel,
        out_shape=jax.ShapeDtypeStruct((pairs, width, width), jnp.float32),
        grid_spec=pltpu.PrefetchScalarGridSpec(
            num_scalar_prefetch=1,
            grid=(n_row, side),
            in_specs=[
                pl.BlockSpec((1, 1, share, total), own_at(True)),
                pl.BlockSpec((1, 1, share, total), own_at(False)),
                pl.BlockSpec((1, 1, share, total), term_at),
                pl.BlockSpec((1, 1, share, total), term_at),
            ],
            out_specs=pl.BlockSpec((pairs, width, width), lambda d, j, p: (0, 0, 0)),
        ),
        cost_estimate=pl.CostEstimate(
            flops=2 * n_row * n_pole * share * pairs * width * width,
            bytes_accessed=3 * n_row * n_pole * share * total,
            transcendentals=0,
        ),
    )(place, own, own, away, keep)


def staged(window, panels, row_map, panel_root, upper_blocks, diag_inverse, weights, pole_order):
    n_row, n_col, n_pole = (lax.axis_size(name) for name in ("row", "col", "pole"))
    row_index, col_index = lax.axis_index("row"), lax.axis_index("col")
    window_block = window[0]
    slab = panels[0, 0]
    width = slab.shape[1]
    group = window_block.shape[0] // n_row
    share = group // n_pole
    pole_weight = jnp.sum(jnp.where(jnp.arange(weights.shape[0]) == pole_order[0], weights, 0.0))
    pole_index = lax.axis_index("pole")
    core, second = pole_index % 2, (pole_index // 2) % 2
    place = jnp.stack([row_index, core, second]).astype(jnp.int32)
    slab_index = (col_index - panel_root[0] + n_col) % n_col
    local_map = row_map % group
    own_start = col_index * group

    slabs = [slab]
    for distance in range(1, n_col):
        slabs.append(shift(slab, "col", distance))
    own_map = lax.dynamic_slice_in_dim(local_map, own_start, group, 1)
    packed_map = jnp.concatenate([own_map // 32, own_map % 32]).astype(jnp.bfloat16).reshape(-1)
    packed_map = jnp.pad(packed_map, (0, -packed_map.shape[0] % width)).reshape(-1, width)
    part_rows = upper_blocks.shape[2]
    pairs = upper_blocks.shape[1]
    gathered = shift_gather(jnp.concatenate([upper_blocks[0].reshape(-1, width), packed_map]), "row")
    own_slab = [shift_gather(lax.dynamic_slice_in_dim(slab, own_start, group, 0), "row")]
    factors = jnp.zeros((pairs, part_rows * n_row, width), upper_blocks.dtype)
    maps = []
    for back, g in enumerate(gathered):
        at = (row_index - back + n_row) % n_row
        factors = lax.dynamic_update_slice_in_dim(
            factors, g[: pairs * part_rows].reshape(pairs, part_rows, width), at * part_rows, 1
        )
        flat = g[pairs * part_rows :].reshape(-1)[: 2 * NS * group].astype(jnp.int32)
        maps.append((flat[: NS * group] * 32 + flat[NS * group :]).reshape(NS, group))

    stacked_slabs = jnp.stack(slabs).reshape(n_col, n_col, group, width)
    stacked_map = jnp.stack([local_map[:, c * group : (c + 1) * group] for c in range(n_col)])
    aligned = reorder(slab_index, stacked_map, stacked_slabs)
    own_slab += [shift_gather(lax.dynamic_slice_in_dim(other, own_start, group, 0), "row") for other in slabs[1:]]

    window_rows = window_block.reshape(n_row * n_pole, share, window_block.shape[1])
    scale = (-pole_weight).reshape(1)
    first_away, first_keep = window_columns(
        place, scale, window_rows, aligned, factors, True, n_row, n_pole
    )
    last_away, last_keep = window_columns(
        place, scale, window_rows, aligned, factors, False, n_row, n_pole
    )
    first_come = swap(first_away, "pole", 1)
    last_come = swap(last_away, "pole", 1)
    step = share // CHUNKS if share % (8 * CHUNKS) == 0 else share
    pieces = [slice(at, at + step) for at in range(0, share, step)]
    sent = [first_keep[:, :, piece] + first_come[:, :, piece] for piece in pieces]
    kept = [last_keep[:, :, piece] + last_come[:, :, piece] for piece in pieces]
    _, own_slab = lax.optimization_barrier((sent, own_slab))
    column_parts = []
    for away, keep in zip(sent, kept):
        code, top = encode(away)
        code = swap(code, "pole", 2)
        top = swap(top, "pole", 2)
        total = keep + decode(code, top)
        column_parts.append(coded_sum(halving_sum(total, "pole", 4), "row"))
    summed_columns = jnp.stack(
        [
            jnp.concatenate([part[:, k * width : (k + 1) * width] for part in column_parts])
            for k in range(NS)
        ]
    )

    stacked_own = jnp.stack([jnp.stack(blocks) for blocks in own_slab])
    own = reorder(slab_index, jnp.stack(maps), stacked_own)
    own = own.reshape(n_row, n_pole, share, NS * width)
    products = inner_products(place, own, first_away, first_keep, True, width)
    products += inner_products(place, own, last_away, last_keep, False, width)
    inner = {(k, m): products[k * (k + 1) // 2 + m] for k in range(NS) for m in range(k + 1)}

    wide = [factors[e].astype(jnp.float32) for e in range(pairs)]
    spread = jnp.zeros((NS, diag_inverse.shape[2] * n_row, width), jnp.float32)
    spread = lax.dynamic_update_slice_in_dim(
        spread, diag_inverse[0] * (pole_weight / n_col), row_index * diag_inverse.shape[2], 1
    )
    diagonals, crossed = [], {}

    def inverse_block(m, n):
        if m == n:
            return diagonals[m]
        return crossed[m, n] if m < n else crossed[n, m].T

    for k in range(NS):
        diagonal = spread[k] - inner[k, k]
        for m in range(k):
            y_block = inner[k, m].T
            for n in range(k):
                y_block = y_block + precise(inverse_block(m, n), wide[pair_index(k, n)])
            crossed[m, k] = -y_block
            diagonal = diagonal + precise(wide[pair_index(k, m)].T, y_block)
        diagonals.append(diagonal)
    blocks = jnp.concatenate(diagonals, axis=1).reshape(n_row, n_pole, -1, NS * width)
    summed_diagonals = shift_sum(halving_sum(blocks, "pole", 1), "row")
    bit = 1
    while bit < n_col:
        summed_diagonals = summed_diagonals + lax.ppermute(
            summed_diagonals, "col", [(i, i ^ bit) for i in range(n_col)]
        )
        bit *= 2
    summed_diagonals = summed_diagonals.reshape(-1, NS, width).transpose(1, 0, 2)
    return (summed_columns[:, None], summed_diagonals)


MESH = pl.DeviceIdType.MESH
LEVELS = 32000.0
NEAREST = 12582912.0


def code_of(value):
    top = jnp.maximum(jnp.max(jnp.abs(value), axis=0, keepdims=True), 1e-30)
    nearest = (value * (LEVELS / top) + NEAREST) - NEAREST
    return nearest.astype(jnp.int32).astype(jnp.int16), top


def value_of(code, top):
    return code.astype(jnp.int32).astype(jnp.float32) * (top * (1.0 / LEVELS))


def fused_kernel(
    weights_ref, order_ref, root_ref, window_ref, slab_ref, map_ref, upper_ref, diag_ref,
    columns_out, diagonal_ref,
    columns_ref, out_sem, win, own_slab, far_slab, maps, fac, al, y, core_in, y_out, y_out_top, y_in, y_in_top,
    z_out, z_out_top, z_in, z_in_top, inner, spread, g_all, g_core, g_out, g_out_top, g_in, g_in_top,
    g_sum, gz_out, gz_out_top, gz_in, gz_in_top, g_x, g_last,
    x_send, x_recv, here, win_sem, own_send, own_recv, small_send, small_recv, share_send, share_recv,
    core_send, core_recv, y_send, y_recv, z_send, z_recv,
    gc_send, gc_recv, gy_send, gy_recv, gz_send, gz_recv, gx_send, gx_recv,
):
    n_row, n_col, n_pole = (lax.axis_size(name) for name in ("row", "col", "pole"))
    r, c, p = (lax.axis_index(name) for name in ("row", "col", "pole"))
    side, core = p // 2, p % 2
    share, width = columns_ref.shape[1:]
    group = share * n_pole
    depth = diagonal_ref.shape[1]
    part = upper_ref.shape[1]
    to_col, to_core, to_side = {"col": 1 - c}, {"pole": side * 2 + 1 - core}, {"pole": (1 - side) * 2 + core}

    def remote(src, dst, send, recv, device):
        return pltpu.make_async_remote_copy(
            src_ref=src, dst_ref=dst, send_sem=send, recv_sem=recv, device_id=device, device_id_type=MESH
        )

    def half(at):
        return pl.ds(pl.multiple_of(at * group, group), group)

    def others():
        return [lax.rem(r + distance, n_row) for distance in range(1, n_row)]

    barrier = pltpu.get_barrier_semaphore()
    for device in [to_col, to_core, to_side] + [{"row": at} for at in others()]:
        pl.semaphore_signal(barrier, inc=1, device_id=device, device_id_type=MESH)
    pl.semaphore_wait(barrier, 2 + n_row)

    def x_copy(at):
        src, dst = ((half(1 - c), own_slab.at[r, 1]), (half(c), far_slab.at[1]))[at]
        return remote(slab_ref.at[src], dst, x_send.at[at], x_recv.at[at], to_col)

    def own_copy(block, j, right, first=False):
        src = slab_ref.at[half(c)] if first else own_slab.at[block, j]
        return remote(
            src, own_slab.at[block, j], own_send.at[block, j, 1 - right], own_recv.at[block, j],
            {"row": r + 1 if right else r - 1},
        )

    piece = part // n_col

    def small_copy(at, sender):
        mine_at = pl.ds(pl.multiple_of(c * piece, piece), piece)
        rows = pl.ds(pl.multiple_of(sender * part + c * piece, piece), piece)
        return (
            remote(
                upper_ref.at[:, mine_at], fac.at[:, rows], small_send.at[at, 0], small_recv.at[sender, 0],
                {"row": at},
            ),
            remote(
                map_ref.at[:, half(c)], maps.at[sender, :, half(c)], small_send.at[at, 1],
                small_recv.at[sender, 1], {"row": at},
            ),
        )

    def share_copy(at, column):
        rows = pl.ds(pl.multiple_of(at * part + column * piece, piece), piece)
        return remote(fac.at[:, rows], fac.at[:, rows], share_send.at[at], share_recv.at[at], to_col)

    def both_ways(j, first):
        for right in (1, 0):
            @pl.when(r < n_row - 1 if right else r > 0)
            def _(right=right):
                own_copy(r, j, right, first).start()

    x_copy(0).start()
    both_ways(0, True)
    x_copy(1).start()
    for at in others():
        for copy in small_copy(at, r):
            copy.start()
    locals_ = [
        pltpu.make_async_copy(slab_ref.at[half(c)], own_slab.at[r, 0], here.at[0]),
        pltpu.make_async_copy(slab_ref.at[half(1 - c)], far_slab.at[0], here.at[1]),
    ]
    loads = []
    for slot, at in ((0, c), (1, 1 - c)):
        for pole in range(n_pole):
            loads.append(
                pltpu.make_async_copy(
                    window_ref.at[:, pole, :, half(at)], win.at[slot, pole], win_sem.at[slot, pole]
                )
            )
    for copy in locals_ + loads:
        copy.start()

    maps[r] = map_ref[...]
    fac[:, pl.ds(pl.multiple_of(r * part, part), part)] = upper_ref[...]
    weight = jnp.float32(0.0)
    for at in range(weights_ref.shape[0]):
        weight += jnp.where(order_ref[0] == at, weights_ref[at], 0.0)
    inner[...] = jnp.zeros_like(inner)

    def reorder(slot, source, block, at):
        def one(k, carry):
            row = maps[block, pl.ds(k, 1), half(at)] - (block * n_col + at) * group
            chosen = lax.broadcasted_iota(jnp.int32, (group, group), 0) == row
            column = lax.rem(root_ref[0, k] + n_col - c, n_col)
            rows = source[0]
            for j in range(1, n_col):
                rows = jnp.where(column == j, source[j], rows)
            placed = lax.dot_general(
                jnp.where(chosen, 1.0, 0.0).astype(rows.dtype), rows, (((0,), (0,)), ((), ())),
                preferred_element_type=jnp.float32,
            )
            al[slot, :, pl.ds(pl.multiple_of(k * width, width), width)] = placed.astype(al.dtype)
            return carry

        lax.fori_loop(0, NS, one, 0)

    near = jnp.minimum(r, n_row - 1 - r)
    toward = jnp.where(r < n_row - 1 - r, 1, -1)

    def block_at(step):
        odd = lax.rem(step, 2)
        zigzag = r + (2 * odd - 1) * ((step + 1) // 2)
        return jnp.where(step <= 2 * near, zigzag, r + toward * (step - near))

    def passes_on():
        return (r > 0) & (r < n_row - 1)

    def pass_on(step, j):
        @pl.when(passes_on())
        def _():
            block = block_at(step)
            own_copy(block, j, 1).wait_recv()

            @pl.when(block < r)
            def _():
                own_copy(block, j, 1).start()

            @pl.when(block > r)
            def _():
                own_copy(block, j, 0).start()

    x_copy(0).wait_recv()
    both_ways(1, False)
    for copy in locals_:
        copy.wait()
    early = range(1, min(3, n_row))
    reorder(0, own_slab.at[r], r, c)
    for step in early:
        pass_on(step, 0)
    for copy in loads[:n_pole]:
        copy.wait()

    def first_pass(pole, carry):
        left = win[0, pole].reshape(n_row * share, group)
        y[pole] = jnp.dot(left, al[0], preferred_element_type=jnp.float32).reshape(n_row, share, NS * width)
        return carry

    lax.fori_loop(0, n_pole, first_pass, 0)
    for at in others():
        for copy in small_copy(at, at):
            copy.wait_recv()
        share_copy(at, c).start()
    x_copy(1).wait_recv()
    reorder(1, far_slab, r, 1 - c)
    for copy in loads[n_pole:]:
        copy.wait()
    for at in others():
        share_copy(at, 1 - c).wait_recv()

    n_half = n_row // 2

    def core_copy(place, h):
        pole = jnp.where(place == 0, 1 - side, side) * 2 + 1 - core
        rows = pl.ds(h * n_half, n_half)
        return remote(
            y.at[pole, rows], core_in.at[place, rows], core_send.at[place, h], core_recv.at[place, h], to_core
        )

    def y_copy(h):
        return (
            remote(y_out.at[h], y_in.at[h], y_send.at[h, 0], y_recv.at[h, 0], to_side),
            remote(y_out_top.at[h], y_in_top.at[h], y_send.at[h, 1], y_recv.at[h, 1], to_side),
        )

    low = r < n_half
    far_half = jnp.where(low, 1, 0)

    def last_pass(i, carry):
        kind = i // 2
        h = jnp.where(lax.rem(i, 2) == 0, far_half, 1 - far_half)
        place = kind // 2
        pole = jnp.where(place == 0, 1 - side, side) * 2 + jnp.where(lax.rem(kind, 2) == 0, 1 - core, core)
        rows = pl.ds(h * n_half, n_half)
        left = win[1, pole, rows].reshape(n_half * share, group)
        total = y[pole, rows].reshape(n_half * share, NS * width)
        total = (total + jnp.dot(left, al[1], preferred_element_type=jnp.float32)) * -weight
        columns, parts = [], []
        for k in range(NS):
            column = total[:, k * width : (k + 1) * width]
            for m in range(k):
                for piece in parts[m]:
                    column = column - jnp.dot(piece, fac[pair_index(k, m)], preferred_element_type=jnp.float32)
            columns.append(column)
            parts.append(split(column))
            y[pole, rows, :, k * width : (k + 1) * width] = column.reshape(n_half, share, width)

        @pl.when(lax.rem(kind, 2) == 0)
        def _():
            core_copy(place, h).start()

        @pl.when(kind == 1)
        def _():
            core_copy(0, h).wait_recv()
            for at in range(n_half):
                code, top = code_of(y[pole, h * n_half + at] + core_in[0, h * n_half + at])
                y_out[h, at] = code
                y_out_top[h, at] = top
            for copy in y_copy(h):
                copy.start()

        @pl.when(i == 3)
        def _():
            for step in early:
                pass_on(step, 1)

        return carry

    lax.fori_loop(0, 8, last_pass, 0)
    mine = side * 2 + core

    def z_copy(at, way):
        device = {"row": r + 1 - 2 * way}
        return (
            remote(z_out.at[at], z_in.at[way, at], z_send.at[at, 0], z_recv.at[way, at, 0], device),
            remote(z_out_top.at[at], z_in_top.at[way, at], z_send.at[at, 1], z_recv.at[way, at, 1], device),
        )

    def finish(h):
        core_copy(1, h).wait_recv()
        for copy in y_copy(h):
            copy.wait_recv()
        for at in range(n_half):
            row = h * n_half + at
            core_in[1, row] = y[mine, row] + core_in[1, row] + value_of(y_in[h, at], y_in_top[h, at])

    def add_come(at, way):
        @pl.when(jnp.where(way == 0, r, n_row - 1 - r) > 0)
        def _():
            for copy in z_copy(at, way):
                copy.wait_recv()
            core_in[1, at] = core_in[1, at] + value_of(z_in[way, at], z_in_top[way, at])

    def forward(at, way):
        @pl.when(jnp.where(way == 0, at - r, r - at) > 0)
        def _():
            add_come(at, way)
            z_out[at], z_out_top[at] = code_of(core_in[1, at])
            for copy in z_copy(at, way):
                copy.start()

    def far(n):
        forward(jnp.where(low, n_row - 1 - n, n), jnp.where(low, 0, 1))

    def close(n):
        forward(jnp.where(low, n, n_row - 1 - n), jnp.where(low, 1, 0))

    def gather_inner(step, carry):
        block = block_at(step)

        @pl.when(step == 1)
        def _():
            for later in range(3, n_row):
                pass_on(later, 0)

        @pl.when(step > 0)
        def _():
            @pl.when((r == 0) | (r == n_row - 1))
            def _():
                for j in range(2):
                    own_copy(block, j, 1).wait_recv()

            reorder(1, own_slab.at[block], block, c)

        slot = jnp.minimum(step, 1)
        for m in range(NS):
            column = jnp.concatenate(
                [y[pole, block, :, m * width : (m + 1) * width] for pole in range(n_pole)]
            )
            pieces = split(column)
            for k in range(m, NS):
                rows = al[slot, :, k * width : (k + 1) * width]
                for piece in pieces:
                    inner[k * (k + 1) // 2 + m] += lax.dot_general(
                        rows, piece, (((0,), (0,)), ((), ())), preferred_element_type=jnp.float32
                    )

        @pl.when(step == n_row - 2)
        def _():
            for later in range(3, n_row):
                pass_on(later, 1)
            finish(far_half)

            @pl.when(jnp.logical_not(passes_on()))
            def _():
                for n in range(n_half):
                    far(n)
                finish(1 - far_half)
                for n in range(n_half, n_row - 1):
                    far(n)

        return carry

    lax.fori_loop(0, n_row, gather_inner, 0)

    @pl.when(passes_on())
    def _():
        far(0)
        finish(1 - far_half)
        for n in range(1, n_row - 1):
            far(n)
        for n in range(n_row - 1):
            close(n)


    spread[...] = jnp.zeros_like(spread)
    spread[:, pl.ds(pl.multiple_of(r * part, part), part)] = diag_ref[...] * (weight * (1.0 / n_col))

    def times_factor(left, e):
        return sum(jnp.dot(piece, fac[e], preferred_element_type=jnp.float32) for piece in split(left))

    def factor_times(e, right):
        dims = (((0,), (0,)), ((), ()))
        return sum(
            lax.dot_general(fac[e], piece, dims, preferred_element_type=jnp.float32) for piece in split(right)
        )

    diagonals, crossed = [], {}

    def inverse_block(m, n):
        if m == n:
            return diagonals[m]
        return crossed[m, n] if m < n else crossed[n, m].T

    for k in range(NS):
        diagonal = spread[k] - inner[k * (k + 1) // 2 + k]
        for m in range(k):
            y_block = inner[k * (k + 1) // 2 + m].T
            for n in range(k):
                y_block = y_block + times_factor(inverse_block(m, n), pair_index(k, n))
            crossed[m, k] = -y_block
            diagonal = diagonal + factor_times(pair_index(k, m), y_block)
        diagonals.append(diagonal)
        blocks = diagonal.reshape(n_row, n_pole, depth, width)
        for pole in range(n_pole):
            g_all[pole, :, :, k * width : (k + 1) * width] = blocks[:, pole]

    def gc_copy(at):
        return remote(g_all.at[at * 2 + 1 - core], g_core.at[at], gc_send.at[at], gc_recv.at[at], to_core)

    for at in range(2):
        gc_copy(at).start()
    gc_copy(1 - side).wait_recv()
    away = g_all[(1 - side) * 2 + core] + g_core[1 - side]
    g_out[...], g_out_top[...] = code_of(away.reshape(n_row * depth, NS * width))

    def gy_copies():
        return (
            remote(g_out, g_in, gy_send.at[0], gy_recv.at[0], to_side),
            remote(g_out_top, g_in_top, gy_send.at[1], gy_recv.at[1], to_side),
        )

    for copy in gy_copies():
        copy.start()
    gc_copy(side).wait_recv()
    for copy in gy_copies():
        copy.wait_recv()
    come = value_of(g_in[...], g_in_top[...]).reshape(n_row, depth, NS * width)
    g_sum[...] = g_all[mine] + g_core[side] + come
    for at in range(n_row):
        gz_out[at], gz_out_top[at] = code_of(g_sum[at])

    def gz_copy(at, slot):
        return (
            remote(gz_out.at[at], gz_in.at[slot], gz_send.at[at, 0], gz_recv.at[slot, 0], {"row": at}),
            remote(gz_out_top.at[at], gz_in_top.at[slot], gz_send.at[at, 1], gz_recv.at[slot, 1], {"row": at}),
        )

    for at in others():
        for copy in gz_copy(at, r):
            copy.start()

    for way in range(2):
        add_come(r, way)
    total = core_in[1, r]
    for k in range(NS):
        columns_ref[k] = total[:, k * width : (k + 1) * width]
    out_copy = pltpu.make_async_copy(columns_ref, columns_out, out_sem)
    out_copy.start()

    total = g_sum[r]
    for at in others():
        for copy in gz_copy(at, at):
            copy.wait_recv()
        total = total + value_of(gz_in[at], gz_in_top[at])
    g_last[...] = total
    gx_copy = remote(g_last, g_x, gx_send, gx_recv, to_col)
    gx_copy.start()
    gx_copy.wait_recv()
    total = total + g_x[...]
    for k in range(NS):
        diagonal_ref[k] = total[:, k * width : (k + 1) * width]

    for at in range(2):
        x_copy(at).wait_send()
        gc_copy(at).wait_send()
        for h in range(2):
            core_copy(at, h).wait_send()
        for copy in y_copy(at):
            copy.wait_send()
    out_copy.wait()
    for copy in gy_copies():
        copy.wait_send()
    gx_copy.wait_send()
    for at in others():
        share_copy(at, c).wait_send()
        for copy in small_copy(at, r) + z_copy(at, 0) + gz_copy(at, r):
            copy.wait_send()
    for j in range(2):
        for right in (1, 0):
            @pl.when(r < n_row - 1 if right else r > 0)
            def _(right=right, j=j):
                own_copy(r, j, right, j == 0).wait_send()

        for step in range(1, n_row):
            @pl.when(passes_on())
            def _(step=step, j=j):
                block = block_at(step)

                @pl.when(block < r)
                def _():
                    own_copy(block, j, 1).wait_send()

                @pl.when(block > r)
                def _():
                    own_copy(block, j, 0).wait_send()


def hand_on(columns_ref, diagonal_ref, columns_out, diagonal_out):
    columns_out[...] = columns_ref[...]
    diagonal_out[...] = diagonal_ref[...]


def fused(window, panels, row_map, panel_root, upper_blocks, diag_inverse, weights, pole_order):
    n_row, n_col, n_pole = (lax.axis_size(name) for name in ("row", "col", "pole"))
    slab = panels[0, 0]
    width = slab.shape[1]
    group = window.shape[1] // n_row
    share = group // n_pole
    depth = width // (n_row * n_pole)
    pairs = upper_blocks.shape[1]
    total = NS * width
    rows = window[0].reshape(n_row, n_pole, share, n_col * group)
    smem, vmem, hbm = (pl.BlockSpec(memory_space=m) for m in (pltpu.SMEM, pltpu.VMEM, pl.ANY))
    bf16, f32, i16, i32 = jnp.bfloat16, jnp.float32, jnp.int16, jnp.int32
    dma = pltpu.SemaphoreType.DMA
    columns, diagonal = pl.pallas_call(
        fused_kernel,
        out_shape=(
            jax.ShapeDtypeStruct((NS, share, width), f32),
            jax.ShapeDtypeStruct((NS, depth, width), f32),
        ),
        in_specs=[smem, smem, smem, hbm, hbm, vmem, vmem, vmem],
        out_specs=(hbm, vmem),
        scratch_shapes=[
            pltpu.VMEM((NS, share, width), f32),
            dma,
            pltpu.VMEM((n_col, n_pole, n_row, share, group), bf16),
            pltpu.VMEM((n_row, n_col, group, width), bf16),
            pltpu.VMEM((n_col, group, width), bf16),
            pltpu.VMEM((n_row, NS, n_col * group), i32),
            pltpu.VMEM((pairs, width, width), bf16),
            pltpu.VMEM((2, group, total), bf16),
            pltpu.VMEM((n_pole, n_row, share, total), f32),
            pltpu.VMEM((2, n_row, share, total), f32),
            pltpu.VMEM((2, n_row // 2, share, total), i16),
            pltpu.VMEM((2, n_row // 2, 1, total), f32),
            pltpu.VMEM((2, n_row // 2, share, total), i16),
            pltpu.VMEM((2, n_row // 2, 1, total), f32),
            pltpu.VMEM((n_row, share, total), i16),
            pltpu.VMEM((n_row, 1, total), f32),
            pltpu.VMEM((2, n_row, share, total), i16),
            pltpu.VMEM((2, n_row, 1, total), f32),
            pltpu.VMEM((NS * (NS + 1) // 2, width, width), f32),
            pltpu.VMEM((NS, width, width), f32),
            pltpu.VMEM((n_pole, n_row, depth, total), f32),
            pltpu.VMEM((2, n_row, depth, total), f32),
            pltpu.VMEM((n_row * depth, total), i16),
            pltpu.VMEM((1, total), f32),
            pltpu.VMEM((n_row * depth, total), i16),
            pltpu.VMEM((1, total), f32),
            pltpu.VMEM((n_row, depth, total), f32),
            pltpu.VMEM((n_row, depth, total), i16),
            pltpu.VMEM((n_row, 1, total), f32),
            pltpu.VMEM((n_row, depth, total), i16),
            pltpu.VMEM((n_row, 1, total), f32),
            pltpu.VMEM((depth, total), f32),
            pltpu.VMEM((depth, total), f32),
            dma((2,)), dma((2,)), dma((2,)), dma((n_col, n_pole)),
            dma((n_row, 2, 2)), dma((n_row, 2)), dma((n_row, 2)), dma((n_row, 2)), dma((n_row,)), dma((n_row,)),
            dma((2, 2)), dma((2, 2)), dma((2, 2)), dma((2, 2)), dma((n_row, 2)), dma((2, n_row, 2)),
            dma((2,)), dma((2,)), dma((2,)), dma((2,)), dma((n_row, 2)), dma((n_row, 2)), dma, dma,
        ],
        compiler_params=pltpu.CompilerParams(
            collective_id=0, has_side_effects=True, vmem_limit_bytes=67043328
        ),
        name="fused",
    )(weights, pole_order, panel_root, rows, slab, row_map, upper_blocks[0], diag_inverse[0])
    blocks = [pl.BlockSpec((1, rows_, width), lambda k: (k, 0, 0)) for rows_ in (share, depth)]
    columns, diagonal = pl.pallas_call(
        hand_on,
        out_shape=(
            jax.ShapeDtypeStruct(columns.shape, f32),
            jax.ShapeDtypeStruct(diagonal.shape, f32),
        ),
        grid=(NS,),
        in_specs=blocks,
        out_specs=tuple(blocks),
        name="hand_on",
    )(columns, diagonal)
    return columns[:, None], diagonal


def fits(mesh, window, upper_blocks):
    n_row, n_col, n_pole = (mesh.shape[name] for name in ("row", "col", "pole"))
    share = window.shape[1] // (n_row * n_col * n_pole)
    depth = upper_blocks.shape[3] // (n_row * n_pole)
    return n_col == 2 and n_pole == 4 and n_row % 2 == 0 and share % 128 == 0 and depth % 8 == 0


def solution(mesh):
    step = jax.shard_map(
        staged,
        mesh=mesh,
        in_specs=(
            P("pole", "col", "row"),
            P("pole", "col", "row", None),
            P(None, "row"),
            P("pole", None),
            P("pole", None, "row", None),
            P("pole", None, "row", None),
            P(),
            P("pole"),
        ),
        out_specs=(P(None, "col", ("row", "pole"), None), P(None, ("row", "pole"), None)),
        check_vma=False,
    )
    staged_step = step
    fused_step = jax.shard_map(
        fused,
        mesh=mesh,
        in_specs=(
            P("pole", "col", "row"),
            P("pole", "col", "row", None),
            P(None, "row"),
            P("pole", None),
            P("pole", None, "row", None),
            P("pole", None, "row", None),
            P(),
            P("pole"),
        ),
        out_specs=(P(None, "col", ("row", "pole"), None), P(None, ("row", "pole"), None)),
        check_vma=False,
    )

    def chosen(window, panels, row_map, panel_root, upper_blocks, *rest):
        one = fused_step if fits(mesh, window, upper_blocks) else staged_step
        return one(window, panels, row_map, panel_root, upper_blocks, *rest)

    return chosen
```
